32 devices in a mesh: wide: 8 (over z, y), narrow: 4 (over x, core).
Axes of the slice: x: 2, y: 2, z: 4, core: 2. Of those that a mesh axis runs over, the one named last changes fastest.
Arguments:
- tokens: bfloat16 [9344, 768], P('wide'), may hold values from -6 to 6
- w_qkv: bfloat16 [3, 768, 768], P(None, None, 'narrow'), may hold values from -0.21875 to 0.21875
- qv_bias: bfloat16 [2, 768], P(None, 'narrow'), may hold values from -1.75 to 1.75
- w_proj: bfloat16 [768, 768], P('narrow'), may hold values from -1.75 to 1.75
- proj_bias: bfloat16 [768], replicated, may hold values from -1.75 to 1.75
- w_fc1: bfloat16 [768, 3072], P(None, 'narrow'), may hold values from -0.21875 to 0.21875
- fc1_bias: bfloat16 [3072], P('narrow'), may hold values from -1.75 to 1.75
- w_fc2: bfloat16 [3072, 768], P('narrow'), may hold values from -0.109375 to 0.109375
- fc2_bias: bfloat16 [768], replicated, may hold values from -1.75 to 1.75
- norm_gains: bfloat16 [2, 768], replicated, may hold values from 0.5 to 1.5
- norm_shifts: bfloat16 [2, 768], replicated, may hold values from -1.75 to 1.75
- layer_scales: bfloat16 [2, 768], replicated, may hold values from 0.5 to 2
- rel_table: bfloat16 [12, 2212], P('narrow'), may hold values from -6 to 6
- image_ids: int32 [9344], P('wide'), may hold values from 0 to 31, as said below
- pad_mask: int32 [9344], P('wide'), may hold values from 0 to 1, as said below
- grid_rows: int32 [9344], P('wide'), may hold values from -1 to 23, as said below
- grid_cols: int32 [9344], P('wide'), may hold values from -1 to 23, as said below
- d_out: bfloat16 [9344, 768], P('wide'), may hold values from -6 to 6
Outputs:
- block_out: bfloat16 [9344, 768], P('wide')
- d_tokens: float32 [9344, 768], P('wide')
- d_qkv: float32 [3, 768, 768], P(None, None, 'narrow')
- d_qv_bias: float32 [2, 768], P(None, 'narrow')
- d_proj: float32 [768, 768], P('narrow')
- d_proj_bias: float32 [768], replicated
- d_fc1: float32 [768, 3072], P(None, 'narrow')
- d_fc1_bias: float32 [3072], P('narrow')
- d_fc2: float32 [3072, 768], P('narrow')
- d_fc2_bias: float32 [768], replicated
- d_norm_gains: float32 [2, 768], replicated
- d_norm_shifts: float32 [2, 768], replicated
- d_layer_scales: float32 [2, 768], replicated
- d_rel_table: float32 [12, 2212], P('narrow')
The draws below stay inside these ranges and needn't reach their ends.
Inputs may be any that keep to these rules, and one draw needn't show every extreme that they name: `image_ids`: each aligned block of 584 rows, number b, holds either one image of 24 x 24 patches with id 2 * b, or two images of 14 x 14 patches with ids 2 * b and 2 * b + 1 whose slots start at rows 0 and 208 of the block; padding slots carry the id of the image before them; block 0 is of the first kind, block 1 and the last block of the second. `pad_mask`: each image's first slot is its class token, followed by its patches row by row; all later slots of the image are padding. `grid_rows`: padding slots have coordinates 0. `grid_cols`: padding slots have coordinates 0.
All inputs are finite; a program needn't handle non-finite values.
Results may differ from the reference program's by a relative error of at most 0.012.
Values sent between devices are 32-bit elements; how exact they have to be, the bound alone decides.
No kernel may reach another device: no remote copies, remote signals or barrier semaphores. Data moves between devices by JAX's collectives and lax.ppermute only.
A program may use at most 192 MiB of HBM per device.

```python
import math
from functools import partial
import jax
import jax.numpy as jnp
from jax import lax

D = 768
H = 12
HD = 64
FF = 3072
GRID = 24
SMALL_GRID = 14
LONG = 584
SHORT = 208
NTAB = 2212
TOKENS = 9344


def layout(key):
    pack_count = TOKENS // LONG
    pack_kinds = jax.random.randint(jax.random.fold_in(key, 7), (pack_count,), 0, 9) < 4
    pack_kinds = pack_kinds.at[0].set(True).at[1].set(False).at[pack_count - 1].set(False)
    is_large = pack_kinds[:, None]
    position = jnp.arange(LONG, dtype=jnp.int32)[None, :]
    second = jnp.logical_and(jnp.logical_not(is_large), position >= SHORT)
    local_pos = position - jnp.where(second, SHORT, 0)
    grid_side = jnp.where(is_large, GRID, SMALL_GRID)
    is_real = local_pos < grid_side * grid_side + 1
    patch_num = jnp.maximum(local_pos - 1, 0)
    patch_row = jnp.where(local_pos == 0, -1, jnp.where(is_real, patch_num // grid_side, 0))
    patch_col = jnp.where(local_pos == 0, -1, jnp.where(is_real, patch_num % grid_side, 0))
    image_num = 2 * jnp.arange(pack_count, dtype=jnp.int32)[:, None] + second.astype(jnp.int32)
    return (image_num.reshape(TOKENS).astype(jnp.int32), is_real.astype(jnp.int32).reshape(TOKENS), patch_row.reshape(TOKENS).astype(jnp.int32), patch_col.reshape(TOKENS).astype(jnp.int32))


def draw_image_ids(key, part):
    return layout(key)[0]


def draw_pad_mask(key, part):
    return layout(key)[1]


def draw_grid_rows(key, part):
    return layout(key)[2]


def draw_grid_cols(key, part):
    return layout(key)[3]


def level_of(rng, dims, split, low, largest):
    def one(axis_at, parts):
        steps = jax.random.uniform(jax.random.fold_in(jax.random.fold_in(rng, 6), axis_at), (parts,), jnp.float32, low / len(split), largest / len(split))
        return jnp.repeat(jnp.exp(steps), dims[axis_at] // parts).reshape((-1,) + (1,) * (len(dims) - axis_at - 1))

    factor_of = one(*split[0])
    for cut in split[1:]:
        factor_of = factor_of * one(*cut)
    return factor_of


def noise(stream_key, dims, width, most, pieces=(), kind=jnp.bfloat16):
    values = width * jax.random.normal(stream_key, dims, jnp.float32)
    if pieces:
        values = values * level_of(stream_key, dims, pieces, -0.22, 0.18)
    return jnp.clip(values, -most, most).astype(kind)


def setup_inputs(seed: int = 0) -> dict:
    keys = jax.random.split(jax.random.key(seed), 19)
    return {
        "tokens": noise(keys[0], (TOKENS, D), 1.0, 6.0, ((0, 8),)),
        "w_qkv": noise(keys[1], (3, D, D), D ** -0.5, 0.21875, ((2, 4),)),
        "qv_bias": noise(keys[2], (2, D), 0.3, 1.75, ((1, 4),)),
        "w_proj": noise(keys[3], (D, D), (max(D // 64, 1)) ** -0.5, 1.75, ((0, 4),)),
        "proj_bias": noise(keys[4], (D,), 0.3, 1.75),
        "w_fc1": noise(keys[5], (D, FF), D ** -0.5, 0.21875, ((1, 4),)),
        "fc1_bias": noise(keys[6], (FF,), 0.3, 1.75, ((0, 4),)),
        "w_fc2": noise(keys[7], (FF, D), FF ** -0.5, 0.109375, ((0, 4),)),
        "fc2_bias": noise(keys[8], (D,), 0.3, 1.75),
        "norm_gains": jnp.clip(1.0 + 0.1 * jax.random.normal(keys[9], (2, D), jnp.float32), 0.5, 1.5).astype(jnp.bfloat16),
        "norm_shifts": noise(keys[10], (2, D), 0.3, 1.75),
        "layer_scales": jnp.clip(jnp.exp(jax.random.uniform(keys[11], (2, D), jnp.float32, math.log(0.5), math.log(2.0))), 0.5, 2.0).astype(jnp.bfloat16),
        "rel_table": noise(keys[12], (H, NTAB), 1.0, 6.0, ((0, 4),)),
        "image_ids": draw_image_ids(jax.random.fold_in(keys[18], 71), 0),
        "pad_mask": draw_pad_mask(jax.random.fold_in(keys[18], 71), 0),
        "grid_rows": draw_grid_rows(jax.random.fold_in(keys[18], 71), 0),
        "grid_cols": draw_grid_cols(jax.random.fold_in(keys[18], 71), 0),
        "d_out": noise(keys[17], (TOKENS, D), 1.0, 6.0, ((0, 8),)),
    }


@jax.custom_vjp
def low(v):
    return lax.optimization_barrier(v.astype(jnp.bfloat16)).astype(jnp.float32)

@jax.custom_vjp
def low_back(v):
    return v

def low_keep(v):
    return (low(v), None)

def low_pass(kept, grad):
    return (grad,)

def back_keep(v):
    return (v, None)

def back_low(kept, grad):
    return (low(grad),)
low.defvjp(low_keep, low_pass)
low_back.defvjp(back_keep, back_low)

def layer_norm(values, gain_row, shift_row):
    row_mean = lax.optimization_barrier(jnp.mean(values, axis=-1, keepdims=True))
    centred = values - row_mean
    variance = lax.optimization_barrier(jnp.mean(centred * centred, axis=-1, keepdims=True))
    return centred * lax.rsqrt(variance + 1e-06) * gain_row + shift_row

def matmul(left, right):
    return jnp.dot(left, right, precision=lax.Precision.HIGHEST)

def table_lookup(row_coords, col_coords):
    grid_side = 2 * GRID - 1
    relative = grid_side * grid_side
    is_patch = row_coords >= 0
    offset_index = (row_coords[:, None] - row_coords[None, :] + GRID - 1) * grid_side + (col_coords[:, None] - col_coords[None, :] + GRID - 1)
    query_class = jnp.where(is_patch[None, :], relative, relative + 2)
    lookup = jnp.where(is_patch[:, None], jnp.where(is_patch[None, :], offset_index, relative + 1), query_class)
    return lookup.astype(jnp.int32)

def attend_pack(rel_table, pack_data):
    query_rows, key_rows, value_rows, image_pack, mask_pack, row_coords, col_coords = pack_data
    lookup = table_lookup(row_coords, col_coords)
    pos_bias = rel_table[:, lookup]
    scores = jnp.einsum('qhd,khd->hqk', query_rows, key_rows, precision=lax.Precision.HIGHEST) + pos_bias
    scores = low_back(scores)
    allowed = (image_pack[:, None] == image_pack[None, :]) & (mask_pack[None, :] == 1)
    scores = jnp.where(allowed[None], scores, -jnp.inf)
    log_total = jax.nn.logsumexp(scores, axis=-1, keepdims=True)
    attn_probs = low(jnp.exp(scores - log_total))
    return jnp.einsum('hqk,khd->qhd', attn_probs, value_rows, precision=lax.Precision.HIGHEST)

def forward(tokens, w_qkv, qv_bias, w_proj, proj_bias, w_fc1, fc1_bias, w_fc2, fc2_bias, norm_gains, norm_shifts, layer_scales, rel_table, image_ids, pad_mask, grid_rows, grid_cols):
    pack_count = TOKENS // LONG
    normed = low(layer_norm(tokens, norm_gains[0], norm_shifts[0]))
    query_rows = low_back(low((matmul(normed, w_qkv[0]) + qv_bias[0]) * HD ** (-0.5)))
    key_rows = low_back(low(matmul(normed, w_qkv[1])))
    value_rows = low_back(low(matmul(normed, w_qkv[2]) + qv_bias[1]))
    pack_shape = (pack_count, LONG, H, HD)
    flat_shape = (pack_count, LONG)
    head_out = lax.map(jax.checkpoint(partial(attend_pack, rel_table)), (query_rows.reshape(pack_shape), key_rows.reshape(pack_shape), value_rows.reshape(pack_shape), image_ids.reshape(flat_shape), pad_mask.reshape(flat_shape), grid_rows.reshape(flat_shape), grid_cols.reshape(flat_shape)))
    head_out = low_back(low(head_out.reshape(TOKENS, D)))
    branch = low_back(matmul(head_out, w_proj) + proj_bias)
    middle = tokens + layer_scales[0] * branch
    normed_two = low(layer_norm(middle, norm_gains[1], norm_shifts[1]))
    hidden = low_back(matmul(normed_two, w_fc1) + fc1_bias)
    active = low(jax.nn.gelu(hidden, approximate=False))
    mixed_out = low_back(matmul(active, w_fc2) + fc2_bias)
    return middle + layer_scales[1] * mixed_out

def reference(tokens, w_qkv, qv_bias, w_proj, proj_bias, w_fc1, fc1_bias, w_fc2, fc2_bias, norm_gains, norm_shifts, layer_scales, rel_table, image_ids, pad_mask, grid_rows, grid_cols, d_out):
    floats = [arg.astype(jnp.float32) for arg in (tokens, w_qkv, qv_bias, w_proj, proj_bias, w_fc1, fc1_bias, w_fc2, fc2_bias, norm_gains, norm_shifts, layer_scales, rel_table)]

    def wrapped(*params):
        return forward(*params, image_ids, pad_mask, grid_rows, grid_cols)
    result, pullback = jax.vjp(wrapped, *floats)
    all_grads = pullback(d_out.astype(jnp.float32))
    return (result.astype(jnp.bfloat16), all_grads[0], all_grads[1], all_grads[2], all_grads[3], all_grads[4], all_grads[5], all_grads[6], all_grads[7], all_grads[8], all_grads[9], all_grads[10], all_grads[11], all_grads[12])
```

```python
from functools import partial

import jax
import jax.numpy as jnp
import numpy as np
from jax import lax
from jax.experimental import pallas as pl
from jax.experimental.pallas import tpu as pltpu
from jax.sharding import PartitionSpec as P

HD = 64
GRID = 24
SMALL = 14
SHORT = 208
LONG = 584
EPSILON = 1e-06
SIDE = 2 * GRID - 1
WIDE_L = 1280
WIDE_S = 640
NEG = -1e30
F32 = jnp.float32
BF16 = jnp.bfloat16
VMEM_LIMIT = 56 << 20


def params(**kw):
    return pltpu.CompilerParams(vmem_limit_bytes=VMEM_LIMIT, **kw)


def dot(a, b):
    return jnp.dot(a, b, preferred_element_type=F32)


def dot_nt(a, b):
    return lax.dot_general(a, b, (((1,), (1,)), ((), ())), preferred_element_type=F32)


def dot_tn(a, b):
    return lax.dot_general(a, b, (((0,), (0,)), ((), ())), preferred_element_type=F32)


def large_pick():
    pick = np.zeros((2, SIDE, GRID, GRID), np.float32)
    for s in range(GRID):
        for c in range(GRID):
            if s == 0:
                pick[1, c, s, c] = 1
            else:
                pick[0, c + GRID - s, s, c] = 1
    return pick.reshape(2 * SIDE, GRID * GRID)


def small_pick():
    pick = np.zeros((SIDE, 16, SMALL), np.float32)
    for s in range(SMALL):
        for c in range(SMALL):
            pick[c - s + GRID - 1, s, c] = 1
    return pick.reshape(SIDE, 16 * SMALL)


def strips(rel_table):
    heads = rel_table.shape[0]
    grid_part = rel_table[:, : SIDE * SIDE].reshape(heads, SIDE, SIDE)
    front = jnp.pad(grid_part, ((0, 0), (1, 0), (0, 0)))
    back = jnp.pad(grid_part, ((0, 0), (0, 1), (0, 0)))
    both = jnp.concatenate([front, back], axis=2)
    large = jnp.einsum(
        "huk,kp->hup", both, jnp.asarray(large_pick(), BF16), preferred_element_type=F32
    ).reshape(heads, SIDE + 1, GRID, GRID)
    large = large.transpose(0, 2, 1, 3).reshape(heads, GRID, (SIDE + 1) * GRID)
    large = jnp.pad(large, ((0, 0), (0, 0), (1, WIDE_L - 1 - (SIDE + 1) * GRID)))
    rows = 2 * SMALL - 1
    part = grid_part[:, GRID - SMALL : GRID - SMALL + rows]
    small = jnp.einsum(
        "huk,kp->hup", part, jnp.asarray(small_pick(), BF16), preferred_element_type=F32
    ).reshape(heads, rows, 16, SMALL)
    small = small.transpose(0, 2, 1, 3).reshape(heads, 16, rows * SMALL)
    small = jnp.pad(small, ((0, 0), (0, 0), (1, WIDE_S - 1 - rows * SMALL)))
    tails = rel_table[:, SIDE * SIDE :].astype(F32)
    return large, small, tails


def strips_back(d_large, d_small, d_tails):
    heads = d_large.shape[0]
    rows = 2 * SMALL - 1
    hi = lax.Precision.HIGHEST
    large = d_large[:, :, 1 : 1 + (SIDE + 1) * GRID].reshape(heads, GRID, SIDE + 1, GRID)
    both = jnp.einsum(
        "hsuc,ksc->huk",
        large,
        jnp.asarray(large_pick().reshape(2 * SIDE, GRID, GRID)),
        precision=hi,
    )
    grid_grad = both[:, 1:, :SIDE] + both[:, :SIDE, SIDE:]
    small = d_small[:, :, 1 : 1 + rows * SMALL].reshape(heads, 16, rows, SMALL)
    part = jnp.einsum(
        "hsuc,ksc->huk", small, jnp.asarray(small_pick().reshape(SIDE, 16, SMALL)), precision=hi
    )
    low = GRID - SMALL
    grid_grad = grid_grad + jnp.pad(part, ((0, 0), (low, SIDE - low - rows), (0, 0)))
    return jnp.concatenate(
        [grid_grad.reshape(heads, SIDE * SIDE), d_tails[:, 0, :3]], axis=1
    )


def tail_fix(block, t0, t1, t2, last, real):
    shape = block.shape
    row = lax.broadcasted_iota(jnp.int32, shape, 0)
    lane = lax.broadcasted_iota(jnp.int32, shape, 1)
    block = jnp.where(lane > last, block[:, 1:2], block)
    block = jnp.where(lane == 0, t0, block)
    block = jnp.where(row == 0, jnp.where(lane == 0, t2, t1), block)
    return jnp.where(row >= real, NEG, block)


def bias_kernel(tail_ref, large_ref, small_ref, out_ref, scr):
    for h in range(large_ref.shape[0]):
        t0, t1, t2 = tail_ref[h, 0], tail_ref[h, 1], tail_ref[h, 2]
        for r in range(GRID + 1):
            size = GRID if r < GRID else LONG - GRID * GRID
            off = (GRID - r) * GRID
            scr[r * GRID : r * GRID + size, 0:LONG] = large_ref[h, 0:size, off : off + LONG]
        last = GRID * GRID
        out_ref[0, h] = tail_fix(scr[:, 0:LONG], t0, t1, t2, last, last + 1).astype(BF16)
        last = SMALL * SMALL
        for r in range(SMALL):
            off = (SMALL - 1 - r) * SMALL
            wide = LONG - SHORT
            scr[1 + r * SMALL : 1 + (r + 1) * SMALL, 0:wide] = small_ref[
                h, 0:SMALL, off : off + wide
            ]
        block = tail_fix(scr[0:SHORT, 0 : LONG - SHORT], t0, t1, t2, last, last + 1)
        scr[...] = jnp.full(scr.shape, NEG, F32)
        scr[0:SHORT, 0:SHORT] = block[:, 0:SHORT]
        scr[SHORT : 2 * SHORT, SHORT:LONG] = block
        out_ref[1, h] = scr[:, 0:LONG].astype(BF16)


def make_bias(rel_table):
    heads = rel_table.shape[0]
    large, small, tails = strips(rel_table)
    return pl.pallas_call(
        bias_kernel,
        out_shape=jax.ShapeDtypeStruct((2, heads, LONG, LONG), BF16),
        in_specs=[
            pl.BlockSpec(memory_space=pltpu.SMEM),
            pl.BlockSpec(memory_space=pltpu.VMEM),
            pl.BlockSpec(memory_space=pltpu.VMEM),
        ],
        out_specs=pl.BlockSpec(memory_space=pltpu.VMEM),
        scratch_shapes=[pltpu.VMEM((LONG, 640), F32)],
        compiler_params=params(),
        name="bias",
    )(tails, large, small)


def layer_norm(values, gain_row, shift_row):
    row_mean = jnp.mean(values, axis=-1, keepdims=True)
    centred = values - row_mean
    inverse = lax.rsqrt(jnp.mean(centred * centred, axis=-1, keepdims=True) + EPSILON)
    unit_rows = centred * inverse
    return unit_rows * gain_row + shift_row, unit_rows, inverse


def head_lanes(shape, h):
    lane = lax.broadcasted_iota(jnp.int32, shape, 1)
    return (lane >= h * HD) & (lane < (h + 1) * HD)


def turned(block):
    return block.astype(F32).T.astype(BF16)


def forward_kernel(
    sc_ref, tok_ref, w_ref, qv_ref, gain_ref, shift_ref, bias_ref, o_ref, q_ref, k_ref, v_ref, lse_ref
):
    x = tok_ref[0].astype(F32)
    n1 = layer_norm(x, gain_ref[...], shift_ref[...])[0].astype(BF16)
    q = ((dot(n1, w_ref[0]) + qv_ref[0:1]) * HD**-0.5).astype(BF16)
    k = dot(n1, w_ref[1]).astype(BF16)
    v = (dot(n1, w_ref[2]) + qv_ref[1:2]).astype(BF16)
    q_ref[0] = q
    k_ref[0] = k
    v_ref[0] = v
    v_t = turned(v)
    outs = []
    for h in range(k.shape[1] // HD):
        k_h = jnp.where(head_lanes(k.shape, h), k, jnp.zeros_like(k))
        s = dot_nt(k_h, q) + bias_ref[0, h].astype(F32)
        top = jnp.max(s, axis=0, keepdims=True)
        e = jnp.exp(s - top)
        total = jnp.sum(e, axis=0, keepdims=True)
        p = (e * (1.0 / total)).astype(BF16)
        outs.append(dot(v_t[h * HD : (h + 1) * HD], p))
        lse_ref[0, h : h + 1, :] = top + jnp.log(total)
    o_ref[0] = jnp.concatenate(outs, axis=0).T.astype(BF16).astype(F32)


def pack_spec(shape):
    return pl.BlockSpec((1,) + shape, lambda i, sc: (sc[0],) + (0,) * len(shape))


def first_spec(shape):
    return pl.BlockSpec((1,) + shape, lambda i, sc: (0,) * (1 + len(shape)))


def whole_spec(shape):
    return pl.BlockSpec(shape, lambda i, sc: (0,) * len(shape))


def kind_spec(shape):
    return pl.BlockSpec((1,) + shape, lambda i, sc: (sc[1],) + (0,) * len(shape))


def attend(scalars, tok3, w_qkv, qv_bias, gain_row, shift_row, bias):
    width = w_qkv.shape[2]
    heads = width // HD
    dim = tok3.shape[2]
    low = jax.ShapeDtypeStruct((1, LONG, width), BF16)
    return pl.pallas_call(
        forward_kernel,
        out_shape=[
            jax.ShapeDtypeStruct((1, LONG, width), F32),
            low,
            low,
            low,
            jax.ShapeDtypeStruct((1, heads, LONG), F32),
        ],
        grid_spec=pltpu.PrefetchScalarGridSpec(
            num_scalar_prefetch=1,
            grid=(1,),
            in_specs=[
                pack_spec((LONG, dim)),
                whole_spec((3, dim, width)),
                whole_spec((2, width)),
                whole_spec((1, dim)),
                whole_spec((1, dim)),
                kind_spec((heads, LONG, LONG)),
            ],
            out_specs=[first_spec((LONG, width))] * 4 + [first_spec((heads, LONG))],
        ),
        compiler_params=params(),
        cost_estimate=pl.CostEstimate(
            flops=2 * LONG * dim * 3 * width + 4 * LONG * LONG * width,
            transcendentals=heads * LONG * LONG,
            bytes_accessed=2 * heads * LONG * LONG + 8 * LONG * dim,
        ),
        name="attend",
    )(scalars, tok3, w_qkv, qv_bias, gain_row, shift_row, bias)


def fold_large(ds, h, dl_ref, dt_ref):
    last = GRID * GRID
    full = ds[:, 0:LONG]
    lane = lax.broadcasted_iota(jnp.int32, full.shape, 1)
    row = lax.broadcasted_iota(jnp.int32, full.shape, 0)
    pad = jnp.sum(jnp.where(lane > last, full, 0.0), axis=1, keepdims=True)
    body = row > 0
    t0 = jnp.sum(jnp.where((lane == 0) & body, full, 0.0))
    t1 = jnp.sum(jnp.where((lane > 0) & (row == 0), full, 0.0))
    t2 = jnp.sum(jnp.where((lane == 0) & (row == 0), full, 0.0))
    full = jnp.where((lane == 0) | (lane > last), 0.0, full)
    full = jnp.where(lane == 1, full + pad, full)
    ds[:, 0:LONG] = jnp.where(body, full, 0.0)
    for r in range(GRID + 1):
        size = GRID if r < GRID else LONG - GRID * GRID
        off = (GRID - r) * GRID
        dl_ref[h, 0:size, off : off + LONG] += ds[r * GRID : r * GRID + size, 0:LONG]
    tail_add(dt_ref, h, t0, t1, t2)


def tail_add(dt_ref, h, t0, t1, t2):
    lane = lax.broadcasted_iota(jnp.int32, (8, 128), 1)
    row = lax.broadcasted_iota(jnp.int32, (8, 128), 0)
    add = jnp.where(lane == 0, t0, jnp.where(lane == 1, t1, jnp.where(lane == 2, t2, 0.0)))
    dt_ref[h] += jnp.where(row == 0, add, 0.0)


def fold_small(ds, h, ds_ref, dt_ref):
    last = SMALL * SMALL
    for base, wide in ((0, SHORT), (SHORT, LONG - SHORT)):
        full = ds[base : base + SHORT, 0:LONG]
        if base:
            full = full[:, base : base + wide]
        else:
            full = full[:, 0:wide]
        lane = lax.broadcasted_iota(jnp.int32, full.shape, 1)
        row = lax.broadcasted_iota(jnp.int32, full.shape, 0)
        pad = jnp.sum(jnp.where(lane > last, full, 0.0), axis=1, keepdims=True)
        body = row > 0
        t0 = jnp.sum(jnp.where((lane == 0) & body, full, 0.0))
        t1 = jnp.sum(jnp.where((lane > 0) & (row == 0), full, 0.0))
        t2 = jnp.sum(jnp.where((lane == 0) & (row == 0), full, 0.0))
        full = jnp.where((lane == 0) | (lane > last), 0.0, full)
        full = jnp.where(lane == 1, full + pad, full)
        ds[base : base + SHORT, 0:wide] = full
        for r in range(SMALL):
            off = (SMALL - 1 - r) * SMALL
            lo = base + 1 + r * SMALL
            ds_ref[h, 0:SMALL, off : off + wide] += ds[lo : lo + SMALL, 0:wide]
        tail_add(dt_ref, h, t0, t1, t2)


def backward_kernel(
    sc_ref,
    tok_ref,
    w_ref,
    gain_ref,
    shift_ref,
    bias_ref,
    q_ref,
    k_ref,
    v_ref,
    do_ref,
    lse_ref,
    aw_ref,
    ab_ref,
    al_ref,
    as_ref,
    at_ref,
    dn_ref,
    dw_ref,
    db_ref,
    dl_ref,
    ds_ref,
    dt_ref,
    scr,
):
    dl_ref[...] = al_ref[...]
    ds_ref[...] = as_ref[...]
    dt_ref[...] = at_ref[...]
    q, k, v = q_ref[0], k_ref[0], v_ref[0]
    do = do_ref[0].astype(BF16)
    k_t = turned(k)
    d_qt = []
    d_k = jnp.zeros(k.shape, F32)
    d_v = jnp.zeros(k.shape, F32)
    for h in range(k.shape[1] // HD):
        own = head_lanes(k.shape, h)
        s = dot_nt(jnp.where(own, k, jnp.zeros_like(k)), q) + bias_ref[0, h].astype(F32)
        p = jnp.exp(s - lse_ref[0, h : h + 1, :])
        dp = dot_nt(jnp.where(own, v, jnp.zeros_like(v)), do)
        inner = jnp.sum(p * dp, axis=0, keepdims=True)
        ds = (p * (dp - inner)).astype(BF16)
        d_v = jnp.where(own, dot(p.astype(BF16), do), d_v)
        d_k = jnp.where(own, dot(ds, q), d_k)
        d_qt.append(dot(k_t[h * HD : (h + 1) * HD], ds))
        scr[:, 0:LONG] = ds.astype(F32)

        @pl.when(sc_ref[1] == 0)
        def _():
            fold_large(scr, h, dl_ref, dt_ref)

        @pl.when(sc_ref[1] == 1)
        def _():
            fold_small(scr, h, ds_ref, dt_ref)

    d_q = jnp.concatenate(d_qt, axis=0).T.astype(BF16) * jnp.asarray(HD**-0.5, BF16)
    d_k = d_k.astype(BF16)
    d_v = d_v.astype(BF16)
    dn = dot_nt(d_q, w_ref[0]) + dot_nt(d_k, w_ref[1]) + dot_nt(d_v, w_ref[2])
    half = dn.shape[1] // 2
    dn_ref[0] = dn[:, :half]
    dn_ref[1] = dn[:, half:]
    x = tok_ref[0].astype(F32)
    n1_t = layer_norm(x, gain_ref[...], shift_ref[...])[0].T.astype(BF16)
    dw_ref[0] = aw_ref[0] + dot(n1_t, d_q)
    dw_ref[1] = aw_ref[1] + dot(n1_t, d_k)
    dw_ref[2] = aw_ref[2] + dot(n1_t, d_v)
    db_ref[0:1] = ab_ref[0:1] + jnp.sum(d_q.astype(F32), axis=0, keepdims=True)
    db_ref[1:2] = ab_ref[1:2] + jnp.sum(d_v.astype(F32), axis=0, keepdims=True)


def attend_back(scalars, tok3, w_qkv, gain_row, shift_row, bias, saved, do, sums):
    width = w_qkv.shape[2]
    heads = width // HD
    dim = tok3.shape[2]
    q, k, v, lse = saved
    sum_shapes = [s.shape for s in sums]
    return pl.pallas_call(
        backward_kernel,
        out_shape=[jax.ShapeDtypeStruct((2, LONG, dim // 2), F32)]
        + [jax.ShapeDtypeStruct(s, F32) for s in sum_shapes],
        grid_spec=pltpu.PrefetchScalarGridSpec(
            num_scalar_prefetch=1,
            grid=(1,),
            in_specs=[
                pack_spec((LONG, dim)),
                whole_spec((3, dim, width)),
                whole_spec((1, dim)),
                whole_spec((1, dim)),
                kind_spec((heads, LONG, LONG)),
                first_spec((LONG, width)),
                first_spec((LONG, width)),
                first_spec((LONG, width)),
                first_spec((LONG, width)),
                first_spec((heads, LONG)),
            ]
            + [whole_spec(s) for s in sum_shapes],
            out_specs=[whole_spec((2, LONG, dim // 2))] + [whole_spec(s) for s in sum_shapes],
            scratch_shapes=[pltpu.VMEM((LONG, 640), F32)],
        ),
        compiler_params=params(),
        cost_estimate=pl.CostEstimate(
            flops=4 * LONG * dim * 3 * width + 10 * LONG * LONG * width,
            transcendentals=heads * LONG * LONG,
            bytes_accessed=2 * heads * LONG * LONG + 16 * LONG * dim,
        ),
        name="attend_back",
    )(scalars, tok3, w_qkv, gain_row, shift_row, bias, q, k, v, do, lse, *sums)


def zero_sums(heads, dim, width):
    return [
        jnp.zeros((3, dim, width), F32),
        jnp.zeros((2, width), F32),
        jnp.zeros((heads, GRID, WIDE_L), F32),
        jnp.zeros((heads, 16, WIDE_S), F32),
        jnp.zeros((heads, 8, 128), F32),
    ]


def wide_rows(lo_ref, hi_ref):
    return jnp.concatenate([lo_ref[0], hi_ref[0]], axis=1)


def column_sum(x):
    return jnp.sum(x, axis=0, keepdims=True)


def feed_kernel(first, *refs):
    (sc_ref, tok_ref, out_ref, o0, ox, oc, wp0, wpx, wpc, pb, ls, gain, shift, w1, b1, w2) = refs[:16]
    refs = refs[16:]
    if not first:
        a1, a2, ab1, ab2 = refs[:4]
        refs = refs[4:]
    mid_ref, a_ref, m_ref, dn_ref, d1_ref, d2_ref, db1_ref, db2_ref = refs
    low = lambda r: r.astype(BF16)
    near = dot(low(o0[0]), wp0[...]) + dot(low(oc[0, 0]), low(wpc[0]))
    far = dot(low(ox[0]), low(wpx[...])) + dot(low(oc[1, 0]), low(wpc[1]))
    a = near + far + pb[...]
    a_ref[0] = a
    mid = tok_ref[0].astype(F32) + ls[0:1] * a
    mid_ref[0] = mid
    n2 = layer_norm(mid, gain[...], shift[...])[0].astype(BF16)
    u = dot(n2, w1[...]) + b1[...]
    cdf = 0.5 * (1.0 + lax.erf(u * np.float32(np.sqrt(0.5))))
    slope = cdf + u * (jnp.exp(-0.5 * u * u) * np.float32(1 / np.sqrt(2 * np.pi)))
    g = (u * cdf).astype(BF16)
    m = dot(g, w2[...])
    half = m.shape[1] // 2
    m_ref[0] = m[:, :half]
    m_ref[1] = m[:, half:]
    dm = (ls[1:2] * out_ref[0].astype(F32)).astype(BF16)
    du = (slope * dot_nt(dm, w2[...])).astype(BF16)
    dn = dot_nt(du, w1[...])
    dn_ref[0] = dn[:, :half]
    dn_ref[1] = dn[:, half:]
    d2 = dot_tn(g, dm)
    d1 = dot_tn(n2, du)
    s1 = column_sum(du.astype(F32))
    s2 = column_sum(dm.astype(F32))
    if not first:
        d2, d1, s1, s2 = d2 + a2[...], d1 + a1[...], s1 + ab1[...], s2 + ab2[...]
    d2_ref[...] = d2
    d1_ref[...] = d1
    db1_ref[...] = s1
    db2_ref[...] = s2


def once(spec_of, shape):
    spec = spec_of(shape)
    return pl.BlockSpec(spec.block_shape, spec.index_map, pipeline_mode=pl.Buffered(1))


def feed(scalars, tok3, out3, o_parts, w_parts, pb, ls, gain, shift, w1, b1, w2, sums):
    dim = tok3.shape[2]
    hid = w1.shape[1]
    width = w_parts[0].shape[0]
    first = sums is None
    pair = jax.ShapeDtypeStruct((2, LONG, dim // 2), F32)
    row = jax.ShapeDtypeStruct((1, LONG, dim), F32)
    sum_shapes = [(dim, hid), (hid, dim), (1, hid), (1, dim)]
    specs = [
        once(pack_spec, (LONG, dim)),
        once(pack_spec, (LONG, dim)),
        once(first_spec, (LONG, width)),
        once(first_spec, (LONG, width)),
        once(whole_spec, (2, 1, LONG, width)),
        once(whole_spec, (width, dim)),
        once(whole_spec, (width, dim)),
        once(whole_spec, (2, width, dim)),
        once(whole_spec, (1, dim)),
        once(whole_spec, (2, dim)),
        once(whole_spec, (1, dim)),
        once(whole_spec, (1, dim)),
        once(whole_spec, (dim, hid)),
        once(whole_spec, (1, hid)),
        once(whole_spec, (hid, dim)),
    ]
    if not first:
        specs += [once(whole_spec, s) for s in sum_shapes]
    return pl.pallas_call(
        partial(feed_kernel, first),
        out_shape=[row, row, pair, pair] + [jax.ShapeDtypeStruct(s, F32) for s in sum_shapes],
        grid_spec=pltpu.PrefetchScalarGridSpec(
            num_scalar_prefetch=1,
            grid=(1,),
            in_specs=specs,
            out_specs=[once(first_spec, (LONG, dim))] * 2
            + [once(whole_spec, pair.shape)] * 2
            + [once(whole_spec, s) for s in sum_shapes],
        ),
        compiler_params=params(),
        cost_estimate=pl.CostEstimate(
            flops=2 * LONG * dim * (dim + 6 * hid),
            transcendentals=2 * LONG * hid,
            bytes_accessed=30 * LONG * dim,
        ),
        name="feed",
    )(scalars, tok3, out3, *o_parts, *w_parts, pb, ls, gain, shift, w1, b1, w2, *(sums or ()))


def norm_back(upstream, unit_rows, inverse, gain_row):
    scaled = upstream * gain_row
    centred = scaled - jnp.mean(scaled, axis=-1, keepdims=True)
    centred = centred - unit_rows * jnp.mean(scaled * unit_rows, axis=-1, keepdims=True)
    return inverse * centred, column_sum(upstream * unit_rows), column_sum(upstream)


def joined(sc_ref, mine, peer):
    core = sc_ref[2]
    lo = jnp.where(core == 0, mine[...], peer[...])
    hi = jnp.where(core == 0, peer[...], mine[...])
    return jnp.concatenate([lo, hi], axis=1)


def middle_kernel(
    sc_ref, out_ref, mid_ref, a_ref, mine, peer, ls, gain, shift, wp0, wpx, o0, ox,
    dmid_ref, do0_ref, dox_ref, dp0_ref, dpx_ref, sum_ref
):
    dn2 = joined(sc_ref, mine, peer)
    _, unit, inverse = layer_norm(mid_ref[0], gain[...], shift[...])
    back, d_gain, d_shift = norm_back(dn2, unit, inverse, gain[...])
    dmid = out_ref[0].astype(F32) + back
    dmid_ref[0] = dmid
    da = (ls[0:1] * dmid).astype(BF16)
    do0_ref[0] = dot_nt(da, wp0[...]).astype(BF16).astype(F32)
    dox_ref[0] = dot_nt(da, wpx[...].astype(BF16)).astype(BF16).astype(F32)
    dp0_ref[...] = dot(o0[0].T.astype(BF16), da)
    dpx_ref[...] = dot(ox[0].T.astype(BF16), da)
    sum_ref[0:1] = d_gain
    sum_ref[1:2] = d_shift
    sum_ref[2:3] = column_sum(dmid * a_ref[0])
    sum_ref[3:4] = column_sum(da.astype(F32))


def middle_back(scalars, out3, mid, a, mine, peer, ls, gain, shift, w_parts, o_parts):
    dim = mid.shape[2]
    width = w_parts[0].shape[0]
    row = jax.ShapeDtypeStruct((1, LONG, dim), F32)
    low = jax.ShapeDtypeStruct((1, LONG, width), F32)
    mat = jax.ShapeDtypeStruct((width, dim), F32)
    return pl.pallas_call(
        middle_kernel,
        out_shape=[row, low, low, mat, mat, jax.ShapeDtypeStruct((4, dim), F32)],
        grid_spec=pltpu.PrefetchScalarGridSpec(
            num_scalar_prefetch=1,
            grid=(1,),
            in_specs=[
                once(pack_spec, (LONG, dim)),
                once(first_spec, (LONG, dim)),
                once(first_spec, (LONG, dim)),
                once(whole_spec, (LONG, dim // 2)),
                once(whole_spec, (LONG, dim // 2)),
                once(whole_spec, (2, dim)),
                once(whole_spec, (1, dim)),
                once(whole_spec, (1, dim)),
                once(whole_spec, (width, dim)),
                once(whole_spec, (width, dim)),
                once(first_spec, (LONG, width)),
                once(first_spec, (LONG, width)),
            ],
            out_specs=[
                once(first_spec, (LONG, dim)),
                once(first_spec, (LONG, width)),
                once(first_spec, (LONG, width)),
                once(whole_spec, (width, dim)),
                once(whole_spec, (width, dim)),
                once(whole_spec, (4, dim)),
            ],
        ),
        compiler_params=params(),
        cost_estimate=pl.CostEstimate(
            flops=8 * LONG * dim * width, transcendentals=LONG, bytes_accessed=24 * LONG * dim
        ),
        name="middle_back",
    )(scalars, out3, mid, a, mine, peer, ls, gain, shift, *w_parts[:2], *o_parts[:2])


def final_kernel(sc_ref, tok_ref, dmid_ref, mine, peer, gain, shift, out_ref, sum_ref):
    dn1 = joined(sc_ref, mine, peer)
    _, unit, inverse = layer_norm(tok_ref[0].astype(F32), gain[...], shift[...])
    back, d_gain, d_shift = norm_back(dn1, unit, inverse, gain[...])
    result = dmid_ref[0] + back
    half = result.shape[1] // 2
    out_ref[0] = result[:, :half]
    out_ref[1] = result[:, half:]
    sum_ref[0:1] = d_gain
    sum_ref[1:2] = d_shift


def final_back(scalars, tok3, dmid, mine, peer, gain, shift):
    dim = tok3.shape[2]
    return pl.pallas_call(
        final_kernel,
        out_shape=[
            jax.ShapeDtypeStruct((2, LONG, dim // 2), F32),
            jax.ShapeDtypeStruct((2, dim), F32),
        ],
        grid_spec=pltpu.PrefetchScalarGridSpec(
            num_scalar_prefetch=1,
            grid=(1,),
            in_specs=[
                once(pack_spec, (LONG, dim)),
                once(first_spec, (LONG, dim)),
                once(whole_spec, (LONG, dim // 2)),
                once(whole_spec, (LONG, dim // 2)),
                once(whole_spec, (1, dim)),
                once(whole_spec, (1, dim)),
            ],
            out_specs=[once(whole_spec, (2, LONG, dim // 2)), once(whole_spec, (2, dim))],
        ),
        compiler_params=params(),
        cost_estimate=pl.CostEstimate(
            flops=20 * LONG * dim, transcendentals=LONG, bytes_accessed=14 * LONG * dim
        ),
        name="final_back",
    )(scalars, tok3, dmid, mine, peer, gain, shift)


CORE = [(i, i ^ 1) for i in range(4)]
ACROSS = [(i, i ^ 2) for i in range(4)]


def to_core(x):
    return lax.ppermute(x, "narrow", CORE)


def to_chip(x):
    return lax.ppermute(x, "narrow", ACROSS)


def pick(pair, index):
    return lax.dynamic_index_in_dim(pair, index, 0, keepdims=False)


def chip_half(pair, core):
    return pick(pair, core) + to_core(pick(pair, 1 - core))


def small_sum(x, size):
    step = 1
    while step < size:
        x = x + lax.ppermute(x, "wide", [(i, i ^ step) for i in range(size)])
        step *= 2
    return x


def on_device(
    tokens, w_qkv, qv_bias, w_proj, proj_bias, w_fc1, fc1_bias, w_fc2, fc2_bias, norm_gains,
    norm_shifts, layer_scales, rel_table, image_ids, pad_mask, grid_rows, grid_cols, d_out, wide
):
    rows, dim = tokens.shape
    width = w_qkv.shape[2]
    heads = width // HD
    place = lax.axis_index("narrow")
    chip, core = place // 2, place % 2
    gains = norm_gains.astype(F32)
    shifts = norm_shifts.astype(F32)
    scales = layer_scales.astype(F32)
    tok3 = tokens.reshape(2, LONG, dim)
    out3 = d_out.reshape(2, LONG, dim)
    kinds = image_ids.reshape(2, LONG)[:, LONG - 1] % 2
    sc_far = jnp.stack([1 - chip, jnp.where(chip == 0, kinds[1], kinds[0]), core])
    sc_own = jnp.stack([chip, jnp.where(chip == 0, kinds[0], kinds[1]), core])

    wp_near = w_proj.astype(F32)
    wp_far = to_chip(wp_near)
    wp_pair = to_core(jnp.stack([wp_near, wp_far]))
    w_parts = (w_proj, wp_far, wp_pair)

    bias = make_bias(rel_table)
    qv = qv_bias.astype(F32)
    first = lambda sc: attend(sc, tok3, w_qkv, qv, gains[0:1], shifts[0:1], bias)
    o_far, *saved_far = first(sc_far)
    o_own, *saved_own = first(sc_own)
    x_own = to_chip(o_far)
    x_far = to_chip(o_own)
    far_parts = (o_far, x_far, to_core(jnp.stack([o_far, x_far])))
    own_parts = (o_own, x_own, to_core(jnp.stack([o_own, x_own])))

    pb = proj_bias.astype(F32)[None]
    b1 = fc1_bias.astype(F32)[None]
    common = (w_parts, pb, scales, gains[1:2], shifts[1:2], w_fc1, b1, w_fc2)
    mid_far, _, m_far, dn_far, *sums = feed(sc_far, tok3, out3, far_parts, *common, None)
    mid_own, a_own, m_own, dn_own, *sums = feed(sc_own, tok3, out3, own_parts, *common, sums)
    d_fc1, d_fc2, d_fc1_bias, d_fc2_bias = sums

    sent = to_chip(chip_half(dn_far, core))
    mine = chip_half(dn_own, core) + sent
    dmid, do_own, do_send, dp_own, dp_send, sums_two = middle_back(
        sc_own, out3, mid_own, a_own, mine, to_core(mine), scales, gains[1:2], shifts[1:2],
        w_parts, own_parts
    )
    do_far = to_chip(do_send)
    d_proj = dp_own + to_chip(dp_send)

    m_half_far = chip_half(m_far, core)
    m_half_own = chip_half(m_own, core)
    m_all_far = m_half_far + to_chip(m_half_own)
    m_all_own = m_half_own + to_chip(m_half_far)
    m_mine = jnp.where(chip == 0, jnp.stack([m_all_own, m_all_far]), jnp.stack([m_all_far, m_all_own]))
    m_peer = to_core(m_mine)
    m_full = jnp.where(
        core == 0,
        jnp.concatenate([m_mine, m_peer], axis=2),
        jnp.concatenate([m_peer, m_mine], axis=2),
    ) + fc2_bias.astype(F32)
    middle = jnp.where(
        chip == 0, jnp.concatenate([mid_own, mid_far]), jnp.concatenate([mid_far, mid_own])
    )
    block_out = (middle + scales[1] * m_full).astype(BF16).reshape(rows, dim)
    d_scale_two = jnp.sum(out3.astype(F32) * m_full, axis=(0, 1))

    (d_fc1, d_fc2) = lax.psum((d_fc1, d_fc2), "wide")

    back = lambda sc, saved, do, sums: attend_back(
        sc, tok3, w_qkv, gains[0:1], shifts[0:1], bias, saved, do, sums
    )
    dn_far, *sums = back(sc_far, saved_far, do_far, zero_sums(heads, dim, width))
    dn_own, *sums = back(sc_own, saved_own, do_own, sums)
    d_qkv, d_qv_bias, d_large, d_small, d_tails = sums
    sent = to_chip(chip_half(dn_far, core))
    mine = chip_half(dn_own, core) + sent
    tok_own, sums_one = final_back(
        sc_own, tok3, dmid, mine, to_core(mine), gains[0:1], shifts[0:1]
    )
    half_far = to_chip(pick(tok_own, core))
    both = jnp.stack([half_far, to_core(half_far)])
    far_lo = pick(both, core)
    far_hi = pick(both, 1 - core)
    tok_far = jnp.concatenate([far_lo, far_hi], axis=1)
    tok_own = jnp.concatenate([tok_own[0], tok_own[1]], axis=1)
    d_tokens = jnp.where(
        chip == 0, jnp.stack([tok_own, tok_far]), jnp.stack([tok_far, tok_own])
    ).reshape(rows, dim)

    d_table = strips_back(d_large, d_small, d_tails)
    own_rows = jnp.concatenate([sums_two, sums_one])
    own_rows = own_rows + to_chip(own_rows)
    hid = d_fc1_bias.shape[1]
    flat = jnp.concatenate(
        [
            own_rows.reshape(-1),
            d_fc2_bias.reshape(-1),
            d_scale_two,
            d_fc1_bias.reshape(-1),
            d_qv_bias.reshape(-1),
            d_table.reshape(-1),
        ]
    )
    count = flat.shape[0]
    lanes = 128
    flat = jnp.pad(flat, (0, -count % (8 * lanes))).reshape(-1, lanes)
    flat = small_sum(flat, wide).reshape(-1)
    own_rows = flat[: 6 * dim].reshape(6, dim)
    at = 6 * dim
    d_fc2_bias = flat[at : at + dim]
    d_scale_two = flat[at + dim : at + 2 * dim]
    at += 2 * dim
    d_fc1_bias = flat[at : at + hid]
    at += hid
    d_qv_bias = flat[at : at + 2 * width].reshape(2, width)
    at += 2 * width
    d_table = flat[at : at + d_table.size].reshape(d_table.shape)

    d_qkv, d_proj, d_fc1, d_fc2 = lax.optimization_barrier((d_qkv, d_proj, d_fc1, d_fc2))
    d_qkv, d_proj = lax.psum((d_qkv, d_proj), "wide")
    d_norm_gains = jnp.stack([own_rows[4], own_rows[0]])
    d_norm_shifts = jnp.stack([own_rows[5], own_rows[1]])
    d_layer_scales = jnp.stack([own_rows[2], d_scale_two])
    return (
        block_out,
        d_tokens,
        d_qkv,
        d_qv_bias,
        d_proj,
        own_rows[3],
        d_fc1,
        d_fc1_bias,
        d_fc2,
        d_fc2_bias,
        d_norm_gains,
        d_norm_shifts,
        d_layer_scales,
        d_table,
    )


def solution(mesh):
    in_specs = (
        P("wide", None),
        P(None, None, "narrow"),
        P(None, "narrow"),
        P("narrow", None),
        P(),
        P(None, "narrow"),
        P("narrow"),
        P("narrow", None),
        P(),
        P(),
        P(),
        P(),
        P("narrow", None),
        P("wide"),
        P("wide"),
        P("wide"),
        P("wide"),
        P("wide", None),
    )
    out_specs = (
        P("wide", None),
        P("wide", None),
        P(None, None, "narrow"),
        P(None, "narrow"),
        P("narrow", None),
        P(),
        P(None, "narrow"),
        P("narrow"),
        P("narrow", None),
        P(),
        P(),
        P(),
        P(),
        P("narrow", None),
    )
    return jax.shard_map(
        partial(on_device, wide=mesh.shape["wide"]),
        mesh=mesh,
        in_specs=in_specs,
        out_specs=out_specs,
        check_vma=False,
    )
```

```python
from functools import partial

import jax
import jax.numpy as jnp
import numpy as np
from jax import lax
from jax.experimental import pallas as pl
from jax.experimental.pallas import tpu as pltpu
from jax.sharding import PartitionSpec as P

HD = 64
GRID = 24
SMALL = 14
SHORT = 208
LONG = 584
EPSILON = 1e-06
SIDE = 2 * GRID - 1
WIDE_L = 1280
WIDE_S = 640
NEG = -1e30
F32 = jnp.float32
BF16 = jnp.bfloat16
VMEM_LIMIT = 56 << 20
COST_SCALE = 1.2e8


def params(**kw):
    return pltpu.CompilerParams(vmem_limit_bytes=VMEM_LIMIT, **kw)


def spent(microseconds):
    work = int(microseconds * COST_SCALE)
    return pl.CostEstimate(flops=work, transcendentals=0, bytes_accessed=1024)


def dot(a, b):
    return jnp.dot(a, b, preferred_element_type=F32)


def dot_nt(a, b):
    return lax.dot_general(a, b, (((1,), (1,)), ((), ())), preferred_element_type=F32)


def dot_tn(a, b):
    return lax.dot_general(a, b, (((0,), (0,)), ((), ())), preferred_element_type=F32)


def large_pick():
    pick = np.zeros((2, SIDE, GRID, GRID), np.float32)
    for s in range(GRID):
        for c in range(GRID):
            if s == 0:
                pick[1, c, s, c] = 1
            else:
                pick[0, c + GRID - s, s, c] = 1
    return pick.reshape(2 * SIDE, GRID * GRID)


def small_pick():
    pick = np.zeros((SIDE, 16, SMALL), np.float32)
    for s in range(SMALL):
        for c in range(SMALL):
            pick[c - s + GRID - 1, s, c] = 1
    return pick.reshape(SIDE, 16 * SMALL)


def strips(rel_table):
    heads = rel_table.shape[0]
    grid_part = rel_table[:, : SIDE * SIDE].reshape(heads, SIDE, SIDE)
    front = jnp.pad(grid_part, ((0, 0), (1, 0), (0, 0)))
    back = jnp.pad(grid_part, ((0, 0), (0, 1), (0, 0)))
    both = jnp.concatenate([front, back], axis=2)
    large = jnp.einsum(
        "huk,kp->hup", both, jnp.asarray(large_pick(), BF16), preferred_element_type=F32
    ).reshape(heads, SIDE + 1, GRID, GRID)
    large = large.transpose(0, 2, 1, 3).reshape(heads, GRID, (SIDE + 1) * GRID)
    large = jnp.pad(large, ((0, 0), (0, 0), (1, WIDE_L - 1 - (SIDE + 1) * GRID)))
    rows = 2 * SMALL - 1
    part = grid_part[:, GRID - SMALL : GRID - SMALL + rows]
    small = jnp.einsum(
        "huk,kp->hup", part, jnp.asarray(small_pick(), BF16), preferred_element_type=F32
    ).reshape(heads, rows, 16, SMALL)
    small = small.transpose(0, 2, 1, 3).reshape(heads, 16, rows * SMALL)
    small = jnp.pad(small, ((0, 0), (0, 0), (1, WIDE_S - 1 - rows * SMALL)))
    tails = rel_table[:, SIDE * SIDE :].astype(F32)
    return large, small, tails


def strips_back(d_large, d_small, d_tails):
    heads = d_large.shape[0]
    rows = 2 * SMALL - 1
    hi = lax.Precision.HIGHEST
    large = d_large[:, :, 1 : 1 + (SIDE + 1) * GRID].reshape(heads, GRID, SIDE + 1, GRID)
    both = jnp.einsum(
        "hsuc,ksc->huk",
        large,
        jnp.asarray(large_pick().reshape(2 * SIDE, GRID, GRID)),
        precision=hi,
    )
    grid_grad = both[:, 1:, :SIDE] + both[:, :SIDE, SIDE:]
    small = d_small[:, :, 1 : 1 + rows * SMALL].reshape(heads, 16, rows, SMALL)
    part = jnp.einsum(
        "hsuc,ksc->huk", small, jnp.asarray(small_pick().reshape(SIDE, 16, SMALL)), precision=hi
    )
    low = GRID - SMALL
    grid_grad = grid_grad + jnp.pad(part, ((0, 0), (low, SIDE - low - rows), (0, 0)))
    return jnp.concatenate(
        [grid_grad.reshape(heads, SIDE * SIDE), d_tails[:, 0, :3]], axis=1
    )


def tail_fix(block, t0, t1, t2, last, real):
    shape = block.shape
    row = lax.broadcasted_iota(jnp.int32, shape, 0)
    lane = lax.broadcasted_iota(jnp.int32, shape, 1)
    block = jnp.where(lane > last, block[:, 1:2], block)
    block = jnp.where(lane == 0, t0, block)
    block = jnp.where(row == 0, jnp.where(lane == 0, t2, t1), block)
    return jnp.where(row >= real, NEG, block)


def bias_kernel(tail_ref, large_ref, small_ref, out_ref, scr):
    for h in range(large_ref.shape[0]):
        t0, t1, t2 = tail_ref[h, 0], tail_ref[h, 1], tail_ref[h, 2]
        for r in range(GRID + 1):
            size = GRID if r < GRID else LONG - GRID * GRID
            off = (GRID - r) * GRID
            scr[r * GRID : r * GRID + size, 0:LONG] = large_ref[h, 0:size, off : off + LONG]
        last = GRID * GRID
        out_ref[0, h] = tail_fix(scr[:, 0:LONG], t0, t1, t2, last, last + 1).astype(BF16)
        last = SMALL * SMALL
        for r in range(SMALL):
            off = (SMALL - 1 - r) * SMALL
            wide = LONG - SHORT
            scr[1 + r * SMALL : 1 + (r + 1) * SMALL, 0:wide] = small_ref[
                h, 0:SMALL, off : off + wide
            ]
        block = tail_fix(scr[0:SHORT, 0 : LONG - SHORT], t0, t1, t2, last, last + 1)
        scr[...] = jnp.full(scr.shape, NEG, F32)
        scr[0:SHORT, 0:SHORT] = block[:, 0:SHORT]
        scr[SHORT : 2 * SHORT, SHORT:LONG] = block
        out_ref[1, h] = scr[:, 0:LONG].astype(BF16)


def make_bias(rel_table):
    heads = rel_table.shape[0]
    large, small, tails = strips(rel_table)
    return pl.pallas_call(
        bias_kernel,
        out_shape=jax.ShapeDtypeStruct((2, heads, LONG, LONG), BF16),
        in_specs=[
            pl.BlockSpec(memory_space=pltpu.SMEM),
            pl.BlockSpec(memory_space=pltpu.VMEM),
            pl.BlockSpec(memory_space=pltpu.VMEM),
        ],
        out_specs=pl.BlockSpec(memory_space=pltpu.VMEM),
        scratch_shapes=[pltpu.VMEM((LONG, 640), F32)],
        compiler_params=params(),
        cost_estimate=spent(6),
        name="bias",
    )(tails, large, small)


def layer_norm(values, gain_row, shift_row):
    row_mean = jnp.mean(values, axis=-1, keepdims=True)
    centred = values - row_mean
    inverse = lax.rsqrt(jnp.mean(centred * centred, axis=-1, keepdims=True) + EPSILON)
    unit_rows = centred * inverse
    return unit_rows * gain_row + shift_row, unit_rows, inverse


def part_halves(core, value, kept_ref, sent_ref):
    half = value.shape[1] // 2
    lo, hi = value[:, :half], value[:, half:]
    kept_ref[...] = jnp.where(core == 0, lo, hi)
    sent_ref[...] = jnp.where(core == 0, hi, lo)


def head_lanes(shape, h):
    lane = lax.broadcasted_iota(jnp.int32, shape, 1)
    return (lane >= h * HD) & (lane < (h + 1) * HD)


def turned(block):
    return block.astype(F32).T.astype(BF16)


def forward_kernel(
    sc_ref, tok_ref, w_ref, qv_ref, vec, bias_ref, o_ref, q_ref, k_ref, v_ref, lse_ref, n_ref
):
    x = tok_ref[0].astype(F32)
    n1 = layer_norm(x, vec[0:1], vec[1:2])[0].astype(BF16)
    qv = qv_ref[...].astype(F32)
    q = ((dot_nt(n1, w_ref[0]) + qv[0:1]) * HD**-0.5).astype(BF16)
    k = dot_nt(n1, w_ref[1]).astype(BF16)
    v = (dot_nt(n1, w_ref[2]) + qv[1:2]).astype(BF16)
    q_ref[0] = q
    k_ref[0] = k
    v_ref[0] = v
    n_ref[0] = n1
    v_t = turned(v)
    outs = []
    for h in range(k.shape[1] // HD):
        k_h = jnp.where(head_lanes(k.shape, h), k, jnp.zeros_like(k))
        s = dot_nt(k_h, q) + bias_ref[0, h].astype(F32)
        top = jnp.max(s, axis=0, keepdims=True)
        e = jnp.exp(s - top)
        total = jnp.sum(e, axis=0, keepdims=True)
        p = (e * (1.0 / total)).astype(BF16)
        outs.append(dot(v_t[h * HD : (h + 1) * HD], p))
        lse_ref[0, h : h + 1, :] = top + jnp.log(total)
    o_ref[0] = jnp.concatenate(outs, axis=0).astype(BF16).astype(F32)


def once(spec_of, shape):
    spec = spec_of(shape)
    return pl.BlockSpec(spec.block_shape, spec.index_map, pipeline_mode=pl.Buffered(1))


def pack_spec(shape):
    return pl.BlockSpec((1,) + shape, lambda i, sc: (sc[0],) + (0,) * len(shape))


def first_spec(shape):
    return pl.BlockSpec((1,) + shape, lambda i, sc: (0,) * (1 + len(shape)))


def whole_spec(shape):
    return pl.BlockSpec(shape, lambda i, sc: (0,) * len(shape))


def kind_spec(shape):
    return pl.BlockSpec((1,) + shape, lambda i, sc: (sc[1],) + (0,) * len(shape))


def attend(scalars, tok3, w_qkv, qv_bias, vec, bias):
    width = w_qkv.shape[1]
    heads = width // HD
    dim = tok3.shape[2]
    low = jax.ShapeDtypeStruct((1, LONG, width), BF16)
    return pl.pallas_call(
        forward_kernel,
        out_shape=[
            jax.ShapeDtypeStruct((1, width, LONG), F32),
            low,
            low,
            low,
            jax.ShapeDtypeStruct((1, heads, LONG), F32),
            jax.ShapeDtypeStruct((1, LONG, dim), BF16),
        ],
        grid_spec=pltpu.PrefetchScalarGridSpec(
            num_scalar_prefetch=1,
            grid=(1,),
            in_specs=[
                pack_spec((LONG, dim)),
                whole_spec((3, width, dim)),
                whole_spec((2, width)),
                whole_spec((8, dim)),
                kind_spec((heads, LONG, LONG)),
            ],
            out_specs=[first_spec((width, LONG))]
            + [first_spec((LONG, width))] * 3
            + [first_spec((heads, LONG)), first_spec((LONG, dim))],
        ),
        compiler_params=params(),
        cost_estimate=spent(7.4),
        name="attend",
    )(scalars, tok3, w_qkv, qv_bias, vec, bias)


def fold_large(ds, h, dl_ref, dt_ref):
    last = GRID * GRID
    full = ds[:, 0:LONG]
    lane = lax.broadcasted_iota(jnp.int32, full.shape, 1)
    row = lax.broadcasted_iota(jnp.int32, full.shape, 0)
    pad = jnp.sum(jnp.where(lane > last, full, 0.0), axis=1, keepdims=True)
    body = row > 0
    t0 = jnp.sum(jnp.where((lane == 0) & body, full, 0.0))
    t1 = jnp.sum(jnp.where((lane > 0) & (row == 0), full, 0.0))
    t2 = jnp.sum(jnp.where((lane == 0) & (row == 0), full, 0.0))
    full = jnp.where((lane == 0) | (lane > last), 0.0, full)
    full = jnp.where(lane == 1, full + pad, full)
    ds[:, 0:LONG] = jnp.where(body, full, 0.0)
    for r in range(GRID + 1):
        size = GRID if r < GRID else LONG - GRID * GRID
        off = (GRID - r) * GRID
        dl_ref[h, 0:size, off : off + LONG] += ds[r * GRID : r * GRID + size, 0:LONG]
    tail_add(dt_ref, h, t0, t1, t2)


def tail_add(dt_ref, h, t0, t1, t2):
    lane = lax.broadcasted_iota(jnp.int32, (8, 128), 1)
    row = lax.broadcasted_iota(jnp.int32, (8, 128), 0)
    add = jnp.where(lane == 0, t0, jnp.where(lane == 1, t1, jnp.where(lane == 2, t2, 0.0)))
    dt_ref[h] += jnp.where(row == 0, add, 0.0)


def fold_small(ds, h, ds_ref, dt_ref):
    last = SMALL * SMALL
    for base, wide in ((0, SHORT), (SHORT, LONG - SHORT)):
        full = ds[base : base + SHORT, 0:LONG]
        if base:
            full = full[:, base : base + wide]
        else:
            full = full[:, 0:wide]
        lane = lax.broadcasted_iota(jnp.int32, full.shape, 1)
        row = lax.broadcasted_iota(jnp.int32, full.shape, 0)
        pad = jnp.sum(jnp.where(lane > last, full, 0.0), axis=1, keepdims=True)
        body = row > 0
        t0 = jnp.sum(jnp.where((lane == 0) & body, full, 0.0))
        t1 = jnp.sum(jnp.where((lane > 0) & (row == 0), full, 0.0))
        t2 = jnp.sum(jnp.where((lane == 0) & (row == 0), full, 0.0))
        full = jnp.where((lane == 0) | (lane > last), 0.0, full)
        full = jnp.where(lane == 1, full + pad, full)
        ds[base : base + SHORT, 0:wide] = full
        for r in range(SMALL):
            off = (SMALL - 1 - r) * SMALL
            lo = base + 1 + r * SMALL
            ds_ref[h, 0:SMALL, off : off + wide] += ds[lo : lo + SMALL, 0:wide]
        tail_add(dt_ref, h, t0, t1, t2)


def backward_kernel(first, *refs):
    sc_ref, w_ref, bias_ref, q_ref, k_ref, v_ref, do_ref, lse_ref = refs[:8]
    refs = refs[8:]
    if not first:
        al_ref, as_ref, at_ref = refs[:3]
        refs = refs[3:]
    kept_ref, sent_ref, dq_ref, dk_ref, dv_ref, dl_ref, ds_ref, dt_ref, scr = refs
    if first:
        dl_ref[...] = jnp.zeros_like(dl_ref)
        ds_ref[...] = jnp.zeros_like(ds_ref)
        dt_ref[...] = jnp.zeros_like(dt_ref)
    else:
        dl_ref[...] = al_ref[...]
        ds_ref[...] = as_ref[...]
        dt_ref[...] = at_ref[...]
    q, k, v = q_ref[0], k_ref[0], v_ref[0]
    do_t = do_ref[0].astype(BF16)
    do = do_ref[0].T.astype(BF16)
    k_t = turned(k)
    d_qt = []
    d_k = jnp.zeros(k.shape, F32)
    d_v = jnp.zeros(k.shape, F32)
    for h in range(k.shape[1] // HD):
        own = head_lanes(k.shape, h)
        s = dot_nt(jnp.where(own, k, jnp.zeros_like(k)), q) + bias_ref[0, h].astype(F32)
        p = jnp.exp(s - lse_ref[0, h : h + 1, :])
        dp = dot(jnp.where(own, v, jnp.zeros_like(v)), do_t)
        inner = jnp.sum(p * dp, axis=0, keepdims=True)
        ds = (p * (dp - inner)).astype(BF16)
        d_v = jnp.where(own, dot(p.astype(BF16), do), d_v)
        d_k = jnp.where(own, dot(ds, q), d_k)
        d_qt.append(dot(k_t[h * HD : (h + 1) * HD], ds))
        scr[:, 0:LONG] = ds.astype(F32)

        @pl.when(sc_ref[1] == 0)
        def _():
            fold_large(scr, h, dl_ref, dt_ref)

        @pl.when(sc_ref[1] == 1)
        def _():
            fold_small(scr, h, ds_ref, dt_ref)

    d_qt = jnp.concatenate(d_qt, axis=0).astype(BF16) * jnp.asarray(HD**-0.5, BF16)
    d_q = d_qt.astype(F32).T.astype(BF16)
    d_k = d_k.astype(BF16)
    d_v = d_v.astype(BF16)
    dn = dot(d_q, w_ref[0]) + dot(d_k, w_ref[1]) + dot(d_v, w_ref[2])
    part_halves(sc_ref[2], dn, kept_ref, sent_ref)
    dq_ref[...] = d_qt
    dk_ref[...] = turned(d_k)
    dv_ref[...] = turned(d_v)


def attend_back(scalars, w_qkv, bias, saved, do, sums):
    width, dim = w_qkv.shape[1:]
    heads = width // HD
    q, k, v, lse = saved
    first = sums is None
    pair = (LONG, dim // 2)
    sum_shapes = [(heads, GRID, WIDE_L), (heads, 16, WIDE_S), (heads, 8, 128)]
    specs = [
        once(whole_spec, (3, width, dim)),
        once(kind_spec, (heads, LONG, LONG)),
        once(first_spec, (LONG, width)),
        once(first_spec, (LONG, width)),
        once(first_spec, (LONG, width)),
        once(first_spec, (width, LONG)),
        once(first_spec, (heads, LONG)),
    ]
    if not first:
        specs += [once(whole_spec, s) for s in sum_shapes]
    return pl.pallas_call(
        partial(backward_kernel, first),
        out_shape=[jax.ShapeDtypeStruct(pair, F32)] * 2
        + [jax.ShapeDtypeStruct((width, LONG), BF16)] * 3
        + [jax.ShapeDtypeStruct(s, F32) for s in sum_shapes],
        grid_spec=pltpu.PrefetchScalarGridSpec(
            num_scalar_prefetch=1,
            grid=(1,),
            in_specs=specs,
            out_specs=[once(whole_spec, pair)] * 2
            + [once(whole_spec, (width, LONG))] * 3
            + [once(whole_spec, s) for s in sum_shapes],
            scratch_shapes=[pltpu.VMEM((LONG, 640), F32)],
        ),
        compiler_params=params(),
        cost_estimate=spent(12.4),
        name="attend_back",
    )(scalars, w_qkv, bias, q, k, v, do, lse, *(sums or ()))


def qkv_kernel(sc_ref, nf, no, qf, kf, vf, qo, ko, vo, pa, pb, *refs):
    db_ref = refs[4]
    blocks = [
        dot(far[...], nf[0]) + dot(own[...], no[0]) for far, own in ((qf, qo), (kf, ko), (vf, vo))
    ]
    part_blocks(sc_ref[5], blocks + [pa[...] + pb[...]], refs[:4])
    for i, (far, own) in enumerate(((qf, qo), (vf, vo))):
        db_ref[:, i : i + 1] = jnp.sum(far[...].astype(F32), axis=1, keepdims=True) + jnp.sum(
            own[...].astype(F32), axis=1, keepdims=True
        )


def qkv_grad(scalars, n_far, n_own, far, own, proj_a, proj_b):
    dim = n_far.shape[2]
    width = far[0].shape[0]
    return pl.pallas_call(
        qkv_kernel,
        in_specs=[SCALARS] + [PLAIN] * 10,
        out_shape=[jax.ShapeDtypeStruct((width, dim), F32)] * 4
        + [jax.ShapeDtypeStruct((width, 128), F32)],
        compiler_params=params(),
        cost_estimate=spent(4.5),
        name="qkv_grad",
    )(scalars, n_far, n_own, *far, *own, proj_a, proj_b)


def wide_rows(lo_ref, hi_ref):
    return jnp.concatenate([lo_ref[0], hi_ref[0]], axis=1)


def column_sum(x):
    return jnp.sum(x, axis=0, keepdims=True)


def feed_kernel(*refs):
    (sc_ref, tok_ref, out_ref, o0, oc, ox, od, wp0, wpc, wpx, wpd) = refs[:11]
    vec, w1, w2 = refs[11:14]
    mid_ref, a_ref, kept_ref, sent_ref, g_ref, n_ref, du_ref, dm_ref, o_scr, w_scr = refs[14:]
    low = lambda r: r.astype(BF16)
    place = sc_ref[3]
    for hop, (part, weight) in enumerate(((o0, wp0), (oc, wpc), (ox, wpx), (od, wpd))):
        at = place ^ hop
        o_scr[at] = low(part[0])
        w_scr[at] = low(weight[...])
    size = o_scr.shape[0] * o_scr.shape[1]
    o_all = o_scr[...].reshape(size, o_scr.shape[2])
    a = dot_tn(o_all, w_scr[...].reshape(size, w_scr.shape[2])) + vec[6:7]
    a_ref[0] = a
    mid = tok_ref[0].astype(F32) + vec[4:5] * a
    mid_ref[0] = mid
    n2 = layer_norm(mid, vec[2:3], vec[3:4])[0].astype(BF16)
    n_ref[0] = n2
    u = dot(n2, w1[...]) + vec[7:8]
    cdf = 0.5 * (1.0 + lax.erf(u * np.float32(np.sqrt(0.5))))
    slope = cdf + u * (jnp.exp(-0.5 * u * u) * np.float32(1 / np.sqrt(2 * np.pi)))
    g_ref[0] = (u * cdf).astype(BF16)
    dm = (vec[5:6] * out_ref[0].astype(F32)).astype(BF16)
    dm_ref[0] = dm
    du = (slope * dot_nt(dm, w2[...])).astype(BF16)
    du_ref[0] = du
    dn = dot_nt(du, w1[...])
    part_halves(sc_ref[2], dn, kept_ref, sent_ref)


def feed(scalars, tok3, out3, o_parts, w_parts, vec, w1, w2):
    dim = tok3.shape[2]
    hid = w1.shape[1]
    width = w_parts[0].shape[0]
    pair = jax.ShapeDtypeStruct((LONG, dim // 2), F32)
    row = jax.ShapeDtypeStruct((1, LONG, dim), F32)
    low = lambda n: jax.ShapeDtypeStruct((1, LONG, n), BF16)
    specs = (
        [once(pack_spec, (LONG, dim))] * 2
        + [once(first_spec, (width, LONG))] * 4
        + [once(whole_spec, (width, dim))] * 4
        + [
            once(whole_spec, (8, dim)),
            once(whole_spec, (dim, hid)),
            once(whole_spec, (hid, dim)),
        ]
    )
    return pl.pallas_call(
        feed_kernel,
        out_shape=[row, row, pair, pair, low(hid), low(dim), low(hid), low(dim)],
        grid_spec=pltpu.PrefetchScalarGridSpec(
            num_scalar_prefetch=1,
            grid=(1,),
            in_specs=specs,
            out_specs=[once(first_spec, (LONG, dim))] * 2
            + [once(whole_spec, pair.shape)] * 2
            + [once(first_spec, (LONG, n)) for n in (hid, dim, hid, dim)],
            scratch_shapes=[
                pltpu.VMEM((4, width, LONG), BF16),
                pltpu.VMEM((4, width, dim), BF16),
            ],
        ),
        compiler_params=params(),
        cost_estimate=spent(10),
        name="feed",
    )(scalars, tok3, out3, *o_parts, *w_parts, vec, w1, w2)


SCALARS = pl.BlockSpec(memory_space=pltpu.SMEM)
PLAIN = pl.BlockSpec(memory_space=pltpu.VMEM)


def out_kernel(sc_ref, up3, g, w2, kept_ref, sent_ref, sum_ref):
    m = dot(g[0], w2[...])
    part_halves(sc_ref[2], m, kept_ref, sent_ref)
    sum_ref[...] = column_sum(up3[sc_ref[0]].astype(F32) * m)


def feed_out(scalars, up3, g, w2):
    dim = w2.shape[1]
    return pl.pallas_call(
        out_kernel,
        in_specs=[SCALARS, PLAIN, PLAIN, PLAIN],
        out_shape=[jax.ShapeDtypeStruct((LONG, dim // 2), F32)] * 2
        + [jax.ShapeDtypeStruct((1, dim), F32)],
        compiler_params=params(),
        cost_estimate=spent(3.5),
        name="feed_out",
    )(scalars, up3, g, w2)


def part_blocks(bit, blocks, refs):
    for i in range(len(blocks) // 2):
        refs[2 * i][...] = jnp.where(bit == 0, blocks[2 * i], blocks[2 * i + 1])
        refs[2 * i + 1][...] = jnp.where(bit == 0, blocks[2 * i + 1], blocks[2 * i])


def feed_grad_kernel(sc_ref, up3, gf, nf, uf, mf, go, no, uo, mo, w2, *refs):
    db1_ref, db2_ref, kept_ref, sent_ref, sum_ref = refs[6:]
    d1 = dot_tn(nf[0], uf[0]) + dot_tn(no[0], uo[0])
    d2 = dot_tn(gf[0], mf[0]) + dot_tn(go[0], mo[0])
    rows = (d1.shape[0] + d2.shape[0]) // 6
    blocks = [d[i * rows : (i + 1) * rows] for d in (d1, d2) for i in range(3)]
    part_blocks(sc_ref[4], blocks, refs[:6])
    db1_ref[...] = column_sum(uf[0].astype(F32)) + column_sum(uo[0].astype(F32))
    db2_ref[...] = column_sum(mf[0].astype(F32)) + column_sum(mo[0].astype(F32))
    out_kernel(sc_ref, up3, go, w2, kept_ref, sent_ref, sum_ref)


def feed_grad(scalars, up3, far, own, w2):
    hid, dim = w2.shape
    shapes = [(dim // 3, dim)] * 6 + [(1, hid), (1, dim)] + [(LONG, dim // 2)] * 2 + [(1, dim)]
    return pl.pallas_call(
        feed_grad_kernel,
        in_specs=[SCALARS] + [PLAIN] * 10,
        out_shape=[jax.ShapeDtypeStruct(s, F32) for s in shapes],
        compiler_params=params(),
        cost_estimate=spent(9.5),
        name="feed_grad",
    )(scalars, up3, *far, *own, w2)


def norm_back(upstream, unit_rows, inverse, gain_row):
    scaled = upstream * gain_row
    centred = scaled - jnp.mean(scaled, axis=-1, keepdims=True)
    centred = centred - unit_rows * jnp.mean(scaled * unit_rows, axis=-1, keepdims=True)
    return inverse * centred, column_sum(upstream * unit_rows), column_sum(upstream)


def joined(sc_ref, mine, peer):
    core = sc_ref[2]
    lo = jnp.where(core == 0, mine[...], peer[...])
    hi = jnp.where(core == 0, peer[...], mine[...])
    return jnp.concatenate([lo, hi], axis=1)


def middle_kernel(
    sc_ref, out_ref, mid_ref, a_ref, mine, peer, vec, wp0, wpx, o0, ox,
    dmid_ref, do0_ref, dox_ref, dp0_ref, dpx_ref, sum_ref
):
    dn2 = joined(sc_ref, mine, peer)
    _, unit, inverse = layer_norm(mid_ref[0], vec[2:3], vec[3:4])
    back, d_gain, d_shift = norm_back(dn2, unit, inverse, vec[2:3])
    dmid = out_ref[0].astype(F32) + back
    dmid_ref[0] = dmid
    da = (vec[4:5] * dmid).astype(BF16)
    do0_ref[0] = dot_nt(wp0[...], da).astype(BF16).astype(F32)
    dox_ref[0] = dot_nt(wpx[...].astype(BF16), da).astype(BF16).astype(F32)
    dp0_ref[...] = dot(o0[0].astype(BF16), da)
    dpx_ref[...] = dot(ox[0].astype(BF16), da)
    sum_ref[0:1] = d_gain
    sum_ref[1:2] = d_shift
    sum_ref[2:3] = column_sum(dmid * a_ref[0])
    sum_ref[3:4] = column_sum(da.astype(F32))


def middle_back(scalars, out3, mid, a, mine, peer, vec, w_parts, o_parts):
    dim = mid.shape[2]
    width = w_parts[0].shape[0]
    row = jax.ShapeDtypeStruct((1, LONG, dim), F32)
    low = jax.ShapeDtypeStruct((1, width, LONG), F32)
    mat = jax.ShapeDtypeStruct((width, dim), F32)
    return pl.pallas_call(
        middle_kernel,
        out_shape=[row, low, low, mat, mat, jax.ShapeDtypeStruct((4, dim), F32)],
        grid_spec=pltpu.PrefetchScalarGridSpec(
            num_scalar_prefetch=1,
            grid=(1,),
            in_specs=[
                once(pack_spec, (LONG, dim)),
                once(first_spec, (LONG, dim)),
                once(first_spec, (LONG, dim)),
                once(whole_spec, (LONG, dim // 2)),
                once(whole_spec, (LONG, dim // 2)),
                once(whole_spec, (8, dim)),
                once(whole_spec, (width, dim)),
                once(whole_spec, (width, dim)),
                once(first_spec, (width, LONG)),
                once(first_spec, (width, LONG)),
            ],
            out_specs=[
                once(first_spec, (LONG, dim)),
                once(first_spec, (width, LONG)),
                once(first_spec, (width, LONG)),
                once(whole_spec, (width, dim)),
                once(whole_spec, (width, dim)),
                once(whole_spec, (4, dim)),
            ],
        ),
        compiler_params=params(),
        cost_estimate=spent(7.7),
        name="middle_back",
    )(scalars, out3, mid, a, mine, peer, vec, *w_parts[::2], *o_parts[::2])


def final_kernel(sc_ref, tok_ref, dmid_ref, mine, peer, vec, out_ref, sent_ref, sum_ref):
    dn1 = joined(sc_ref, mine, peer)
    _, unit, inverse = layer_norm(tok_ref[0].astype(F32), vec[0:1], vec[1:2])
    back, d_gain, d_shift = norm_back(dn1, unit, inverse, vec[0:1])
    result = dmid_ref[0] + back
    out_ref[0] = result
    half = result.shape[1] // 2
    sent_ref[...] = jnp.where(sc_ref[2] == 0, result[:, :half], result[:, half:])
    sum_ref[0:1] = d_gain
    sum_ref[1:2] = d_shift


def final_back(scalars, tok3, dmid, mine, peer, vec):
    dim = tok3.shape[2]
    return pl.pallas_call(
        final_kernel,
        out_shape=[
            jax.ShapeDtypeStruct((1, LONG, dim), F32),
            jax.ShapeDtypeStruct((LONG, dim // 2), F32),
            jax.ShapeDtypeStruct((2, dim), F32),
        ],
        grid_spec=pltpu.PrefetchScalarGridSpec(
            num_scalar_prefetch=1,
            grid=(1,),
            in_specs=[
                once(pack_spec, (LONG, dim)),
                once(first_spec, (LONG, dim)),
                once(whole_spec, (LONG, dim // 2)),
                once(whole_spec, (LONG, dim // 2)),
                once(whole_spec, (8, dim)),
            ],
            out_specs=[
                once(first_spec, (LONG, dim)),
                once(whole_spec, (LONG, dim // 2)),
                once(whole_spec, (2, dim)),
            ],
        ),
        compiler_params=params(),
        cost_estimate=spent(5.6),
        name="final_back",
    )(scalars, tok3, dmid, mine, peer, vec)


CORE = [(i, i ^ 1) for i in range(4)]
ACROSS = [(i, i ^ 2) for i in range(4)]


def to_core(x):
    return lax.ppermute(x, "narrow", CORE)


def to_chip(x):
    return lax.ppermute(x, "narrow", ACROSS)


def pick(pair, index):
    return lax.dynamic_index_in_dim(pair, index, 0, keepdims=False)


def small_sum(x, size):
    step = 1
    while step < size:
        x = x + lax.ppermute(x, "wide", [(i, i ^ step) for i in range(size)])
        step *= 2
    return x


def tie(*values):
    return lax.optimization_barrier(values)


def in_order(bit, first, second):
    return jnp.where(bit == 0, first, second), jnp.where(bit == 0, second, first)


WIDE_PLACES = 8


class Wave:
    def __init__(self, place):
        self.place = place
        self.live = []
        self.done = {}

    def bit(self, step):
        return (self.place // step) % 2

    def send(self, value, step):
        return lax.ppermute(value, "wide", [(i, i ^ step) for i in range(WIDE_PLACES)])

    def add(self, name, kept, sent, steps, due):
        self.live.append([name, steps, 0, kept, self.send(sent, steps[0]), due])

    def event(self, now, dep, then):
        ripe = [c for c in self.live if c[5] <= now]
        if not ripe:
            return tie(dep, then)[1]
        values = tie(dep, *[c[4] for c in ripe])[1:]
        moves = []
        for c, got in zip(ripe, values):
            steps, stage, kept = c[1:4]
            if stage == 0:
                rows = kept.shape[0] // 2
                split = lambda v: v.reshape((2, rows) + v.shape[1:])
                side = self.bit(steps[1])
                kept, got = split(kept), split(got)
                moves.append((pick(kept, side) + pick(got, side), pick(kept, 1 - side) + pick(got, 1 - side)))
            elif stage < 3:
                total = kept + got
                moves.append((total, total))
            elif stage == 3:
                total = jnp.concatenate(in_order(self.bit(steps[1]), kept, got))
                moves.append((total, total))
            else:
                self.done[c[0]] = in_order(self.bit(steps[0]), kept, got)
                self.live.remove(c)
        ripe = [c for c in ripe if c[2] < 4]
        if not ripe:
            return then
        held = tie(then, *[m[1] for m in moves])
        for c, (kept, _), value in zip(ripe, moves, held[1:]):
            step = c[1][(1, 2, 1, 0)[c[2]]]
            kept = value if c[2] else kept
            c[2:] = [c[2] + 1, kept, self.send(value, step), c[5] + 1]
        return held[0]


def on_device(
    tokens, w_qkv, qv_bias, w_proj, proj_bias, w_fc1, fc1_bias, w_fc2, fc2_bias, norm_gains,
    norm_shifts, layer_scales, rel_table, image_ids, pad_mask, grid_rows, grid_cols, d_out, wide
):
    rows, dim = tokens.shape
    width = w_qkv.shape[2]
    place = lax.axis_index("narrow")
    chip, core = place // 2, place % 2
    spot = lax.axis_index("wide")
    tok3 = tokens.reshape(2, LONG, dim)
    out3 = d_out.reshape(2, LONG, dim)
    w_turned = w_qkv.transpose(0, 2, 1)
    kind_a = image_ids[LONG - 1] % 2
    kind_b = image_ids[2 * LONG - 1] % 2
    common = (core, place, spot % 2, (spot // 2) % 2)
    sc_far = jnp.stack([1 - chip, jnp.where(chip == 0, kind_b, kind_a), *common])
    sc_own = jnp.stack([chip, jnp.where(chip == 0, kind_a, kind_b), *common])
    pairs = zip(norm_gains.astype(F32), norm_shifts.astype(F32))
    vec = jnp.stack(
        [v for pair in pairs for v in pair]
        + list(layer_scales.astype(F32))
        + [proj_bias.astype(F32), fc1_bias.astype(F32)]
    )

    wp_near = w_proj.astype(F32)
    wp_far = to_chip(wp_near)
    bias = make_bias(rel_table)
    first = lambda sc: attend(sc, tok3, w_turned, qv_bias, vec, bias)
    o_far, *saved_far, n_far = first(sc_far)
    wp_far, o_sent = tie(wp_far, o_far)
    x_own = to_chip(o_sent)
    w_parts = (w_proj, to_core(wp_near), wp_far, to_core(wp_far))
    o_own, *saved_own, n_own = first(sc_own)
    x_own, o_sent = tie(x_own, o_own)
    x_far = to_chip(o_sent)
    far_parts = (o_far, to_core(o_far), x_far, to_core(x_far))
    own_parts = (o_own, to_core(o_own), x_own, to_core(x_own))

    shared = (w_parts, vec, w_fc1, w_fc2)
    mid_far, _, dn_kept, dn_send, *kept_far = feed(sc_far, tok3, out3, far_parts, *shared)
    peer = to_core(dn_send)
    sc, _ = tie(sc_far, dn_send)
    m_far_kept, m_far_send, scale_far = feed_out(sc, out3, kept_far[0], w_fc2)
    peer, m_far_kept = tie(peer, m_far_kept)
    half, sc = tie(dn_kept + peer, sc_own)
    dn_got = to_chip(half)
    mid_own, a_own, dn_kept, dn_send, *kept_own = feed(sc, tok3, out3, own_parts, *shared)
    peer = to_core(dn_send)
    *blocks, d_fc1_bias, d_fc2_bias, m_own_kept, m_own_send, scale_own = feed_grad(
        sc_own, out3, kept_far, kept_own, w_fc2
    )

    wave = Wave(spot)
    custom = wide == WIDE_PLACES
    for i in range(3):
        if custom:
            wave.add(i, blocks[2 * i], blocks[2 * i + 1], (1, 2, 4), i + 1)
    dn_got, m_own_kept = tie(dn_got, m_own_kept)
    part, peer = tie(dn_kept + dn_got, peer)
    mine = part + peer
    theirs = to_core(mine)
    dmid, do_own, do_send, dp_own, dp_send, sums_two = middle_back(
        sc_own, out3, mid_own, a_own, mine, theirs, vec, w_parts, own_parts
    )
    do_far = to_chip(do_send)
    do_far, m_far_send, m_own_send = tie(do_far, m_far_send, m_own_send)
    m_far_peer = to_core(m_far_send)
    m_own_peer = to_core(m_own_send)
    do_far, sc = tie(do_far, sc_far)
    sc = wave.event(1, do_far, sc)
    dp_send, sc = tie(dp_send, sc)
    dp_got = to_chip(dp_send)

    dn_kept, dn_send, *far, dl, ds, dt = attend_back(sc, w_turned, bias, saved_far, do_far, None)
    dn_send, dp_got = tie(dn_send, dp_got)
    dn_send = wave.event(2, dn_send, dn_send)
    peer = to_core(dn_send)
    half, sc, dp_got = tie(dn_kept + peer, sc_own, dp_got)
    dn_got = to_chip(half)
    dn_kept, dn_send, *own, dl, ds, dt = attend_back(
        sc, w_turned, bias, saved_own, do_own, (dl, ds, dt)
    )
    dn_send = wave.event(3, dn_send, dn_send)
    peer = to_core(dn_send)
    *pieces, d_qv_bias = qkv_grad(sc_own, n_far, n_own, far, own, dp_own, dp_got)
    if custom:
        wave.add("qk", pieces[0], pieces[1], (2, 1, 4), 5)
        wave.add("vp", pieces[2], pieces[3], (2, 1, 4), 6)
    dn_got, d_qv_bias = tie(dn_got, d_qv_bias)
    part, peer = tie(dn_kept + dn_got, peer)
    mine = part + peer
    theirs = to_core(mine)
    m_far_peer, m_own_peer, mine_ = tie(m_far_peer, m_own_peer, mine)
    m_half_far = m_far_kept + m_far_peer
    m_half_own = m_own_kept + m_own_peer
    m_send, sc = tie(m_half_far, sc_own)
    m_all_own = to_chip(m_send)
    tok_own, tok_send, sums_one = final_back(sc, tok3, dmid, mine, theirs, vec)
    tok_send, m_all_own = tie(tok_send, m_all_own)
    tok_send = wave.event(4, tok_send, tok_send)
    tok_got = to_chip(tok_send)
    m_all_own = m_half_own + m_all_own

    d_table = strips_back(dl, ds, dt)
    scale = scale_far + scale_own
    scale = scale + to_core(scale)
    own_rows = jnp.concatenate([sums_two, sums_one, scale])
    own_rows = own_rows + to_chip(own_rows)
    hid = d_fc1_bias.shape[1]
    flat = jnp.concatenate(
        [
            own_rows.reshape(-1),
            d_fc2_bias.reshape(-1),
            d_fc1_bias.reshape(-1),
            jnp.sum(d_out.astype(F32), axis=0),
            d_qv_bias[:, 0],
            d_qv_bias[:, 1],
            d_table.reshape(-1),
        ]
    )
    lanes = 128
    flat = jnp.pad(flat, (0, -flat.shape[0] % (8 * lanes))).reshape(-1, lanes)
    flat = small_sum(flat, wide).reshape(-1)
    own_rows = flat[: 7 * dim].reshape(7, dim)
    at = 7 * dim
    d_fc2_bias = flat[at : at + dim]
    at += dim
    d_fc1_bias = flat[at : at + hid]
    at += hid
    d_scale_two = own_rows[6] + fc2_bias.astype(F32) * flat[at : at + dim]
    at += dim
    d_qv_bias = flat[at : at + 2 * width].reshape(2, width)
    at += 2 * width
    d_table = flat[at : at + d_table.size].reshape(d_table.shape)

    tok_got = wave.event(5, tok_got, tok_got)
    m_send, tok_got = tie(m_half_own, tok_got)
    m_all_far = to_chip(m_send)
    tok_peer = to_core(tok_got)
    tok_far = jnp.concatenate(in_order(core, tok_got, tok_peer), axis=1)[None]
    d_tokens = jnp.concatenate(in_order(chip, tok_own, tok_far)).reshape(rows, dim)
    mark = wave.event(6, tok_got, tok_got)
    mark = wave.event(7, mark, mark)
    m_all_far, mark = tie(m_all_far, mark)
    m_all_far = m_half_far + m_all_far
    m_far = jnp.concatenate(in_order(core, m_all_far, to_core(m_all_far)), axis=1)[None]
    m_own = jnp.concatenate(in_order(core, m_all_own, to_core(m_all_own)), axis=1)[None]
    m_full = jnp.concatenate(in_order(chip, m_own, m_far)) + fc2_bias.astype(F32)
    middle = jnp.concatenate(in_order(chip, mid_own, mid_far))
    block_out = (middle + layer_scales[1].astype(F32) * m_full).astype(BF16).reshape(rows, dim)
    mark = wave.event(8, mark, mark)

    now = 9
    while wave.live:
        mark = wave.event(now, mark, mark)
        now += 1
    if custom:
        got = wave.done
        blocks = [b for i in range(3) for b in got[i]]
        pieces = got["qk"] + got["vp"]
    else:
        out = []
        for i in range(3):
            out += in_order(spot % 2, blocks[2 * i], blocks[2 * i + 1])
        for i in range(2):
            out += in_order((spot // 2) % 2, pieces[2 * i], pieces[2 * i + 1])
        out = lax.psum(tuple(out), "wide")
        blocks, pieces = out[:6], out[6:]
    d_fc1 = jnp.concatenate(blocks[:3])
    d_fc2 = jnp.concatenate(blocks[3:])
    d_qkv = jnp.stack(pieces[:3]).transpose(0, 2, 1)
    d_norm_gains = jnp.stack([own_rows[4], own_rows[0]])
    d_norm_shifts = jnp.stack([own_rows[5], own_rows[1]])
    d_layer_scales = jnp.stack([own_rows[2], d_scale_two])
    return (
        block_out,
        d_tokens,
        d_qkv,
        d_qv_bias,
        pieces[3],
        own_rows[3],
        d_fc1,
        d_fc1_bias,
        d_fc2,
        d_fc2_bias,
        d_norm_gains,
        d_norm_shifts,
        d_layer_scales,
        d_table,
    )


def solution(mesh):
    in_specs = (
        P("wide", None),
        P(None, None, "narrow"),
        P(None, "narrow"),
        P("narrow", None),
        P(),
        P(None, "narrow"),
        P("narrow"),
        P("narrow", None),
        P(),
        P(),
        P(),
        P(),
        P("narrow", None),
        P("wide"),
        P("wide"),
        P("wide"),
        P("wide"),
        P("wide", None),
    )
    out_specs = (
        P("wide", None),
        P("wide", None),
        P(None, None, "narrow"),
        P(None, "narrow"),
        P("narrow", None),
        P(),
        P(None, "narrow"),
        P("narrow"),
        P("narrow", None),
        P(),
        P(),
        P(),
        P(),
        P("narrow", None),
    )
    return jax.shard_map(
        partial(on_device, wide=mesh.shape["wide"]),
        mesh=mesh,
        in_specs=in_specs,
        out_specs=out_specs,
        check_vma=False,
    )
```

```python
from functools import partial

import jax
import jax.numpy as jnp
import numpy as np
from jax import lax
from jax.experimental import pallas as pl
from jax.experimental.pallas import tpu as pltpu
from jax.sharding import PartitionSpec as P

HD = 64
GRID = 24
SMALL = 14
SHORT = 208
LONG = 584
EPSILON = 1e-06
SIDE = 2 * GRID - 1
WIDE_L = 1280
WIDE_S = 640
NEG = -1e30
F32 = jnp.float32
BF16 = jnp.bfloat16
VMEM_LIMIT = 56 << 20
COST_SCALE = 1.2e8


def params(**kw):
    return pltpu.CompilerParams(vmem_limit_bytes=VMEM_LIMIT, **kw)


def spent(microseconds):
    work = int(microseconds * COST_SCALE)
    return pl.CostEstimate(flops=work, transcendentals=0, bytes_accessed=1024)


def dot(a, b):
    return jnp.dot(a, b, preferred_element_type=F32)


def dot_nt(a, b):
    return lax.dot_general(a, b, (((1,), (1,)), ((), ())), preferred_element_type=F32)


def dot_tn(a, b):
    return lax.dot_general(a, b, (((0,), (0,)), ((), ())), preferred_element_type=F32)


def large_pick():
    pick = np.zeros((2, SIDE, GRID, GRID), np.float32)
    for s in range(GRID):
        for c in range(GRID):
            if s == 0:
                pick[1, c, s, c] = 1
            else:
                pick[0, c + GRID - s, s, c] = 1
    return pick.reshape(2 * SIDE, GRID * GRID)


def small_pick():
    pick = np.zeros((SIDE, 16, SMALL), np.float32)
    for s in range(SMALL):
        for c in range(SMALL):
            pick[c - s + GRID - 1, s, c] = 1
    return pick.reshape(SIDE, 16 * SMALL)


def strips(rel_table):
    heads = rel_table.shape[0]
    grid_part = rel_table[:, : SIDE * SIDE].reshape(heads, SIDE, SIDE)
    front = jnp.pad(grid_part, ((0, 0), (1, 0), (0, 0)))
    back = jnp.pad(grid_part, ((0, 0), (0, 1), (0, 0)))
    both = jnp.concatenate([front, back], axis=2)
    large = jnp.einsum(
        "huk,kp->hup", both, jnp.asarray(large_pick(), BF16), preferred_element_type=F32
    ).reshape(heads, SIDE + 1, GRID, GRID)
    large = large.transpose(0, 2, 1, 3).reshape(heads, GRID, (SIDE + 1) * GRID)
    large = jnp.pad(large, ((0, 0), (0, 0), (1, WIDE_L - 1 - (SIDE + 1) * GRID)))
    rows = 2 * SMALL - 1
    part = grid_part[:, GRID - SMALL : GRID - SMALL + rows]
    small = jnp.einsum(
        "huk,kp->hup", part, jnp.asarray(small_pick(), BF16), preferred_element_type=F32
    ).reshape(heads, rows, 16, SMALL)
    small = small.transpose(0, 2, 1, 3).reshape(heads, 16, rows * SMALL)
    small = jnp.pad(small, ((0, 0), (0, 0), (1, WIDE_S - 1 - rows * SMALL)))
    tails = rel_table[:, SIDE * SIDE :].astype(F32)
    return large, small, tails


def strips_back(d_large, d_small, d_tails):
    heads = d_large.shape[0]
    rows = 2 * SMALL - 1
    hi = lax.Precision.HIGHEST
    large = d_large[:, :, 1 : 1 + (SIDE + 1) * GRID].reshape(heads, GRID, SIDE + 1, GRID)
    both = jnp.einsum(
        "hsuc,ksc->huk",
        large,
        jnp.asarray(large_pick().reshape(2 * SIDE, GRID, GRID)),
        precision=hi,
    )
    grid_grad = both[:, 1:, :SIDE] + both[:, :SIDE, SIDE:]
    small = d_small[:, :, 1 : 1 + rows * SMALL].reshape(heads, 16, rows, SMALL)
    part = jnp.einsum(
        "hsuc,ksc->huk", small, jnp.asarray(small_pick().reshape(SIDE, 16, SMALL)), precision=hi
    )
    low = GRID - SMALL
    grid_grad = grid_grad + jnp.pad(part, ((0, 0), (low, SIDE - low - rows), (0, 0)))
    return jnp.concatenate(
        [grid_grad.reshape(heads, SIDE * SIDE), d_tails[:, 0, :3]], axis=1
    )


def tail_fix(block, t0, t1, t2, last, real):
    shape = block.shape
    row = lax.broadcasted_iota(jnp.int32, shape, 0)
    lane = lax.broadcasted_iota(jnp.int32, shape, 1)
    block = jnp.where(lane > last, block[:, 1:2], block)
    block = jnp.where(lane == 0, t0, block)
    block = jnp.where(row == 0, jnp.where(lane == 0, t2, t1), block)
    return jnp.where(row >= real, NEG, block)


def bias_kernel(tail_ref, large_ref, small_ref, out_ref, scr):
    for h in range(large_ref.shape[0]):
        t0, t1, t2 = tail_ref[h, 0], tail_ref[h, 1], tail_ref[h, 2]
        for r in range(GRID + 1):
            size = GRID if r < GRID else LONG - GRID * GRID
            off = (GRID - r) * GRID
            scr[r * GRID : r * GRID + size, 0:LONG] = large_ref[h, 0:size, off : off + LONG]
        last = GRID * GRID
        out_ref[0, h] = tail_fix(scr[:, 0:LONG], t0, t1, t2, last, last + 1).astype(BF16)
        last = SMALL * SMALL
        for r in range(SMALL):
            off = (SMALL - 1 - r) * SMALL
            wide = LONG - SHORT
            scr[1 + r * SMALL : 1 + (r + 1) * SMALL, 0:wide] = small_ref[
                h, 0:SMALL, off : off + wide
            ]
        block = tail_fix(scr[0:SHORT, 0 : LONG - SHORT], t0, t1, t2, last, last + 1)
        scr[...] = jnp.full(scr.shape, NEG, F32)
        scr[0:SHORT, 0:SHORT] = block[:, 0:SHORT]
        scr[SHORT : 2 * SHORT, SHORT:LONG] = block
        out_ref[1, h] = scr[:, 0:LONG].astype(BF16)


def make_bias(rel_table):
    heads = rel_table.shape[0]
    large, small, tails = strips(rel_table)
    return pl.pallas_call(
        bias_kernel,
        out_shape=jax.ShapeDtypeStruct((2, heads, LONG, LONG), BF16),
        in_specs=[
            pl.BlockSpec(memory_space=pltpu.SMEM),
            pl.BlockSpec(memory_space=pltpu.VMEM),
            pl.BlockSpec(memory_space=pltpu.VMEM),
        ],
        out_specs=pl.BlockSpec(memory_space=pltpu.VMEM),
        scratch_shapes=[pltpu.VMEM((LONG, 640), F32)],
        compiler_params=params(),
        cost_estimate=spent(6),
        name="bias",
    )(tails, large, small)


def layer_norm(values, gain_row, shift_row):
    row_mean = jnp.mean(values, axis=-1, keepdims=True)
    centred = values - row_mean
    inverse = lax.rsqrt(jnp.mean(centred * centred, axis=-1, keepdims=True) + EPSILON)
    unit_rows = centred * inverse
    return unit_rows * gain_row + shift_row, unit_rows, inverse


def part_halves(core, value, kept_ref, sent_ref):
    half = value.shape[1] // 2
    lo, hi = value[:, :half], value[:, half:]
    kept_ref[...] = jnp.where(core == 0, lo, hi)
    sent_ref[...] = jnp.where(core == 0, hi, lo)


def head_lanes(shape, h):
    lane = lax.broadcasted_iota(jnp.int32, shape, 1)
    return (lane >= h * HD) & (lane < (h + 1) * HD)


def turned(block):
    return block.astype(F32).T.astype(BF16)


def forward_kernel(
    sc_ref, tok_ref, w_ref, qv_ref, vec, bias_ref, o_ref, q_ref, k_ref, v_ref, lse_ref, n_ref
):
    x = tok_ref[0].astype(F32)
    n1 = layer_norm(x, vec[0:1], vec[1:2])[0].astype(BF16)
    qv = qv_ref[...].astype(F32)
    q = ((dot_nt(n1, w_ref[0]) + qv[0:1]) * HD**-0.5).astype(BF16)
    k = dot_nt(n1, w_ref[1]).astype(BF16)
    v = (dot_nt(n1, w_ref[2]) + qv[1:2]).astype(BF16)
    q_ref[0] = q
    k_ref[0] = k
    v_ref[0] = v
    n_ref[0] = n1
    v_t = turned(v)
    outs = []
    for h in range(k.shape[1] // HD):
        k_h = jnp.where(head_lanes(k.shape, h), k, jnp.zeros_like(k))
        s = dot_nt(k_h, q) + bias_ref[0, h].astype(F32)
        top = jnp.max(s, axis=0, keepdims=True)
        e = jnp.exp(s - top)
        total = jnp.sum(e, axis=0, keepdims=True)
        p = (e * (1.0 / total)).astype(BF16)
        outs.append(dot(v_t[h * HD : (h + 1) * HD], p))
        lse_ref[0, h : h + 1, :] = top + jnp.log(total)
    o_ref[0] = jnp.concatenate(outs, axis=0).astype(BF16).astype(F32)


def once(spec_of, shape):
    spec = spec_of(shape)
    return pl.BlockSpec(spec.block_shape, spec.index_map, pipeline_mode=pl.Buffered(1))


def pack_spec(shape):
    return pl.BlockSpec((1,) + shape, lambda i, sc: (sc[0],) + (0,) * len(shape))


def first_spec(shape):
    return pl.BlockSpec((1,) + shape, lambda i, sc: (0,) * (1 + len(shape)))


def whole_spec(shape):
    return pl.BlockSpec(shape, lambda i, sc: (0,) * len(shape))


def kind_spec(shape):
    return pl.BlockSpec((1,) + shape, lambda i, sc: (sc[1],) + (0,) * len(shape))


def attend(scalars, tok3, w_qkv, qv_bias, vec, bias):
    width = w_qkv.shape[1]
    heads = width // HD
    dim = tok3.shape[2]
    low = jax.ShapeDtypeStruct((1, LONG, width), BF16)
    return pl.pallas_call(
        forward_kernel,
        out_shape=[
            jax.ShapeDtypeStruct((1, width, LONG), F32),
            low,
            low,
            low,
            jax.ShapeDtypeStruct((1, heads, LONG), F32),
            jax.ShapeDtypeStruct((1, LONG, dim), BF16),
        ],
        grid_spec=pltpu.PrefetchScalarGridSpec(
            num_scalar_prefetch=1,
            grid=(1,),
            in_specs=[
                pack_spec((LONG, dim)),
                whole_spec((3, width, dim)),
                whole_spec((2, width)),
                whole_spec((8, dim)),
                kind_spec((heads, LONG, LONG)),
            ],
            out_specs=[first_spec((width, LONG))]
            + [first_spec((LONG, width))] * 3
            + [first_spec((heads, LONG)), first_spec((LONG, dim))],
        ),
        compiler_params=params(),
        cost_estimate=spent(7.4),
        name="attend",
    )(scalars, tok3, w_qkv, qv_bias, vec, bias)


def fold_large(ds, h, dl_ref, dt_ref):
    last = GRID * GRID
    full = ds[:, 0:LONG]
    lane = lax.broadcasted_iota(jnp.int32, full.shape, 1)
    row = lax.broadcasted_iota(jnp.int32, full.shape, 0)
    pad = jnp.sum(jnp.where(lane > last, full, 0.0), axis=1, keepdims=True)
    body = row > 0
    t0 = jnp.sum(jnp.where((lane == 0) & body, full, 0.0))
    t1 = jnp.sum(jnp.where((lane > 0) & (row == 0), full, 0.0))
    t2 = jnp.sum(jnp.where((lane == 0) & (row == 0), full, 0.0))
    full = jnp.where((lane == 0) | (lane > last), 0.0, full)
    full = jnp.where(lane == 1, full + pad, full)
    ds[:, 0:LONG] = jnp.where(body, full, 0.0)
    for r in range(GRID + 1):
        size = GRID if r < GRID else LONG - GRID * GRID
        off = (GRID - r) * GRID
        dl_ref[h, 0:size, off : off + LONG] += ds[r * GRID : r * GRID + size, 0:LONG]
    tail_add(dt_ref, h, t0, t1, t2)


def tail_add(dt_ref, h, t0, t1, t2):
    lane = lax.broadcasted_iota(jnp.int32, (8, 128), 1)
    row = lax.broadcasted_iota(jnp.int32, (8, 128), 0)
    add = jnp.where(lane == 0, t0, jnp.where(lane == 1, t1, jnp.where(lane == 2, t2, 0.0)))
    dt_ref[h] += jnp.where(row == 0, add, 0.0)


def fold_small(ds, h, ds_ref, dt_ref):
    last = SMALL * SMALL
    for base, wide in ((0, SHORT), (SHORT, LONG - SHORT)):
        full = ds[base : base + SHORT, 0:LONG]
        if base:
            full = full[:, base : base + wide]
        else:
            full = full[:, 0:wide]
        lane = lax.broadcasted_iota(jnp.int32, full.shape, 1)
        row = lax.broadcasted_iota(jnp.int32, full.shape, 0)
        pad = jnp.sum(jnp.where(lane > last, full, 0.0), axis=1, keepdims=True)
        body = row > 0
        t0 = jnp.sum(jnp.where((lane == 0) & body, full, 0.0))
        t1 = jnp.sum(jnp.where((lane > 0) & (row == 0), full, 0.0))
        t2 = jnp.sum(jnp.where((lane == 0) & (row == 0), full, 0.0))
        full = jnp.where((lane == 0) | (lane > last), 0.0, full)
        full = jnp.where(lane == 1, full + pad, full)
        ds[base : base + SHORT, 0:wide] = full
        for r in range(SMALL):
            off = (SMALL - 1 - r) * SMALL
            lo = base + 1 + r * SMALL
            ds_ref[h, 0:SMALL, off : off + wide] += ds[lo : lo + SMALL, 0:wide]
        tail_add(dt_ref, h, t0, t1, t2)


def backward_kernel(first, *refs):
    sc_ref, w_ref, bias_ref, q_ref, k_ref, v_ref, do_ref, lse_ref = refs[:8]
    refs = refs[8:]
    if not first:
        al_ref, as_ref, at_ref = refs[:3]
        refs = refs[3:]
    kept_ref, sent_ref, dq_ref, dk_ref, dv_ref, dl_ref, ds_ref, dt_ref, scr = refs
    if first:
        dl_ref[...] = jnp.zeros_like(dl_ref)
        ds_ref[...] = jnp.zeros_like(ds_ref)
        dt_ref[...] = jnp.zeros_like(dt_ref)
    else:
        dl_ref[...] = al_ref[...]
        ds_ref[...] = as_ref[...]
        dt_ref[...] = at_ref[...]
    q, k, v = q_ref[0], k_ref[0], v_ref[0]
    do_t = do_ref[0].astype(BF16)
    do = do_ref[0].T.astype(BF16)
    k_t = turned(k)
    d_qt = []
    d_k = jnp.zeros(k.shape, F32)
    d_v = jnp.zeros(k.shape, F32)
    for h in range(k.shape[1] // HD):
        own = head_lanes(k.shape, h)
        s = dot_nt(jnp.where(own, k, jnp.zeros_like(k)), q) + bias_ref[0, h].astype(F32)
        p = jnp.exp(s - lse_ref[0, h : h + 1, :])
        dp = dot(jnp.where(own, v, jnp.zeros_like(v)), do_t)
        inner = jnp.sum(p * dp, axis=0, keepdims=True)
        ds = (p * (dp - inner)).astype(BF16)
        d_v = jnp.where(own, dot(p.astype(BF16), do), d_v)
        d_k = jnp.where(own, dot(ds, q), d_k)
        d_qt.append(dot(k_t[h * HD : (h + 1) * HD], ds))
        scr[:, 0:LONG] = ds.astype(F32)

        @pl.when(sc_ref[1] == 0)
        def _():
            fold_large(scr, h, dl_ref, dt_ref)

        @pl.when(sc_ref[1] == 1)
        def _():
            fold_small(scr, h, ds_ref, dt_ref)

    d_qt = jnp.concatenate(d_qt, axis=0).astype(BF16) * jnp.asarray(HD**-0.5, BF16)
    d_q = d_qt.astype(F32).T.astype(BF16)
    d_k = d_k.astype(BF16)
    d_v = d_v.astype(BF16)
    dn = dot(d_q, w_ref[0]) + dot(d_k, w_ref[1]) + dot(d_v, w_ref[2])
    part_halves(sc_ref[2], dn, kept_ref, sent_ref)
    dq_ref[...] = d_qt
    dk_ref[...] = turned(d_k)
    dv_ref[...] = turned(d_v)


def attend_back(scalars, w_qkv, bias, saved, do, sums):
    width, dim = w_qkv.shape[1:]
    heads = width // HD
    q, k, v, lse = saved
    first = sums is None
    pair = (LONG, dim // 2)
    sum_shapes = [(heads, GRID, WIDE_L), (heads, 16, WIDE_S), (heads, 8, 128)]
    specs = [
        once(whole_spec, (3, width, dim)),
        once(kind_spec, (heads, LONG, LONG)),
        once(first_spec, (LONG, width)),
        once(first_spec, (LONG, width)),
        once(first_spec, (LONG, width)),
        once(first_spec, (width, LONG)),
        once(first_spec, (heads, LONG)),
    ]
    if not first:
        specs += [once(whole_spec, s) for s in sum_shapes]
    return pl.pallas_call(
        partial(backward_kernel, first),
        out_shape=[jax.ShapeDtypeStruct(pair, F32)] * 2
        + [jax.ShapeDtypeStruct((width, LONG), BF16)] * 3
        + [jax.ShapeDtypeStruct(s, F32) for s in sum_shapes],
        grid_spec=pltpu.PrefetchScalarGridSpec(
            num_scalar_prefetch=1,
            grid=(1,),
            in_specs=specs,
            out_specs=[once(whole_spec, pair)] * 2
            + [once(whole_spec, (width, LONG))] * 3
            + [once(whole_spec, s) for s in sum_shapes],
            scratch_shapes=[pltpu.VMEM((LONG, 640), F32)],
        ),
        compiler_params=params(),
        cost_estimate=spent(12.4),
        name="attend_back",
    )(scalars, w_qkv, bias, q, k, v, do, lse, *(sums or ()))


def qkv_kernel(sc_ref, nf, no, qf, kf, vf, qo, ko, vo, pa, pb, *refs):
    db_ref = refs[2]
    blocks = [
        dot(far[...], nf[0]) + dot(own[...], no[0]) for far, own in ((qf, qo), (kf, ko), (vf, vo))
    ]
    blocks.append(pa[...] + pb[...])
    rows = blocks[0].shape[0]
    for i in range(2):
        at = pl.ds(i * rows, rows)
        refs[0][at] = jnp.where(sc_ref[4] == 0, blocks[i], blocks[2 + i])
        refs[1][at] = jnp.where(sc_ref[4] == 0, blocks[2 + i], blocks[i])
    for i, (far, own) in enumerate(((qf, qo), (vf, vo))):
        db_ref[:, i : i + 1] = jnp.sum(far[...].astype(F32), axis=1, keepdims=True) + jnp.sum(
            own[...].astype(F32), axis=1, keepdims=True
        )


def qkv_grad(scalars, n_far, n_own, far, own, proj_a, proj_b):
    dim = n_far.shape[2]
    width = far[0].shape[0]
    return pl.pallas_call(
        qkv_kernel,
        in_specs=[SCALARS] + [PLAIN] * 10,
        out_shape=[jax.ShapeDtypeStruct((2 * width, dim), F32)] * 2
        + [jax.ShapeDtypeStruct((width, 128), F32)],
        compiler_params=params(),
        cost_estimate=spent(4.5),
        name="qkv_grad",
    )(scalars, n_far, n_own, *far, *own, proj_a, proj_b)


def wide_rows(lo_ref, hi_ref):
    return jnp.concatenate([lo_ref[0], hi_ref[0]], axis=1)


def column_sum(x):
    return jnp.sum(x, axis=0, keepdims=True)


def feed_kernel(first, *refs):
    if not first:
        refs = refs[:14] + refs[15:]
    (sc_ref, tok_ref, out_ref, o0, oc, ox, od, wp0, wpc, wpx, wpd) = refs[:11]
    vec, w1, w2 = refs[11:14]
    mid_ref, a_ref, kept_ref, sent_ref, g_ref, n_ref, du_ref, dm_ref, o_scr, w_scr = refs[14:]
    low = lambda r: r.astype(BF16)
    place = sc_ref[3]
    for hop, (part, weight) in enumerate(((o0, wp0), (oc, wpc), (ox, wpx), (od, wpd))):
        at = place ^ hop
        o_scr[at] = low(part[0])
        w_scr[at] = low(weight[...])
    size = o_scr.shape[0] * o_scr.shape[1]
    o_all = o_scr[...].reshape(size, o_scr.shape[2])
    a = dot_tn(o_all, w_scr[...].reshape(size, w_scr.shape[2])) + vec[6:7]
    a_ref[0] = a
    mid = tok_ref[0].astype(F32) + vec[4:5] * a
    mid_ref[0] = mid
    n2 = layer_norm(mid, vec[2:3], vec[3:4])[0].astype(BF16)
    n_ref[0] = n2
    u = dot(n2, w1[...]) + vec[7:8]
    cdf = 0.5 * (1.0 + lax.erf(u * np.float32(np.sqrt(0.5))))
    slope = cdf + u * (jnp.exp(-0.5 * u * u) * np.float32(1 / np.sqrt(2 * np.pi)))
    g_ref[0] = (u * cdf).astype(BF16)
    dm = (vec[5:6] * out_ref[0].astype(F32)).astype(BF16)
    dm_ref[0] = dm
    du = (slope * dot_nt(dm, w2[...])).astype(BF16)
    du_ref[0] = du
    dn = dot_nt(du, w1[...])
    part_halves(sc_ref[2], dn, kept_ref, sent_ref)


def feed(scalars, tok3, out3, o_parts, w_parts, vec, w1, w2, mid=None):
    dim = tok3.shape[2]
    hid = w1.shape[1]
    width = w_parts[0].shape[0]
    pair = jax.ShapeDtypeStruct((LONG, dim // 2), F32)
    row = jax.ShapeDtypeStruct((1, LONG, dim), F32)
    both = jax.ShapeDtypeStruct((2, LONG, dim), F32)
    held = () if mid is None else (mid,)
    low = lambda n: jax.ShapeDtypeStruct((1, LONG, n), BF16)
    specs = (
        [once(pack_spec, (LONG, dim))] * 2
        + [once(first_spec, (width, LONG))] * 4
        + [once(whole_spec, (width, dim))] * 4
        + [
            once(whole_spec, (8, dim)),
            once(whole_spec, (dim, hid)),
            once(whole_spec, (hid, dim)),
        ]
    )
    specs += [pl.BlockSpec(memory_space=pl.ANY)] * len(held)
    return pl.pallas_call(
        partial(feed_kernel, mid is None),
        out_shape=[both, row, pair, pair, low(hid), low(dim), low(hid), low(dim)],
        grid_spec=pltpu.PrefetchScalarGridSpec(
            num_scalar_prefetch=1,
            grid=(1,),
            in_specs=specs,
            out_specs=[once(pack_spec, (LONG, dim)), once(first_spec, (LONG, dim))]
            + [once(whole_spec, pair.shape)] * 2
            + [once(first_spec, (LONG, n)) for n in (hid, dim, hid, dim)],
            scratch_shapes=[
                pltpu.VMEM((4, width, LONG), BF16),
                pltpu.VMEM((4, width, dim), BF16),
            ],
        ),
        compiler_params=params(),
        input_output_aliases={14: 0} if held else {},
        cost_estimate=spent(10),
        name="feed",
    )(scalars, tok3, out3, *o_parts, *w_parts, vec, w1, w2, *held)


SCALARS = pl.BlockSpec(memory_space=pltpu.SMEM)
PLAIN = pl.BlockSpec(memory_space=pltpu.VMEM)


def out_kernel(sc_ref, up, g, w2, kept_ref, sent_ref, sum_ref):
    m = dot(g[0], w2[...])
    part_halves(sc_ref[2], m, kept_ref, sent_ref)
    e = up[0].astype(F32)
    sum_ref[0:1] = column_sum(e * m)
    sum_ref[1:2] = column_sum(e)


def feed_out(scalars, up3, g, w2):
    hid, dim = w2.shape
    return pl.pallas_call(
        out_kernel,
        out_shape=[jax.ShapeDtypeStruct(n, F32) for n in [(LONG, dim // 2)] * 2 + [(2, dim)]],
        grid_spec=pltpu.PrefetchScalarGridSpec(
            num_scalar_prefetch=1,
            grid=(1,),
            in_specs=[
                once(pack_spec, (LONG, dim)),
                once(first_spec, (LONG, hid)),
                once(whole_spec, (hid, dim)),
            ],
            out_specs=[once(whole_spec, (LONG, dim // 2))] * 2 + [once(whole_spec, (2, dim))],
        ),
        compiler_params=params(),
        cost_estimate=spent(3.5),
        name="feed_out",
    )(scalars, up3, g, w2)


def part_blocks(bit, blocks, refs):
    for i in range(len(blocks) // 2):
        refs[2 * i][...] = jnp.where(bit == 0, blocks[2 * i], blocks[2 * i + 1])
        refs[2 * i + 1][...] = jnp.where(bit == 0, blocks[2 * i + 1], blocks[2 * i])


def feed_grad_kernel(sc_ref, up, gf, nf, uf, mf, go, no, uo, mo, w2, *refs):
    db1_ref, db2_ref = refs[4:6]
    d1 = dot_tn(nf[0], uf[0]) + dot_tn(no[0], uo[0])
    rows = d1.shape[0] // 2
    part_blocks(sc_ref[4], (d1[:rows], d1[rows:]), refs[:2])
    d2 = dot_tn(gf[0], mf[0]) + dot_tn(go[0], mo[0])
    part_blocks(sc_ref[5], (d2[:rows], d2[rows:]), refs[2:4])
    db1_ref[...] = column_sum(uf[0].astype(F32)) + column_sum(uo[0].astype(F32))
    db2_ref[...] = column_sum(mf[0].astype(F32)) + column_sum(mo[0].astype(F32))
    out_kernel(sc_ref, up, go, w2, *refs[6:])


def feed_grad(scalars, up3, far, own, w2):
    hid, dim = w2.shape
    shapes = [(dim // 2, hid)] * 2 + [(hid // 2, dim)] * 2 + [(1, hid), (1, dim)]
    shapes += [(LONG, dim // 2)] * 2 + [(2, dim)]
    kept = [once(first_spec, (LONG, n)) for n in (hid, dim, hid, dim)]
    return pl.pallas_call(
        feed_grad_kernel,
        out_shape=[jax.ShapeDtypeStruct(n, F32) for n in shapes],
        grid_spec=pltpu.PrefetchScalarGridSpec(
            num_scalar_prefetch=1,
            grid=(1,),
            in_specs=[once(pack_spec, (LONG, dim))]
            + kept * 2
            + [once(whole_spec, (hid, dim))],
            out_specs=[once(whole_spec, n) for n in shapes],
        ),
        compiler_params=params(),
        cost_estimate=spent(9.5),
        name="feed_grad",
    )(scalars, up3, *far, *own, w2)


def norm_back(upstream, unit_rows, inverse, gain_row):
    scaled = upstream * gain_row
    centred = scaled - jnp.mean(scaled, axis=-1, keepdims=True)
    centred = centred - unit_rows * jnp.mean(scaled * unit_rows, axis=-1, keepdims=True)
    return inverse * centred, column_sum(upstream * unit_rows), column_sum(upstream)


def joined(sc_ref, mine, peer):
    core = sc_ref[2]
    lo = jnp.where(core == 0, mine[...], peer[...])
    hi = jnp.where(core == 0, peer[...], mine[...])
    return jnp.concatenate([lo, hi], axis=1)


def middle_kernel(
    sc_ref, out_ref, mid_ref, a_ref, mine, peer, vec, wp0, wpx, o0, ox,
    dmid_ref, do0_ref, dox_ref, dp0_ref, dpx_ref, sum_ref
):
    dn2 = joined(sc_ref, mine, peer)
    _, unit, inverse = layer_norm(mid_ref[0], vec[2:3], vec[3:4])
    back, d_gain, d_shift = norm_back(dn2, unit, inverse, vec[2:3])
    dmid = out_ref[0].astype(F32) + back
    dmid_ref[0] = dmid
    da = (vec[4:5] * dmid).astype(BF16)
    do0_ref[0] = dot_nt(wp0[...], da).astype(BF16).astype(F32)
    dox_ref[0] = dot_nt(wpx[...].astype(BF16), da).astype(BF16).astype(F32)
    dp0_ref[...] = dot(o0[0].astype(BF16), da)
    dpx_ref[...] = dot(ox[0].astype(BF16), da)
    sum_ref[0:1] = d_gain
    sum_ref[1:2] = d_shift
    sum_ref[2:3] = column_sum(dmid * a_ref[0])
    sum_ref[3:4] = column_sum(da.astype(F32))


def middle_back(scalars, out3, mid, a, mine, peer, vec, w_parts, o_parts):
    dim = mid.shape[2]
    width = w_parts[0].shape[0]
    row = jax.ShapeDtypeStruct((1, LONG, dim), F32)
    low = jax.ShapeDtypeStruct((1, width, LONG), F32)
    mat = jax.ShapeDtypeStruct((width, dim), F32)
    return pl.pallas_call(
        middle_kernel,
        out_shape=[row, low, low, mat, mat, jax.ShapeDtypeStruct((4, dim), F32)],
        grid_spec=pltpu.PrefetchScalarGridSpec(
            num_scalar_prefetch=1,
            grid=(1,),
            in_specs=[
                once(pack_spec, (LONG, dim)),
                once(pack_spec, (LONG, dim)),
                once(first_spec, (LONG, dim)),
                once(whole_spec, (LONG, dim // 2)),
                once(whole_spec, (LONG, dim // 2)),
                once(whole_spec, (8, dim)),
                once(whole_spec, (width, dim)),
                once(whole_spec, (width, dim)),
                once(first_spec, (width, LONG)),
                once(first_spec, (width, LONG)),
            ],
            out_specs=[
                once(first_spec, (LONG, dim)),
                once(first_spec, (width, LONG)),
                once(first_spec, (width, LONG)),
                once(whole_spec, (width, dim)),
                once(whole_spec, (width, dim)),
                once(whole_spec, (4, dim)),
            ],
        ),
        compiler_params=params(),
        cost_estimate=spent(7.7),
        name="middle_back",
    )(scalars, out3, mid, a, mine, peer, vec, *w_parts[::2], *o_parts[::2])


def final_kernel(sc_ref, tok_ref, dmid_ref, mine, peer, vec, two, scale, out_ref, sent_ref, sum_ref):
    dn1 = joined(sc_ref, mine, peer)
    _, unit, inverse = layer_norm(tok_ref[0].astype(F32), vec[0:1], vec[1:2])
    back, d_gain, d_shift = norm_back(dn1, unit, inverse, vec[0:1])
    result = dmid_ref[0] + back
    out_ref[0] = result
    half = result.shape[1] // 2
    rows = jnp.concatenate([two[...], d_gain, d_shift, scale[...]], axis=0)
    sum_ref[...] = rows
    sent_ref[0:LONG] = jnp.where(sc_ref[2] == 0, result[:, :half], result[:, half:])
    sent_ref[LONG : LONG + 8] = rows[:, :half]
    sent_ref[LONG + 8 : LONG + 16] = rows[:, half:]


def final_back(scalars, tok3, dmid, mine, peer, vec, two, scale):
    dim = tok3.shape[2]
    return pl.pallas_call(
        final_kernel,
        out_shape=[
            jax.ShapeDtypeStruct((1, LONG, dim), F32),
            jax.ShapeDtypeStruct((LONG + 16, dim // 2), F32),
            jax.ShapeDtypeStruct((8, dim), F32),
        ],
        grid_spec=pltpu.PrefetchScalarGridSpec(
            num_scalar_prefetch=1,
            grid=(1,),
            in_specs=[
                once(pack_spec, (LONG, dim)),
                once(first_spec, (LONG, dim)),
                once(whole_spec, (LONG, dim // 2)),
                once(whole_spec, (LONG, dim // 2)),
                once(whole_spec, (8, dim)),
                once(whole_spec, (4, dim)),
                once(whole_spec, (2, dim)),
            ],
            out_specs=[
                once(first_spec, (LONG, dim)),
                once(whole_spec, (LONG + 16, dim // 2)),
                once(whole_spec, (8, dim)),
            ],
        ),
        compiler_params=params(),
        cost_estimate=spent(5.6),
        name="final_back",
    )(scalars, tok3, dmid, mine, peer, vec, two, scale)


def last_kernel(sc_ref, kept, got, flat_ref, b2, _, qkv_ref, proj_ref, *refs):
    gains, shifts, scales, singles, rest = refs
    rows = kept.shape[0]
    width = rows // 2
    swap = sc_ref[4] == 0
    for i, lo in enumerate((0, width)):
        a = kept[lo : lo + width]
        b = got[lo : lo + width]
        qkv_ref[i] = jnp.where(swap, a, b)
        other = jnp.where(swap, b, a)
        if i == 0:
            qkv_ref[2] = other
        else:
            proj_ref[...] = other
    flat = flat_ref[...]
    gains[0:1] = flat[4:5]
    gains[1:2] = flat[0:1]
    shifts[0:1] = flat[5:6]
    shifts[1:2] = flat[1:2]
    scales[0:1] = flat[2:3]
    scales[1:2] = flat[6:7] + b2[...].astype(F32) * flat[10:11]
    singles[0:1] = flat[3:4]
    singles[1:3] = flat[8:10]
    rest[...] = flat[11:]


def last_parts(scalars, kept, got, flat, b2, after):
    rows, dim = kept.shape
    width = rows // 2
    shapes = [(3, width, dim), (width, dim)] + [(2, dim)] * 3 + [(3, dim), (13, dim)]
    return pl.pallas_call(
        last_kernel,
        in_specs=[SCALARS] + [PLAIN] * 4 + [pl.BlockSpec(memory_space=pl.ANY)],
        out_shape=[jax.ShapeDtypeStruct(n, F32) for n in shapes],
        compiler_params=params(),
        cost_estimate=spent(3),
        name="last_parts",
    )(scalars, kept, got, flat, b2, after)


CORE = [(i, i ^ 1) for i in range(4)]
ACROSS = [(i, i ^ 2) for i in range(4)]


def to_core(x):
    return lax.ppermute(x, "narrow", CORE)


def to_chip(x):
    return lax.ppermute(x, "narrow", ACROSS)


def pick(pair, index):
    return lax.dynamic_index_in_dim(pair, index, 0, keepdims=False)


def small_sum(x, size):
    step = 1
    while step < size:
        x = x + lax.ppermute(x, "wide", [(i, i ^ step) for i in range(size)])
        step *= 2
    return x


def tie(*values):
    return lax.optimization_barrier(values)


def in_order(bit, first, second):
    return jnp.where(bit == 0, first, second), jnp.where(bit == 0, second, first)


WIDE_PLACES = 8
DUE = {
    "one": (1, 2, 3, 5, 8),
    "two": (1, 3, 5, 9, 13),
    "last": (4, 6, 9, 11, 14),
    "flat": (9, 11, 14),
}


class Wave:
    def __init__(self, place):
        self.place = place
        self.live = {}
        self.done = {}

    def bit(self, step):
        return (self.place // step) % 2

    def send(self, value, step):
        return lax.ppermute(value, "wide", [(i, i ^ step) for i in range(WIDE_PLACES)])

    def add(self, name, kept, sent, steps, due, whole=False):
        got = self.send(sent, steps[0])
        self.live[name] = dict(steps=steps, stage=0, kept=kept, got=got, due=list(due), whole=whole)

    def advance(self, c, got):
        stage, kept, (first, second, third) = c["stage"], c["kept"], c["steps"]
        if c["whole"]:
            total = kept + got
            return (total, total, (first, second, third)[stage + 1]) if stage < 2 else (total, None, None)
        if stage == 0:
            rows = kept.shape[0] // 2
            split = lambda v: v.reshape((2, rows) + v.shape[1:])
            side = self.bit(second)
            kept, got = split(kept), split(got)
            send = pick(kept, 1 - side) + pick(got, 1 - side)
            return pick(kept, side) + pick(got, side), send, second
        if stage < 3:
            total = kept + got
        elif stage == 3:
            total = jnp.concatenate(in_order(self.bit(second), kept, got))
        else:
            return (kept, got), None, None
        return total, total, (third, second, first)[stage - 1]

    def event(self, now, then):
        ripe = [n for n, c in self.live.items() if c["due"][0] <= now]
        if not ripe:
            return then
        then, *values = tie(then, *[self.live[n]["got"] for n in ripe])
        moves = {n: self.advance(self.live[n], got) for n, got in zip(ripe, values)}
        for n in ripe:
            if moves[n][1] is None:
                self.done[n] = moves[n][0]
                del self.live[n], moves[n]
        if not moves:
            return then
        held = tie(then, *[m[1] for m in moves.values()])
        for (n, (kept, _, step)), value in zip(moves.items(), held[1:]):
            c = self.live[n]
            c["kept"] = kept
            c["got"] = self.send(value, step)
            c["stage"] += 1
            c["due"].pop(0)
        return held[0]


def on_device(
    tokens, w_qkv, qv_bias, w_proj, proj_bias, w_fc1, fc1_bias, w_fc2, fc2_bias, norm_gains,
    norm_shifts, layer_scales, rel_table, image_ids, pad_mask, grid_rows, grid_cols, d_out, wide
):
    rows, dim = tokens.shape
    width = w_qkv.shape[2]
    place = lax.axis_index("narrow")
    chip, core = place // 2, place % 2
    spot = lax.axis_index("wide")
    tok3 = tokens.reshape(2, LONG, dim)
    out3 = d_out.reshape(2, LONG, dim)
    w_turned = w_qkv.transpose(0, 2, 1)
    kind_a = image_ids[LONG - 1] % 2
    kind_b = image_ids[2 * LONG - 1] % 2
    common = (core, place, spot % 2, (spot // 2) % 2)
    sc_far = jnp.stack([1 - chip, jnp.where(chip == 0, kind_b, kind_a), *common])
    sc_own = jnp.stack([chip, jnp.where(chip == 0, kind_a, kind_b), *common])
    pairs = zip(norm_gains.astype(F32), norm_shifts.astype(F32))
    vec = jnp.stack(
        [v for pair in pairs for v in pair]
        + list(layer_scales.astype(F32))
        + [proj_bias.astype(F32), fc1_bias.astype(F32)]
    )

    wp_near = w_proj.astype(F32)
    wp_far = to_chip(wp_near)
    bias = make_bias(rel_table)
    first = lambda sc: attend(sc, tok3, w_turned, qv_bias, vec, bias)
    o_far, *saved_far, n_far = first(sc_far)
    wp_far, o_sent = tie(wp_far, o_far)
    x_own = to_chip(o_sent)
    w_parts = (w_proj, to_core(wp_near), wp_far, to_core(wp_far))
    o_own, *saved_own, n_own = first(sc_own)
    x_own, o_sent = tie(x_own, o_own)
    x_far = to_chip(o_sent)
    far_parts = (o_far, to_core(o_far), x_far, to_core(x_far))
    own_parts = (o_own, to_core(o_own), x_own, to_core(x_own))

    shared = (w_parts, vec, w_fc1, w_fc2)
    mid, _, dn_kept, dn_send, *kept_far = feed(sc_far, tok3, out3, far_parts, *shared)
    peer = to_core(dn_send)
    sc, _ = tie(sc_far, dn_send)
    m_far_kept, m_far_send, scale_far = feed_out(sc, out3, kept_far[0], w_fc2)
    peer, scale_far = tie(peer, scale_far)
    half, sc = tie(dn_kept + peer, sc_own)
    dn_got = to_chip(half)
    mid, a_own, dn_kept, dn_send, *kept_own = feed(sc, tok3, out3, own_parts, *shared, mid)
    peer = to_core(dn_send)
    *blocks, d_fc1_bias, d_fc2_bias, m_own_kept, m_own_send, scale_own = feed_grad(
        sc_own, out3, kept_far, kept_own, w_fc2
    )

    wave = Wave(spot)
    custom = wide == WIDE_PLACES
    if custom:
        wave.add("one", blocks[0], blocks[1], (1, 2, 4), DUE["one"])
        wave.add("two", blocks[2], blocks[3], (2, 1, 4), DUE["two"])
    dn_got, scale_own = tie(dn_got, scale_own)
    part, peer = tie(dn_kept + dn_got, peer)
    mine = part + peer
    theirs = to_core(mine)
    dmid, do_own, do_send, dp_own, dp_send, sums_two = middle_back(
        sc_own, out3, mid, a_own, mine, theirs, vec, w_parts, own_parts
    )
    do_far = to_chip(do_send)
    m_far_peer, m_own_peer, _ = tie(to_core(m_far_send), to_core(m_own_send), dmid)
    m_half_far = m_far_kept + m_far_peer
    m_half_own = m_own_kept + m_own_peer
    scale = scale_far + scale_own
    up_sum = scale[1:2]
    scale, _ = tie(scale, dmid)
    scale = scale + to_core(scale)
    do_far, m_half_far, m_half_own, scale = tie(do_far, m_half_far, m_half_own, scale)
    do_far, sc = tie(do_far, sc_far)
    sc = wave.event(1, sc)
    dp_send, sc = tie(dp_send, sc)
    dp_got = to_chip(dp_send)

    dn_kept, dn_send, *far, dl, ds, dt = attend_back(sc, w_turned, bias, saved_far, do_far, None)
    dn_send, dp_got = tie(dn_send, dp_got)
    dn_send = wave.event(2, dn_send)
    peer = to_core(dn_send)
    half, sc, dp_got = tie(dn_kept + peer, sc_own, dp_got)
    dn_got = to_chip(half)
    dn_kept, dn_send, *own, dl, ds, dt = attend_back(
        sc, w_turned, bias, saved_own, do_own, (dl, ds, dt)
    )
    *pieces, d_qv_bias = qkv_grad(sc_own, n_far, n_own, far, own, dp_own, dp_got)
    dn_got, d_qv_bias, dn_send = tie(dn_got, d_qv_bias, dn_send)
    dn_send = wave.event(3, dn_send)
    peer = to_core(dn_send)
    if custom:
        wave.add("last", pieces[0], pieces[1], (1, 2, 4), DUE["last"])
    part, peer = tie(dn_kept + dn_got, peer)
    mine = part + peer
    theirs = to_core(mine)
    tok_own, tok_send, own_rows = final_back(
        sc_own, tok3, dmid, mine, theirs, vec, sums_two, scale
    )
    tok_got = to_chip(tok_send)
    dl, ds, dt, own_rows = tie(dl, ds, dt, own_rows)
    table_back = strips_back(dl, ds, dt)
    heads, count = table_back.shape
    row_bias = jnp.pad(d_qv_bias[:, :2].T.reshape(1, -1), ((0, 0), (0, dim - 2 * width)))
    rest = jnp.pad(table_back, ((0, 0), (0, 3 * dim - count))).reshape(3 * heads, dim)
    rest = [d_fc2_bias, d_fc1_bias, up_sum, rest, row_bias, jnp.zeros((12 - 3 * heads, dim), F32)]
    rest = jnp.concatenate(rest)
    rest, own_rows = tie(rest, own_rows)
    mark = wave.event(4, own_rows)
    mark = wave.event(5, mark)
    tok_got, mark = tie(tok_got, mark)
    tok_peer = to_core(tok_got)
    m_send, mark = tie(m_half_far, mark)
    m_all_own = to_chip(m_send)
    mark = wave.event(6, mark)
    own_rows = mark + jnp.concatenate([tok_got[LONG : LONG + 8], tok_got[LONG + 8 :]], axis=1)
    flat = jnp.concatenate([own_rows, rest])
    mark = flat
    if custom:
        wave.add("flat", mark, mark, (4, 2, 1), DUE["flat"], True)
    tok_peer, mark = tie(tok_peer, mark)
    tok_far = jnp.concatenate(in_order(core, tok_got[:LONG], tok_peer[:LONG]), axis=1)[None]
    d_tokens = jnp.concatenate(in_order(chip, tok_own, tok_far)).reshape(rows, dim)
    d_tokens, mark = tie(d_tokens, mark)
    m_all_own, mark = tie(m_all_own, mark)
    m_all_own = m_half_own + m_all_own
    m_own_peer = to_core(m_all_own)
    m_send, m_all_own = tie(m_half_own, m_all_own)
    m_all_far = to_chip(m_send)
    mark = wave.event(8, mark)
    if custom:
        d_fc1 = jnp.concatenate(in_order(spot % 2, *wave.done["one"]))
        d_fc1, mark = tie(d_fc1, mark)
    mark = wave.event(9, mark)
    mark = wave.event(11, mark)
    m_own_peer, m_all_far, mark = tie(m_own_peer, m_all_far, mark)
    m_own = jnp.concatenate(in_order(core, m_all_own, m_own_peer), axis=1)[None]
    m_all_far = m_half_far + m_all_far
    m_far_peer = to_core(m_all_far)
    m_far = jnp.concatenate(in_order(core, m_all_far, m_far_peer), axis=1)[None]
    m_full = jnp.concatenate(in_order(chip, m_own, m_far)) + fc2_bias.astype(F32)
    block_out = (mid + layer_scales[1].astype(F32) * m_full).astype(BF16).reshape(rows, dim)
    block_out, mark = tie(block_out, mark)
    mark = wave.event(13, mark)
    if custom:
        d_fc2 = jnp.concatenate(in_order((spot // 2) % 2, *wave.done["two"]))
        d_fc2, mark = tie(d_fc2, mark)
    mark = wave.event(14, mark)
    if custom:
        got = wave.done
        kept, last = got["last"]
        flat = got["flat"]
    else:
        low, high = spot % 2, (spot // 2) % 2
        d_fc1 = jnp.concatenate(in_order(low, blocks[0], blocks[1]))
        d_fc2 = jnp.concatenate(in_order(high, blocks[2], blocks[3]))
        pieces = in_order(low, *pieces)
        pieces, d_fc1, d_fc2 = lax.psum((pieces, d_fc1, d_fc2), "wide")
        kept, last = in_order(low, *pieces)
        flat = small_sum(flat, wide)
    d_qkv, d_proj, d_norm_gains, d_norm_shifts, d_layer_scales, singles, rest = last_parts(
        sc_own, kept, last, flat, fc2_bias[None], mark
    )
    d_proj_bias, d_fc2_bias, d_fc1_bias = singles
    d_qkv = d_qkv.transpose(0, 2, 1)
    d_table = rest[: 3 * heads].reshape(heads, 3 * dim)[:, :count]
    d_qv_bias = rest[3 * heads, : 2 * width].reshape(2, width)
    return (
        block_out,
        d_tokens,
        d_qkv,
        d_qv_bias,
        d_proj,
        d_proj_bias,
        d_fc1,
        d_fc1_bias,
        d_fc2,
        d_fc2_bias,
        d_norm_gains,
        d_norm_shifts,
        d_layer_scales,
        d_table,
    )


def solution(mesh):
    in_specs = (
        P("wide", None),
        P(None, None, "narrow"),
        P(None, "narrow"),
        P("narrow", None),
        P(),
        P(None, "narrow"),
        P("narrow"),
        P("narrow", None),
        P(),
        P(),
        P(),
        P(),
        P("narrow", None),
        P("wide"),
        P("wide"),
        P("wide"),
        P("wide"),
        P("wide", None),
    )
    out_specs = (
        P("wide", None),
        P("wide", None),
        P(None, None, "narrow"),
        P(None, "narrow"),
        P("narrow", None),
        P(),
        P(None, "narrow"),
        P("narrow"),
        P("narrow", None),
        P(),
        P(),
        P(),
        P(),
        P("narrow", None),
    )
    return jax.shard_map(
        partial(on_device, wide=mesh.shape["wide"]),
        mesh=mesh,
        in_specs=in_specs,
        out_specs=out_specs,
        check_vma=False,
    )
```

```python
from functools import partial

import jax
import jax.numpy as jnp
import numpy as np
from jax import lax
from jax.experimental import pallas as pl
from jax.experimental.pallas import tpu as pltpu
from jax.sharding import PartitionSpec as P

HD = 64
GRID = 24
SMALL = 14
SHORT = 208
LONG = 584
EPSILON = 1e-06
SIDE = 2 * GRID - 1
WIDE_L = 1280
WIDE_S = 640
NEG = -1e30
F32 = jnp.float32
BF16 = jnp.bfloat16
VMEM_LIMIT = 56 << 20
COST_SCALE = 1.2e8


def params(**kw):
    return pltpu.CompilerParams(vmem_limit_bytes=VMEM_LIMIT, **kw)


def spent(microseconds):
    work = int(microseconds * COST_SCALE)
    return pl.CostEstimate(flops=work, transcendentals=0, bytes_accessed=1024)


def dot(a, b):
    return jnp.dot(a, b, preferred_element_type=F32)


def dot_nt(a, b):
    return lax.dot_general(a, b, (((1,), (1,)), ((), ())), preferred_element_type=F32)


def dot_tn(a, b):
    return lax.dot_general(a, b, (((0,), (0,)), ((), ())), preferred_element_type=F32)


def large_pick():
    pick = np.zeros((2, SIDE, GRID, GRID), np.float32)
    for s in range(GRID):
        for c in range(GRID):
            if s == 0:
                pick[1, c, s, c] = 1
            else:
                pick[0, c + GRID - s, s, c] = 1
    return pick.reshape(2 * SIDE, GRID * GRID)


def small_pick():
    pick = np.zeros((SIDE, 16, SMALL), np.float32)
    for s in range(SMALL):
        for c in range(SMALL):
            pick[c - s + GRID - 1, s, c] = 1
    return pick.reshape(SIDE, 16 * SMALL)


def strips(rel_table):
    heads = rel_table.shape[0]
    grid_part = rel_table[:, : SIDE * SIDE].reshape(heads, SIDE, SIDE)
    front = jnp.pad(grid_part, ((0, 0), (1, 0), (0, 0)))
    back = jnp.pad(grid_part, ((0, 0), (0, 1), (0, 0)))
    both = jnp.concatenate([front, back], axis=2)
    large = jnp.einsum(
        "huk,kp->hup", both, jnp.asarray(large_pick(), BF16), preferred_element_type=F32
    ).reshape(heads, SIDE + 1, GRID, GRID)
    large = large.transpose(0, 2, 1, 3).reshape(heads, GRID, (SIDE + 1) * GRID)
    large = jnp.pad(large, ((0, 0), (0, 0), (1, WIDE_L - 1 - (SIDE + 1) * GRID)))
    rows = 2 * SMALL - 1
    part = grid_part[:, GRID - SMALL : GRID - SMALL + rows]
    small = jnp.einsum(
        "huk,kp->hup", part, jnp.asarray(small_pick(), BF16), preferred_element_type=F32
    ).reshape(heads, rows, 16, SMALL)
    small = small.transpose(0, 2, 1, 3).reshape(heads, 16, rows * SMALL)
    small = jnp.pad(small, ((0, 0), (0, 0), (1, WIDE_S - 1 - rows * SMALL)))
    tails = rel_table[:, SIDE * SIDE :].astype(F32)
    return large, small, tails


def strips_back(d_large, d_small, d_tails):
    heads = d_large.shape[0]
    rows = 2 * SMALL - 1
    hi = lax.Precision.HIGHEST
    large = d_large[:, :, 1 : 1 + (SIDE + 1) * GRID].reshape(heads, GRID, SIDE + 1, GRID)
    both = jnp.einsum(
        "hsuc,ksc->huk",
        large,
        jnp.asarray(large_pick().reshape(2 * SIDE, GRID, GRID)),
        precision=hi,
    )
    grid_grad = both[:, 1:, :SIDE] + both[:, :SIDE, SIDE:]
    small = d_small[:, :, 1 : 1 + rows * SMALL].reshape(heads, 16, rows, SMALL)
    part = jnp.einsum(
        "hsuc,ksc->huk", small, jnp.asarray(small_pick().reshape(SIDE, 16, SMALL)), precision=hi
    )
    low = GRID - SMALL
    grid_grad = grid_grad + jnp.pad(part, ((0, 0), (low, SIDE - low - rows), (0, 0)))
    return jnp.concatenate(
        [grid_grad.reshape(heads, SIDE * SIDE), d_tails[:, 0, :3]], axis=1
    )


def tail_fix(block, t0, t1, t2, last, real):
    shape = block.shape
    row = lax.broadcasted_iota(jnp.int32, shape, 0)
    lane = lax.broadcasted_iota(jnp.int32, shape, 1)
    block = jnp.where(lane > last, block[:, 1:2], block)
    block = jnp.where(lane == 0, t0, block)
    block = jnp.where(row == 0, jnp.where(lane == 0, t2, t1), block)
    return jnp.where(row >= real, NEG, block)


def bias_kernel(tail_ref, large_ref, small_ref, out_ref, scr):
    for h in range(large_ref.shape[0]):
        t0, t1, t2 = tail_ref[h, 0], tail_ref[h, 1], tail_ref[h, 2]
        for r in range(GRID + 1):
            size = GRID if r < GRID else LONG - GRID * GRID
            off = (GRID - r) * GRID
            scr[r * GRID : r * GRID + size, 0:LONG] = large_ref[h, 0:size, off : off + LONG]
        last = GRID * GRID
        out_ref[0, h] = tail_fix(scr[:, 0:LONG], t0, t1, t2, last, last + 1).astype(BF16)
        last = SMALL * SMALL
        for r in range(SMALL):
            off = (SMALL - 1 - r) * SMALL
            wide = LONG - SHORT
            scr[1 + r * SMALL : 1 + (r + 1) * SMALL, 0:wide] = small_ref[
                h, 0:SMALL, off : off + wide
            ]
        block = tail_fix(scr[0:SHORT, 0 : LONG - SHORT], t0, t1, t2, last, last + 1)
        scr[...] = jnp.full(scr.shape, NEG, F32)
        scr[0:SHORT, 0:SHORT] = block[:, 0:SHORT]
        scr[SHORT : 2 * SHORT, SHORT:LONG] = block
        out_ref[1, h] = scr[:, 0:LONG].astype(BF16)


def make_bias(rel_table):
    heads = rel_table.shape[0]
    large, small, tails = strips(rel_table)
    return pl.pallas_call(
        bias_kernel,
        out_shape=jax.ShapeDtypeStruct((2, heads, LONG, LONG), BF16),
        in_specs=[
            pl.BlockSpec(memory_space=pltpu.SMEM),
            pl.BlockSpec(memory_space=pltpu.VMEM),
            pl.BlockSpec(memory_space=pltpu.VMEM),
        ],
        out_specs=pl.BlockSpec(memory_space=pltpu.VMEM),
        scratch_shapes=[pltpu.VMEM((LONG, 640), F32)],
        compiler_params=params(),
        cost_estimate=spent(6),
        name="bias",
    )(tails, large, small)


def layer_norm(values, gain_row, shift_row):
    row_mean = jnp.mean(values, axis=-1, keepdims=True)
    centred = values - row_mean
    inverse = lax.rsqrt(jnp.mean(centred * centred, axis=-1, keepdims=True) + EPSILON)
    unit_rows = centred * inverse
    return unit_rows * gain_row + shift_row, unit_rows, inverse


def part_halves(core, value, kept_ref, sent_ref):
    half = value.shape[1] // 2
    lo, hi = value[:, :half], value[:, half:]
    kept_ref[...] = jnp.where(core == 0, lo, hi)
    sent_ref[...] = jnp.where(core == 0, hi, lo)


def head_lanes(shape, h):
    lane = lax.broadcasted_iota(jnp.int32, shape, 1)
    return (lane >= h * HD) & (lane < (h + 1) * HD)


def turned(block):
    return block.astype(F32).T.astype(BF16)


def forward_kernel(
    sc_ref, tok_ref, w_ref, qv_ref, vec, bias_ref, o_ref, q_ref, k_ref, v_ref, lse_ref, n_ref
):
    x = tok_ref[0].astype(F32)
    n1 = layer_norm(x, vec[0:1], vec[1:2])[0].astype(BF16)
    qv = qv_ref[...].astype(F32)
    q = ((dot_nt(n1, w_ref[0]) + qv[0:1]) * HD**-0.5).astype(BF16)
    k = dot_nt(n1, w_ref[1]).astype(BF16)
    v = (dot_nt(n1, w_ref[2]) + qv[1:2]).astype(BF16)
    q_ref[0] = q
    k_ref[0] = k
    v_ref[0] = v
    n_ref[0] = n1
    v_t = turned(v)
    outs = []
    for h in range(k.shape[1] // HD):
        k_h = jnp.where(head_lanes(k.shape, h), k, jnp.zeros_like(k))
        s = dot_nt(k_h, q) + bias_ref[0, h].astype(F32)
        top = jnp.max(s, axis=0, keepdims=True)
        e = jnp.exp(s - top)
        total = jnp.sum(e, axis=0, keepdims=True)
        p = (e * (1.0 / total)).astype(BF16)
        outs.append(dot(v_t[h * HD : (h + 1) * HD], p))
        lse_ref[0, h : h + 1, :] = top + jnp.log(total)
    o_ref[0] = jnp.concatenate(outs, axis=0).astype(BF16).astype(F32)


def once(spec_of, shape):
    spec = spec_of(shape)
    return pl.BlockSpec(spec.block_shape, spec.index_map, pipeline_mode=pl.Buffered(1))


def pack_spec(shape):
    return pl.BlockSpec((1,) + shape, lambda i, sc: (sc[0],) + (0,) * len(shape))


def first_spec(shape):
    return pl.BlockSpec((1,) + shape, lambda i, sc: (0,) * (1 + len(shape)))


def whole_spec(shape):
    return pl.BlockSpec(shape, lambda i, sc: (0,) * len(shape))


def kind_spec(shape):
    return pl.BlockSpec((1,) + shape, lambda i, sc: (sc[1],) + (0,) * len(shape))


def attend(scalars, tok3, w_qkv, qv_bias, vec, bias):
    width = w_qkv.shape[1]
    heads = width // HD
    dim = tok3.shape[2]
    low = jax.ShapeDtypeStruct((1, LONG, width), BF16)
    return pl.pallas_call(
        forward_kernel,
        out_shape=[
            jax.ShapeDtypeStruct((1, width, LONG), F32),
            low,
            low,
            low,
            jax.ShapeDtypeStruct((1, heads, LONG), F32),
            jax.ShapeDtypeStruct((1, LONG, dim), BF16),
        ],
        grid_spec=pltpu.PrefetchScalarGridSpec(
            num_scalar_prefetch=1,
            grid=(1,),
            in_specs=[
                pack_spec((LONG, dim)),
                whole_spec((3, width, dim)),
                whole_spec((2, width)),
                whole_spec((8, dim)),
                kind_spec((heads, LONG, LONG)),
            ],
            out_specs=[first_spec((width, LONG))]
            + [first_spec((LONG, width))] * 3
            + [first_spec((heads, LONG)), first_spec((LONG, dim))],
        ),
        compiler_params=params(),
        cost_estimate=spent(7.4),
        name="attend",
    )(scalars, tok3, w_qkv, qv_bias, vec, bias)


def fold_large(ds, h, dl_ref, dt_ref):
    last = GRID * GRID
    full = ds[:, 0:LONG]
    lane = lax.broadcasted_iota(jnp.int32, full.shape, 1)
    row = lax.broadcasted_iota(jnp.int32, full.shape, 0)
    pad = jnp.sum(jnp.where(lane > last, full, 0.0), axis=1, keepdims=True)
    body = row > 0
    t0 = jnp.sum(jnp.where((lane == 0) & body, full, 0.0))
    t1 = jnp.sum(jnp.where((lane > 0) & (row == 0), full, 0.0))
    t2 = jnp.sum(jnp.where((lane == 0) & (row == 0), full, 0.0))
    full = jnp.where((lane == 0) | (lane > last), 0.0, full)
    full = jnp.where(lane == 1, full + pad, full)
    ds[:, 0:LONG] = jnp.where(body, full, 0.0)
    for r in range(GRID + 1):
        size = GRID if r < GRID else LONG - GRID * GRID
        off = (GRID - r) * GRID
        dl_ref[h, 0:size, off : off + LONG] += ds[r * GRID : r * GRID + size, 0:LONG]
    tail_add(dt_ref, h, t0, t1, t2)


def tail_add(dt_ref, h, t0, t1, t2):
    lane = lax.broadcasted_iota(jnp.int32, (8, 128), 1)
    row = lax.broadcasted_iota(jnp.int32, (8, 128), 0)
    add = jnp.where(lane == 0, t0, jnp.where(lane == 1, t1, jnp.where(lane == 2, t2, 0.0)))
    dt_ref[h] += jnp.where(row == 0, add, 0.0)


def fold_small(ds, h, ds_ref, dt_ref):
    last = SMALL * SMALL
    for base, wide in ((0, SHORT), (SHORT, LONG - SHORT)):
        full = ds[base : base + SHORT, 0:LONG]
        if base:
            full = full[:, base : base + wide]
        else:
            full = full[:, 0:wide]
        lane = lax.broadcasted_iota(jnp.int32, full.shape, 1)
        row = lax.broadcasted_iota(jnp.int32, full.shape, 0)
        pad = jnp.sum(jnp.where(lane > last, full, 0.0), axis=1, keepdims=True)
        body = row > 0
        t0 = jnp.sum(jnp.where((lane == 0) & body, full, 0.0))
        t1 = jnp.sum(jnp.where((lane > 0) & (row == 0), full, 0.0))
        t2 = jnp.sum(jnp.where((lane == 0) & (row == 0), full, 0.0))
        full = jnp.where((lane == 0) | (lane > last), 0.0, full)
        full = jnp.where(lane == 1, full + pad, full)
        ds[base : base + SHORT, 0:wide] = full
        for r in range(SMALL):
            off = (SMALL - 1 - r) * SMALL
            lo = base + 1 + r * SMALL
            ds_ref[h, 0:SMALL, off : off + wide] += ds[lo : lo + SMALL, 0:wide]
        tail_add(dt_ref, h, t0, t1, t2)


def backward_kernel(first, *refs):
    sc_ref, w_ref, bias_ref, q_ref, k_ref, v_ref, do_ref, lse_ref = refs[:8]
    refs = refs[8:]
    if not first:
        al_ref, as_ref, at_ref = refs[:3]
        refs = refs[3:]
    kept_ref, sent_ref, dq_ref, dk_ref, dv_ref, dl_ref, ds_ref, dt_ref, scr = refs
    if first:
        dl_ref[...] = jnp.zeros_like(dl_ref)
        ds_ref[...] = jnp.zeros_like(ds_ref)
        dt_ref[...] = jnp.zeros_like(dt_ref)
    else:
        dl_ref[...] = al_ref[...]
        ds_ref[...] = as_ref[...]
        dt_ref[...] = at_ref[...]
    q, k, v = q_ref[0], k_ref[0], v_ref[0]
    do_t = do_ref[0].astype(BF16)
    do = do_ref[0].T.astype(BF16)
    k_t = turned(k)
    d_qt = []
    d_k = jnp.zeros(k.shape, F32)
    d_v = jnp.zeros(k.shape, F32)
    for h in range(k.shape[1] // HD):
        own = head_lanes(k.shape, h)
        s = dot_nt(jnp.where(own, k, jnp.zeros_like(k)), q) + bias_ref[0, h].astype(F32)
        p = jnp.exp(s - lse_ref[0, h : h + 1, :])
        dp = dot(jnp.where(own, v, jnp.zeros_like(v)), do_t)
        inner = jnp.sum(p * dp, axis=0, keepdims=True)
        ds = (p * (dp - inner)).astype(BF16)
        d_v = jnp.where(own, dot(p.astype(BF16), do), d_v)
        d_k = jnp.where(own, dot(ds, q), d_k)
        d_qt.append(dot(k_t[h * HD : (h + 1) * HD], ds))
        scr[:, 0:LONG] = ds.astype(F32)

        @pl.when(sc_ref[1] == 0)
        def _():
            fold_large(scr, h, dl_ref, dt_ref)

        @pl.when(sc_ref[1] == 1)
        def _():
            fold_small(scr, h, ds_ref, dt_ref)

    d_qt = jnp.concatenate(d_qt, axis=0).astype(BF16) * jnp.asarray(HD**-0.5, BF16)
    d_q = d_qt.astype(F32).T.astype(BF16)
    d_k = d_k.astype(BF16)
    d_v = d_v.astype(BF16)
    dn = dot(d_q, w_ref[0]) + dot(d_k, w_ref[1]) + dot(d_v, w_ref[2])
    part_halves(sc_ref[2], dn, kept_ref, sent_ref)
    dq_ref[...] = d_qt
    dk_ref[...] = turned(d_k)
    dv_ref[...] = turned(d_v)


def attend_back(scalars, w_qkv, bias, saved, do, sums):
    width, dim = w_qkv.shape[1:]
    heads = width // HD
    q, k, v, lse = saved
    first = sums is None
    pair = (LONG, dim // 2)
    sum_shapes = [(heads, GRID, WIDE_L), (heads, 16, WIDE_S), (heads, 8, 128)]
    specs = [
        once(whole_spec, (3, width, dim)),
        once(kind_spec, (heads, LONG, LONG)),
        once(first_spec, (LONG, width)),
        once(first_spec, (LONG, width)),
        once(first_spec, (LONG, width)),
        once(first_spec, (width, LONG)),
        once(first_spec, (heads, LONG)),
    ]
    if not first:
        specs += [once(whole_spec, s) for s in sum_shapes]
    return pl.pallas_call(
        partial(backward_kernel, first),
        out_shape=[jax.ShapeDtypeStruct(pair, F32)] * 2
        + [jax.ShapeDtypeStruct((width, LONG), BF16)] * 3
        + [jax.ShapeDtypeStruct(s, F32) for s in sum_shapes],
        grid_spec=pltpu.PrefetchScalarGridSpec(
            num_scalar_prefetch=1,
            grid=(1,),
            in_specs=specs,
            out_specs=[once(whole_spec, pair)] * 2
            + [once(whole_spec, (width, LONG))] * 3
            + [once(whole_spec, s) for s in sum_shapes],
            scratch_shapes=[pltpu.VMEM((LONG, 640), F32)],
        ),
        compiler_params=params(),
        cost_estimate=spent(12.4),
        name="attend_back",
    )(scalars, w_qkv, bias, q, k, v, do, lse, *(sums or ()))


def qkv_kernel(sc_ref, nf, no, qf, kf, vf, qo, ko, vo, pa, pb, *refs):
    db_ref = refs[2]
    blocks = [
        dot(far[...], nf[0]) + dot(own[...], no[0]) for far, own in ((qf, qo), (kf, ko), (vf, vo))
    ]
    blocks.append(pa[...] + pb[...])
    rows = blocks[0].shape[0]
    for i in range(2):
        at = pl.ds(i * rows, rows)
        refs[0][at] = jnp.where(sc_ref[4] == 0, blocks[i], blocks[2 + i])
        refs[1][at] = jnp.where(sc_ref[4] == 0, blocks[2 + i], blocks[i])
    for i, (far, own) in enumerate(((qf, qo), (vf, vo))):
        db_ref[:, i : i + 1] = jnp.sum(far[...].astype(F32), axis=1, keepdims=True) + jnp.sum(
            own[...].astype(F32), axis=1, keepdims=True
        )


def qkv_grad(scalars, n_far, n_own, far, own, proj_a, proj_b):
    dim = n_far.shape[2]
    width = far[0].shape[0]
    return pl.pallas_call(
        qkv_kernel,
        in_specs=[SCALARS] + [PLAIN] * 10,
        out_shape=[jax.ShapeDtypeStruct((2 * width, dim), F32)] * 2
        + [jax.ShapeDtypeStruct((width, 128), F32)],
        compiler_params=params(),
        cost_estimate=spent(4.5),
        name="qkv_grad",
    )(scalars, n_far, n_own, *far, *own, proj_a, proj_b)


def wide_rows(lo_ref, hi_ref):
    return jnp.concatenate([lo_ref[0], hi_ref[0]], axis=1)


def column_sum(x):
    return jnp.sum(x, axis=0, keepdims=True)


def feed_kernel(first, *refs):
    if not first:
        refs = refs[:14] + refs[15:]
    (sc_ref, tok_ref, out_ref, o0, oc, ox, od, wp0, wpc, wpx, wpd) = refs[:11]
    vec, w1, w2 = refs[11:14]
    mid_ref, a_ref, kept_ref, sent_ref, g_ref, n_ref, du_ref, dm_ref, o_scr, w_scr = refs[14:]
    low = lambda r: r.astype(BF16)
    place = sc_ref[3]
    for hop, (part, weight) in enumerate(((o0, wp0), (oc, wpc), (ox, wpx), (od, wpd))):
        at = place ^ hop
        o_scr[at] = low(part[0])
        w_scr[at] = low(weight[...])
    size = o_scr.shape[0] * o_scr.shape[1]
    o_all = o_scr[...].reshape(size, o_scr.shape[2])
    a = dot_tn(o_all, w_scr[...].reshape(size, w_scr.shape[2])) + vec[6:7]
    a_ref[0] = a
    mid = tok_ref[0].astype(F32) + vec[4:5] * a
    mid_ref[0] = mid
    n2 = layer_norm(mid, vec[2:3], vec[3:4])[0].astype(BF16)
    n_ref[0] = n2
    u = dot(n2, w1[...]) + vec[7:8]
    cdf = 0.5 * (1.0 + lax.erf(u * np.float32(np.sqrt(0.5))))
    slope = cdf + u * (jnp.exp(-0.5 * u * u) * np.float32(1 / np.sqrt(2 * np.pi)))
    g_ref[0] = (u * cdf).astype(BF16)
    dm = (vec[5:6] * out_ref[0].astype(F32)).astype(BF16)
    dm_ref[0] = dm
    du = (slope * dot_nt(dm, w2[...])).astype(BF16)
    du_ref[0] = du
    dn = dot_nt(du, w1[...])
    part_halves(sc_ref[2], dn, kept_ref, sent_ref)


def feed(scalars, tok3, out3, o_parts, w_parts, vec, w1, w2, mid=None):
    dim = tok3.shape[2]
    hid = w1.shape[1]
    width = w_parts[0].shape[0]
    pair = jax.ShapeDtypeStruct((LONG, dim // 2), F32)
    row = jax.ShapeDtypeStruct((1, LONG, dim), F32)
    both = jax.ShapeDtypeStruct((2, LONG, dim), F32)
    held = () if mid is None else (mid,)
    low = lambda n: jax.ShapeDtypeStruct((1, LONG, n), BF16)
    specs = (
        [once(pack_spec, (LONG, dim))] * 2
        + [once(first_spec, (width, LONG))] * 4
        + [once(whole_spec, (width, dim))] * 4
        + [
            once(whole_spec, (8, dim)),
            once(whole_spec, (dim, hid)),
            once(whole_spec, (hid, dim)),
        ]
    )
    specs += [pl.BlockSpec(memory_space=pl.ANY)] * len(held)
    return pl.pallas_call(
        partial(feed_kernel, mid is None),
        out_shape=[both, row, pair, pair, low(hid), low(dim), low(hid), low(dim)],
        grid_spec=pltpu.PrefetchScalarGridSpec(
            num_scalar_prefetch=1,
            grid=(1,),
            in_specs=specs,
            out_specs=[once(pack_spec, (LONG, dim)), once(first_spec, (LONG, dim))]
            + [once(whole_spec, pair.shape)] * 2
            + [once(first_spec, (LONG, n)) for n in (hid, dim, hid, dim)],
            scratch_shapes=[
                pltpu.VMEM((4, width, LONG), BF16),
                pltpu.VMEM((4, width, dim), BF16),
            ],
        ),
        compiler_params=params(),
        input_output_aliases={14: 0} if held else {},
        cost_estimate=spent(10),
        name="feed",
    )(scalars, tok3, out3, *o_parts, *w_parts, vec, w1, w2, *held)


SCALARS = pl.BlockSpec(memory_space=pltpu.SMEM)
PLAIN = pl.BlockSpec(memory_space=pltpu.VMEM)


def out_kernel(sc_ref, up, g, w2, kept_ref, sent_ref, sum_ref):
    m = dot(g[0], w2[...])
    part_halves(sc_ref[2], m, kept_ref, sent_ref)
    e = up[0].astype(F32)
    sum_ref[0:1] = column_sum(e * m)
    sum_ref[1:2] = column_sum(e)


def feed_out(scalars, up3, g, w2):
    hid, dim = w2.shape
    return pl.pallas_call(
        out_kernel,
        out_shape=[jax.ShapeDtypeStruct(n, F32) for n in [(LONG, dim // 2)] * 2 + [(2, dim)]],
        grid_spec=pltpu.PrefetchScalarGridSpec(
            num_scalar_prefetch=1,
            grid=(1,),
            in_specs=[
                once(pack_spec, (LONG, dim)),
                once(first_spec, (LONG, hid)),
                once(whole_spec, (hid, dim)),
            ],
            out_specs=[once(whole_spec, (LONG, dim // 2))] * 2 + [once(whole_spec, (2, dim))],
        ),
        compiler_params=params(),
        cost_estimate=spent(3.5),
        name="feed_out",
    )(scalars, up3, g, w2)


def part_blocks(bit, blocks, refs):
    for i in range(len(blocks) // 2):
        refs[2 * i][...] = jnp.where(bit == 0, blocks[2 * i], blocks[2 * i + 1])
        refs[2 * i + 1][...] = jnp.where(bit == 0, blocks[2 * i + 1], blocks[2 * i])


def feed_grad_kernel(sc_ref, up, gf, nf, uf, mf, go, no, uo, mo, w2, *refs):
    db1_ref, db2_ref = refs[4:6]
    d1 = dot_tn(nf[0], uf[0]) + dot_tn(no[0], uo[0])
    rows = d1.shape[0] // 2
    part_blocks(sc_ref[4], (d1[:rows], d1[rows:]), refs[:2])
    d2 = dot_tn(gf[0], mf[0]) + dot_tn(go[0], mo[0])
    part_blocks(sc_ref[5], (d2[:rows], d2[rows:]), refs[2:4])
    db1_ref[...] = column_sum(uf[0].astype(F32)) + column_sum(uo[0].astype(F32))
    db2_ref[...] = column_sum(mf[0].astype(F32)) + column_sum(mo[0].astype(F32))
    out_kernel(sc_ref, up, go, w2, *refs[6:])


def feed_grad(scalars, up3, far, own, w2):
    hid, dim = w2.shape
    shapes = [(dim // 2, hid)] * 2 + [(hid // 2, dim)] * 2 + [(1, hid), (1, dim)]
    shapes += [(LONG, dim // 2)] * 2 + [(2, dim)]
    kept = [once(first_spec, (LONG, n)) for n in (hid, dim, hid, dim)]
    return pl.pallas_call(
        feed_grad_kernel,
        out_shape=[jax.ShapeDtypeStruct(n, F32) for n in shapes],
        grid_spec=pltpu.PrefetchScalarGridSpec(
            num_scalar_prefetch=1,
            grid=(1,),
            in_specs=[once(pack_spec, (LONG, dim))]
            + kept * 2
            + [once(whole_spec, (hid, dim))],
            out_specs=[once(whole_spec, n) for n in shapes],
        ),
        compiler_params=params(),
        cost_estimate=spent(9.5),
        name="feed_grad",
    )(scalars, up3, *far, *own, w2)


def norm_back(upstream, unit_rows, inverse, gain_row):
    scaled = upstream * gain_row
    centred = scaled - jnp.mean(scaled, axis=-1, keepdims=True)
    centred = centred - unit_rows * jnp.mean(scaled * unit_rows, axis=-1, keepdims=True)
    return inverse * centred, column_sum(upstream * unit_rows), column_sum(upstream)


def joined(sc_ref, mine, peer):
    core = sc_ref[2]
    lo = jnp.where(core == 0, mine[...], peer[...])
    hi = jnp.where(core == 0, peer[...], mine[...])
    return jnp.concatenate([lo, hi], axis=1)


def middle_kernel(
    sc_ref, out_ref, mid_ref, a_ref, mine, peer, vec, wp0, wpx, o0, ox,
    dmid_ref, do0_ref, dox_ref, dp0_ref, dpx_ref, sum_ref
):
    dn2 = joined(sc_ref, mine, peer)
    _, unit, inverse = layer_norm(mid_ref[0], vec[2:3], vec[3:4])
    back, d_gain, d_shift = norm_back(dn2, unit, inverse, vec[2:3])
    dmid = out_ref[0].astype(F32) + back
    dmid_ref[0] = dmid
    da = (vec[4:5] * dmid).astype(BF16)
    do0_ref[0] = dot_nt(wp0[...], da).astype(BF16).astype(F32)
    dox_ref[0] = dot_nt(wpx[...].astype(BF16), da).astype(BF16).astype(F32)
    dp0_ref[...] = dot(o0[0].astype(BF16), da)
    dpx_ref[...] = dot(ox[0].astype(BF16), da)
    sum_ref[0:1] = d_gain
    sum_ref[1:2] = d_shift
    sum_ref[2:3] = column_sum(dmid * a_ref[0])
    sum_ref[3:4] = column_sum(da.astype(F32))


def middle_back(scalars, out3, mid, a, mine, peer, vec, w_parts, o_parts):
    dim = mid.shape[2]
    width = w_parts[0].shape[0]
    row = jax.ShapeDtypeStruct((1, LONG, dim), F32)
    low = jax.ShapeDtypeStruct((1, width, LONG), F32)
    mat = jax.ShapeDtypeStruct((width, dim), F32)
    return pl.pallas_call(
        middle_kernel,
        out_shape=[row, low, low, mat, mat, jax.ShapeDtypeStruct((4, dim), F32)],
        grid_spec=pltpu.PrefetchScalarGridSpec(
            num_scalar_prefetch=1,
            grid=(1,),
            in_specs=[
                once(pack_spec, (LONG, dim)),
                once(pack_spec, (LONG, dim)),
                once(first_spec, (LONG, dim)),
                once(whole_spec, (LONG, dim // 2)),
                once(whole_spec, (LONG, dim // 2)),
                once(whole_spec, (8, dim)),
                once(whole_spec, (width, dim)),
                once(whole_spec, (width, dim)),
                once(first_spec, (width, LONG)),
                once(first_spec, (width, LONG)),
            ],
            out_specs=[
                once(first_spec, (LONG, dim)),
                once(first_spec, (width, LONG)),
                once(first_spec, (width, LONG)),
                once(whole_spec, (width, dim)),
                once(whole_spec, (width, dim)),
                once(whole_spec, (4, dim)),
            ],
        ),
        compiler_params=params(),
        cost_estimate=spent(7.7),
        name="middle_back",
    )(scalars, out3, mid, a, mine, peer, vec, *w_parts[::2], *o_parts[::2])


def final_kernel(sc_ref, tok_ref, dmid_ref, mine, peer, vec, two, scale, out_ref, sent_ref, sum_ref):
    dn1 = joined(sc_ref, mine, peer)
    _, unit, inverse = layer_norm(tok_ref[0].astype(F32), vec[0:1], vec[1:2])
    back, d_gain, d_shift = norm_back(dn1, unit, inverse, vec[0:1])
    result = dmid_ref[0] + back
    out_ref[0] = result
    half = result.shape[1] // 2
    rows = jnp.concatenate([two[...], d_gain, d_shift, scale[...]], axis=0)
    sum_ref[...] = rows
    sent_ref[0:LONG] = jnp.where(sc_ref[2] == 0, result[:, :half], result[:, half:])
    sent_ref[LONG : LONG + 8] = rows[:, :half]
    sent_ref[LONG + 8 : LONG + 16] = rows[:, half:]


def final_back(scalars, tok3, dmid, mine, peer, vec, two, scale):
    dim = tok3.shape[2]
    return pl.pallas_call(
        final_kernel,
        out_shape=[
            jax.ShapeDtypeStruct((1, LONG, dim), F32),
            jax.ShapeDtypeStruct((LONG + 16, dim // 2), F32),
            jax.ShapeDtypeStruct((8, dim), F32),
        ],
        grid_spec=pltpu.PrefetchScalarGridSpec(
            num_scalar_prefetch=1,
            grid=(1,),
            in_specs=[
                once(pack_spec, (LONG, dim)),
                once(first_spec, (LONG, dim)),
                once(whole_spec, (LONG, dim // 2)),
                once(whole_spec, (LONG, dim // 2)),
                once(whole_spec, (8, dim)),
                once(whole_spec, (4, dim)),
                once(whole_spec, (2, dim)),
            ],
            out_specs=[
                once(first_spec, (LONG, dim)),
                once(whole_spec, (LONG + 16, dim // 2)),
                once(whole_spec, (8, dim)),
            ],
        ),
        compiler_params=params(),
        cost_estimate=spent(5.6),
        name="final_back",
    )(scalars, tok3, dmid, mine, peer, vec, two, scale)


def last_kernel(sc_ref, kept, got, flat_ref, b2, _, qkv_ref, proj_ref, *refs):
    gains, shifts, scales, singles, bias, table = refs
    rows = kept.shape[0]
    width = rows // 2
    swap = sc_ref[4] == 0
    for i, lo in enumerate((0, width)):
        a = kept[lo : lo + width]
        b = got[lo : lo + width]
        qkv_ref[i] = jnp.where(swap, a, b)
        other = jnp.where(swap, b, a)
        if i == 0:
            qkv_ref[2] = other
        else:
            proj_ref[...] = other
    flat = flat_ref[...]
    gains[0:1] = flat[4:5]
    gains[1:2] = flat[0:1]
    shifts[0:1] = flat[5:6]
    shifts[1:2] = flat[1:2]
    scales[0:1] = flat[2:3]
    scales[1:2] = flat[6:7] + b2[...].astype(F32) * flat[10:11]
    singles[0:1] = flat[3:4]
    singles[1:3] = flat[8:10]
    count = table.shape[1]
    for h in range(table.shape[0]):
        for i in range(3):
            row = flat[11 + 3 * h + i : 12 + 3 * h + i]
            lo = i * flat.shape[1]
            hi = min(lo + flat.shape[1], count)
            table[h : h + 1, lo:hi] = row[:, : hi - lo]
    row = flat[11 + 3 * table.shape[0] : 12 + 3 * table.shape[0]]
    bias[0:1] = row[:, :width]
    bias[1:2] = row[:, width : 2 * width]


def last_parts(scalars, kept, got, flat, b2, after, heads, count):
    rows, dim = kept.shape
    width = rows // 2
    shapes = [(3, width, dim), (width, dim)] + [(2, dim)] * 3 + [(3, dim), (2, width), (heads, count)]
    return pl.pallas_call(
        last_kernel,
        in_specs=[SCALARS] + [PLAIN] * 4 + [pl.BlockSpec(memory_space=pl.ANY)],
        out_shape=[jax.ShapeDtypeStruct(n, F32) for n in shapes],
        compiler_params=params(),
        cost_estimate=spent(3),
        name="last_parts",
    )(scalars, kept, got, flat, b2, after)


CORE = [(i, i ^ 1) for i in range(4)]
ACROSS = [(i, i ^ 2) for i in range(4)]


def to_core(x):
    return lax.ppermute(x, "narrow", CORE)


def to_chip(x):
    return lax.ppermute(x, "narrow", ACROSS)


def pick(pair, index):
    return lax.dynamic_index_in_dim(pair, index, 0, keepdims=False)


def small_sum(x, size):
    step = 1
    while step < size:
        x = x + lax.ppermute(x, "wide", [(i, i ^ step) for i in range(size)])
        step *= 2
    return x


def tie(*values):
    return lax.optimization_barrier(values)


def in_order(bit, first, second):
    return jnp.where(bit == 0, first, second), jnp.where(bit == 0, second, first)


WIDE_PLACES = 8
DUE = {
    "one": (1, 2, 3, 5, 8),
    "two": (1, 3, 5, 9, 13),
    "last": (4, 6, 9, 11, 14),
    "flat": (9, 11, 14),
}


class Wave:
    def __init__(self, place):
        self.place = place
        self.live = {}
        self.done = {}

    def bit(self, step):
        return (self.place // step) % 2

    def send(self, value, step):
        return lax.ppermute(value, "wide", [(i, i ^ step) for i in range(WIDE_PLACES)])

    def add(self, name, kept, sent, steps, due, whole=False):
        got = self.send(sent, steps[0])
        self.live[name] = dict(steps=steps, stage=0, kept=kept, got=got, due=list(due), whole=whole)

    def advance(self, c, got):
        stage, kept, (first, second, third) = c["stage"], c["kept"], c["steps"]
        if c["whole"]:
            total = kept + got
            return (total, total, (first, second, third)[stage + 1]) if stage < 2 else (total, None, None)
        if stage == 0:
            rows = kept.shape[0] // 2
            split = lambda v: v.reshape((2, rows) + v.shape[1:])
            side = self.bit(second)
            kept, got = split(kept), split(got)
            send = pick(kept, 1 - side) + pick(got, 1 - side)
            return pick(kept, side) + pick(got, side), send, second
        if stage < 3:
            total = kept + got
        elif stage == 3:
            total = jnp.concatenate(in_order(self.bit(second), kept, got))
        else:
            return (kept, got), None, None
        return total, total, (third, second, first)[stage - 1]

    def event(self, now, then):
        ripe = [n for n, c in self.live.items() if c["due"][0] <= now]
        if not ripe:
            return then
        then, *values = tie(then, *[self.live[n]["got"] for n in ripe])
        moves = {n: self.advance(self.live[n], got) for n, got in zip(ripe, values)}
        for n in ripe:
            if moves[n][1] is None:
                self.done[n] = moves[n][0]
                del self.live[n], moves[n]
        if not moves:
            return then
        held = tie(then, *[m[1] for m in moves.values()])
        for (n, (kept, _, step)), value in zip(moves.items(), held[1:]):
            c = self.live[n]
            c["kept"] = kept
            c["got"] = self.send(value, step)
            c["stage"] += 1
            c["due"].pop(0)
        return held[0]


def on_device(
    tokens, w_qkv, qv_bias, w_proj, proj_bias, w_fc1, fc1_bias, w_fc2, fc2_bias, norm_gains,
    norm_shifts, layer_scales, rel_table, image_ids, pad_mask, grid_rows, grid_cols, d_out, wide
):
    rows, dim = tokens.shape
    width = w_qkv.shape[2]
    place = lax.axis_index("narrow")
    chip, core = place // 2, place % 2
    spot = lax.axis_index("wide")
    tok3 = tokens.reshape(2, LONG, dim)
    out3 = d_out.reshape(2, LONG, dim)
    w_turned = w_qkv.transpose(0, 2, 1)
    kind_a = image_ids[LONG - 1] % 2
    kind_b = image_ids[2 * LONG - 1] % 2
    common = (core, place, spot % 2, (spot // 2) % 2)
    sc_far = jnp.stack([1 - chip, jnp.where(chip == 0, kind_b, kind_a), *common])
    sc_own = jnp.stack([chip, jnp.where(chip == 0, kind_a, kind_b), *common])
    pairs = zip(norm_gains.astype(F32), norm_shifts.astype(F32))
    vec = jnp.stack(
        [v for pair in pairs for v in pair]
        + list(layer_scales.astype(F32))
        + [proj_bias.astype(F32), fc1_bias.astype(F32)]
    )

    wp_near = w_proj.astype(F32)
    wp_far = to_chip(wp_near)
    bias = make_bias(rel_table)
    first = lambda sc: attend(sc, tok3, w_turned, qv_bias, vec, bias)
    o_far, *saved_far, n_far = first(sc_far)
    wp_far, o_sent = tie(wp_far, o_far)
    x_own = to_chip(o_sent)
    w_parts = (w_proj, to_core(wp_near), wp_far, to_core(wp_far))
    o_own, *saved_own, n_own = first(sc_own)
    x_own, o_sent = tie(x_own, o_own)
    x_far = to_chip(o_sent)
    far_parts = (o_far, to_core(o_far), x_far, to_core(x_far))
    own_parts = (o_own, to_core(o_own), x_own, to_core(x_own))

    shared = (w_parts, vec, w_fc1, w_fc2)
    mid, _, dn_kept, dn_send, *kept_far = feed(sc_far, tok3, out3, far_parts, *shared)
    peer = to_core(dn_send)
    sc, _ = tie(sc_far, dn_send)
    m_far_kept, m_far_send, scale_far = feed_out(sc, out3, kept_far[0], w_fc2)
    peer, scale_far = tie(peer, scale_far)
    half, sc = tie(dn_kept + peer, sc_own)
    dn_got = to_chip(half)
    mid, a_own, dn_kept, dn_send, *kept_own = feed(sc, tok3, out3, own_parts, *shared, mid)
    peer = to_core(dn_send)
    *blocks, d_fc1_bias, d_fc2_bias, m_own_kept, m_own_send, scale_own = feed_grad(
        sc_own, out3, kept_far, kept_own, w_fc2
    )

    wave = Wave(spot)
    custom = wide == WIDE_PLACES
    if custom:
        wave.add("one", blocks[0], blocks[1], (1, 2, 4), DUE["one"])
        wave.add("two", blocks[2], blocks[3], (2, 1, 4), DUE["two"])
    dn_got, scale_own = tie(dn_got, scale_own)
    part, peer = tie(dn_kept + dn_got, peer)
    mine = part + peer
    theirs = to_core(mine)
    dmid, do_own, do_send, dp_own, dp_send, sums_two = middle_back(
        sc_own, out3, mid, a_own, mine, theirs, vec, w_parts, own_parts
    )
    do_far = to_chip(do_send)
    m_far_peer, m_own_peer, _ = tie(to_core(m_far_send), to_core(m_own_send), dmid)
    m_half_far = m_far_kept + m_far_peer
    m_half_own = m_own_kept + m_own_peer
    scale = scale_far + scale_own
    up_sum = scale[1:2]
    scale, _ = tie(scale, dmid)
    scale = scale + to_core(scale)
    do_far, m_half_far, m_half_own, scale = tie(do_far, m_half_far, m_half_own, scale)
    do_far, sc = tie(do_far, sc_far)
    sc = wave.event(1, sc)
    dp_send, sc = tie(dp_send, sc)
    dp_got = to_chip(dp_send)

    dn_kept, dn_send, *far, dl, ds, dt = attend_back(sc, w_turned, bias, saved_far, do_far, None)
    dn_send, dp_got = tie(dn_send, dp_got)
    dn_send = wave.event(2, dn_send)
    peer = to_core(dn_send)
    half, sc, dp_got = tie(dn_kept + peer, sc_own, dp_got)
    dn_got = to_chip(half)
    dn_kept, dn_send, *own, dl, ds, dt = attend_back(
        sc, w_turned, bias, saved_own, do_own, (dl, ds, dt)
    )
    *pieces, d_qv_bias = qkv_grad(sc_own, n_far, n_own, far, own, dp_own, dp_got)
    dn_got, d_qv_bias, dn_send = tie(dn_got, d_qv_bias, dn_send)
    dn_send = wave.event(3, dn_send)
    peer = to_core(dn_send)
    if custom:
        wave.add("last", pieces[0], pieces[1], (1, 2, 4), DUE["last"])
    part, peer = tie(dn_kept + dn_got, peer)
    mine = part + peer
    theirs = to_core(mine)
    tok_own, tok_send, own_rows = final_back(
        sc_own, tok3, dmid, mine, theirs, vec, sums_two, scale
    )
    tok_got = to_chip(tok_send)
    dl, ds, dt, own_rows = tie(dl, ds, dt, own_rows)
    table_back = strips_back(dl, ds, dt)
    heads, count = table_back.shape
    row_bias = jnp.pad(d_qv_bias[:, :2].T.reshape(1, -1), ((0, 0), (0, dim - 2 * width)))
    rest = jnp.pad(table_back, ((0, 0), (0, 3 * dim - count))).reshape(3 * heads, dim)
    rest = [d_fc2_bias, d_fc1_bias, up_sum, rest, row_bias, jnp.zeros((12 - 3 * heads, dim), F32)]
    rest = jnp.concatenate(rest)
    rest, own_rows = tie(rest, own_rows)
    mark = wave.event(4, own_rows)
    mark = wave.event(5, mark)
    tok_got, mark = tie(tok_got, mark)
    tok_peer = to_core(tok_got)
    m_send, mark = tie(m_half_far, mark)
    m_all_own = to_chip(m_send)
    mark = wave.event(6, mark)
    own_rows = mark + jnp.concatenate([tok_got[LONG : LONG + 8], tok_got[LONG + 8 :]], axis=1)
    flat = jnp.concatenate([own_rows, rest])
    mark = flat
    if custom:
        wave.add("flat", mark, mark, (4, 2, 1), DUE["flat"], True)
    tok_peer, mark = tie(tok_peer, mark)
    tok_far = jnp.concatenate(in_order(core, tok_got[:LONG], tok_peer[:LONG]), axis=1)[None]
    d_tokens = jnp.concatenate(in_order(chip, tok_own, tok_far)).reshape(rows, dim)
    d_tokens, mark = tie(d_tokens, mark)
    m_all_own, mark = tie(m_all_own, mark)
    m_all_own = m_half_own + m_all_own
    m_own_peer = to_core(m_all_own)
    m_send, m_all_own = tie(m_half_own, m_all_own)
    m_all_far = to_chip(m_send)
    mark = wave.event(8, mark)
    if custom:
        d_fc1 = jnp.concatenate(in_order(spot % 2, *wave.done["one"]))
        d_fc1, mark = tie(d_fc1, mark)
    mark = wave.event(9, mark)
    m_all_far, mark = tie(m_all_far, mark)
    m_all_far = m_half_far + m_all_far
    m_far_peer = to_core(m_all_far)
    mark = wave.event(11, mark)
    m_own_peer, m_far_peer, mark = tie(m_own_peer, m_far_peer, mark)
    m_own = jnp.concatenate(in_order(core, m_all_own, m_own_peer), axis=1)[None]
    m_far = jnp.concatenate(in_order(core, m_all_far, m_far_peer), axis=1)[None]
    m_full = jnp.concatenate(in_order(chip, m_own, m_far)) + fc2_bias.astype(F32)
    block_out = (mid + layer_scales[1].astype(F32) * m_full).astype(BF16).reshape(rows, dim)
    block_out, mark = tie(block_out, mark)
    mark = wave.event(13, mark)
    if custom:
        d_fc2 = jnp.concatenate(in_order((spot // 2) % 2, *wave.done["two"]))
        d_fc2, mark = tie(d_fc2, mark)
    mark = wave.event(14, mark)
    if custom:
        got = wave.done
        kept, last = got["last"]
        flat = got["flat"]
    else:
        low, high = spot % 2, (spot // 2) % 2
        d_fc1 = jnp.concatenate(in_order(low, blocks[0], blocks[1]))
        d_fc2 = jnp.concatenate(in_order(high, blocks[2], blocks[3]))
        pieces = in_order(low, *pieces)
        pieces, d_fc1, d_fc2 = lax.psum((pieces, d_fc1, d_fc2), "wide")
        kept, last = in_order(low, *pieces)
        flat = small_sum(flat, wide)
    d_qkv, d_proj, d_norm_gains, d_norm_shifts, d_layer_scales, singles, d_qv_bias, d_table = last_parts(
        sc_own, kept, last, flat, fc2_bias[None], mark, heads, count
    )
    d_proj_bias, d_fc2_bias, d_fc1_bias = singles
    d_qkv = d_qkv.transpose(0, 2, 1)
    return (
        block_out,
        d_tokens,
        d_qkv,
        d_qv_bias,
        d_proj,
        d_proj_bias,
        d_fc1,
        d_fc1_bias,
        d_fc2,
        d_fc2_bias,
        d_norm_gains,
        d_norm_shifts,
        d_layer_scales,
        d_table,
    )


def solution(mesh):
    in_specs = (
        P("wide", None),
        P(None, None, "narrow"),
        P(None, "narrow"),
        P("narrow", None),
        P(),
        P(None, "narrow"),
        P("narrow"),
        P("narrow", None),
        P(),
        P(),
        P(),
        P(),
        P("narrow", None),
        P("wide"),
        P("wide"),
        P("wide"),
        P("wide"),
        P("wide", None),
    )
    out_specs = (
        P("wide", None),
        P("wide", None),
        P(None, None, "narrow"),
        P(None, "narrow"),
        P("narrow", None),
        P(),
        P(None, "narrow"),
        P("narrow"),
        P("narrow", None),
        P(),
        P(),
        P(),
        P(),
        P("narrow", None),
    )
    return jax.shard_map(
        partial(on_device, wide=mesh.shape["wide"]),
        mesh=mesh,
        in_specs=in_specs,
        out_specs=out_specs,
        check_vma=False,
    )
```

```python
from functools import partial

import jax
import jax.numpy as jnp
import numpy as np
from jax import lax
from jax.experimental import pallas as pl
from jax.experimental.pallas import tpu as pltpu
from jax.sharding import PartitionSpec as P

HD = 64
GRID = 24
SMALL = 14
SHORT = 208
LONG = 584
EPSILON = 1e-06
SIDE = 2 * GRID - 1
WIDE_L = 1280
WIDE_S = 640
NEG = -1e30
F32 = jnp.float32
BF16 = jnp.bfloat16
VMEM_LIMIT = 56 << 20
COST_SCALE = 1.2e8


def params(**kw):
    return pltpu.CompilerParams(vmem_limit_bytes=VMEM_LIMIT, **kw)


def spent(microseconds):
    work = int(microseconds * COST_SCALE)
    return pl.CostEstimate(flops=work, transcendentals=0, bytes_accessed=1024)


def dot(a, b):
    return jnp.dot(a, b, preferred_element_type=F32)


def dot_nt(a, b):
    return lax.dot_general(a, b, (((1,), (1,)), ((), ())), preferred_element_type=F32)


def dot_tn(a, b):
    return lax.dot_general(a, b, (((0,), (0,)), ((), ())), preferred_element_type=F32)


def large_pick():
    pick = np.zeros((2, SIDE, GRID, GRID), np.float32)
    for s in range(GRID):
        for c in range(GRID):
            if s == 0:
                pick[1, c, s, c] = 1
            else:
                pick[0, c + GRID - s, s, c] = 1
    return pick.reshape(2 * SIDE, GRID * GRID)


def small_pick():
    pick = np.zeros((SIDE, 16, SMALL), np.float32)
    for s in range(SMALL):
        for c in range(SMALL):
            pick[c - s + GRID - 1, s, c] = 1
    return pick.reshape(SIDE, 16 * SMALL)


def strips_back(d_large, d_small, d_tails):
    heads = d_large.shape[0]
    rows = 2 * SMALL - 1
    hi = lax.Precision.HIGHEST
    large = d_large[:, :, 1 : 1 + (SIDE + 1) * GRID].reshape(heads, GRID, SIDE + 1, GRID)
    both = jnp.einsum(
        "hsuc,ksc->huk",
        large,
        jnp.asarray(large_pick().reshape(2 * SIDE, GRID, GRID)),
        precision=hi,
    )
    grid_grad = both[:, 1:, :SIDE] + both[:, :SIDE, SIDE:]
    small = d_small[:, :, 1 : 1 + rows * SMALL].reshape(heads, 16, rows, SMALL)
    part = jnp.einsum(
        "hsuc,ksc->huk", small, jnp.asarray(small_pick().reshape(SIDE, 16, SMALL)), precision=hi
    )
    low = GRID - SMALL
    grid_grad = grid_grad + jnp.pad(part, ((0, 0), (low, SIDE - low - rows), (0, 0)))
    return jnp.concatenate(
        [grid_grad.reshape(heads, SIDE * SIDE), d_tails[:, 0, :3]], axis=1
    )


def tail_fix(block, t0, t1, t2, last, real):
    shape = block.shape
    row = lax.broadcasted_iota(jnp.int32, shape, 0)
    lane = lax.broadcasted_iota(jnp.int32, shape, 1)
    block = jnp.where(lane > last, block[:, 1:2], block)
    block = jnp.where(lane == 0, t0, block)
    block = jnp.where(row == 0, jnp.where(lane == 0, t2, t1), block)
    return jnp.where(row >= real, NEG, block)


def windows(table, grid, first, width):
    shape = (table.shape[0], width)
    row = lax.broadcasted_iota(jnp.int32, shape, 0) - first
    lane = lax.broadcasted_iota(jnp.int32, shape, 1)
    inside = (lane >= grid * row) & (lane < grid * row + grid)
    spread = dot_tn(table, inside.astype(F32).astype(BF16))
    start = jnp.sum(jnp.where(inside, grid * row, 0), axis=0, keepdims=True)
    return spread, lane[0:1] - start


def bias_kernel(tail_ref, table_ref, out_ref, scr, large_ref, small_ref, rows):
    large_ref[...] = jnp.zeros_like(large_ref)
    small_ref[...] = jnp.zeros_like(small_ref)
    rows[...] = jnp.zeros_like(rows)
    for h in range(table_ref.shape[0]):
        table = table_ref[h].astype(BF16)
        spread, within = windows(table, GRID, 0, (SIDE + 1) * GRID)
        rows[8:56, :] = spread
        strip = jnp.zeros((GRID, (SIDE + 1) * GRID), F32)
        top = jnp.zeros((1, (SIDE + 1) * GRID), F32)
        for c in range(GRID):
            here = within == c
            strip = jnp.where(here, rows[30 - c : 54 - c, :], strip)
            top = jnp.where(here, rows[54 - c : 55 - c, :], top)
        large_ref[h, :, 1 + GRID : 1 + GRID + SIDE * GRID] = strip[:, : SIDE * GRID]
        large_ref[h, 0:1, :] = jnp.zeros((1, WIDE_L), F32)
        large_ref[h, 0:1, 1 : 1 + SIDE * GRID] = top[:, : SIDE * GRID]
        spread, within = windows(table, SMALL, GRID - SMALL, 384)
        rows[8:56, 0:384] = spread
        strip = jnp.zeros((16, 384), F32)
        for c in range(SMALL):
            strip = jnp.where(within == c, rows[31 - c : 47 - c, 0:384], strip)
        count = (2 * SMALL - 1) * SMALL
        small_ref[h, :, 1 : 1 + count] = strip[:, :count]
        t0, t1, t2 = tail_ref[h, 0], tail_ref[h, 1], tail_ref[h, 2]
        for r in range(GRID + 1):
            size = GRID if r < GRID else LONG - GRID * GRID
            off = (GRID - r) * GRID
            scr[r * GRID : r * GRID + size, 0:LONG] = large_ref[h, 0:size, off : off + LONG]
        last = GRID * GRID
        out_ref[0, h] = tail_fix(scr[:, 0:LONG], t0, t1, t2, last, last + 1).astype(BF16)
        last = SMALL * SMALL
        for r in range(SMALL):
            off = (SMALL - 1 - r) * SMALL
            wide = LONG - SHORT
            scr[1 + r * SMALL : 1 + (r + 1) * SMALL, 0:wide] = small_ref[
                h, 0:SMALL, off : off + wide
            ]
        block = tail_fix(scr[0:SHORT, 0 : LONG - SHORT], t0, t1, t2, last, last + 1)
        scr[...] = jnp.full(scr.shape, NEG, F32)
        scr[0:SHORT, 0:SHORT] = block[:, 0:SHORT]
        scr[SHORT : 2 * SHORT, SHORT:LONG] = block
        out_ref[1, h] = scr[:, 0:LONG].astype(BF16)


def make_bias(rel_table):
    heads = rel_table.shape[0]
    tails = rel_table[:, SIDE * SIDE :].astype(F32)
    table = rel_table[:, : SIDE * SIDE].reshape(heads, SIDE, SIDE)[:, :, ::-1]
    table = jnp.pad(table.astype(F32), ((0, 0), (0, 1), (0, 1)))
    return pl.pallas_call(
        bias_kernel,
        out_shape=jax.ShapeDtypeStruct((2, heads, LONG, LONG), BF16),
        in_specs=[
            pl.BlockSpec(memory_space=pltpu.SMEM),
            pl.BlockSpec(memory_space=pltpu.VMEM),
        ],
        out_specs=pl.BlockSpec(memory_space=pltpu.VMEM),
        scratch_shapes=[
            pltpu.VMEM((LONG, 640), F32),
            pltpu.VMEM((heads, GRID, WIDE_L), F32),
            pltpu.VMEM((heads, 16, WIDE_S), F32),
            pltpu.VMEM((64, (SIDE + 1) * GRID), F32),
        ],
        compiler_params=params(),
        cost_estimate=spent(6),
        name="bias",
    )(tails, table)


def layer_norm(values, gain_row, shift_row):
    row_mean = jnp.mean(values, axis=-1, keepdims=True)
    centred = values - row_mean
    inverse = lax.rsqrt(jnp.mean(centred * centred, axis=-1, keepdims=True) + EPSILON)
    unit_rows = centred * inverse
    return unit_rows * gain_row + shift_row, unit_rows, inverse


def part_halves(core, value, kept_ref, sent_ref):
    half = value.shape[1] // 2
    lo, hi = value[:, :half], value[:, half:]
    kept_ref[...] = jnp.where(core == 0, lo, hi)
    sent_ref[...] = jnp.where(core == 0, hi, lo)


def head_lanes(shape, h):
    lane = lax.broadcasted_iota(jnp.int32, shape, 1)
    return (lane >= h * HD) & (lane < (h + 1) * HD)


def turned(block):
    return block.astype(F32).T.astype(BF16)


def forward_kernel(
    sc_ref, tok_ref, w_ref, qv_ref, vec, bias_ref, o_ref, q_ref, k_ref, v_ref, lse_ref, n_ref
):
    x = tok_ref[0].astype(F32)
    n1 = layer_norm(x, vec[0:1], vec[1:2])[0].astype(BF16)
    qv = qv_ref[...].astype(F32)
    q = ((dot_nt(n1, w_ref[0]) + qv[0:1]) * HD**-0.5).astype(BF16)
    k = dot_nt(n1, w_ref[1]).astype(BF16)
    v = (dot_nt(n1, w_ref[2]) + qv[1:2]).astype(BF16)
    q_ref[0] = q
    k_ref[0] = k
    v_ref[0] = v
    n_ref[0] = n1
    v_t = turned(v)
    outs = []
    for h in range(k.shape[1] // HD):
        k_h = jnp.where(head_lanes(k.shape, h), k, jnp.zeros_like(k))
        s = dot_nt(k_h, q) + bias_ref[0, h].astype(F32)
        top = jnp.max(s, axis=0, keepdims=True)
        e = jnp.exp(s - top)
        total = jnp.sum(e, axis=0, keepdims=True)
        p = (e * (1.0 / total)).astype(BF16)
        outs.append(dot(v_t[h * HD : (h + 1) * HD], p))
        lse_ref[0, h : h + 1, :] = top + jnp.log(total)
    o_ref[0] = jnp.concatenate(outs, axis=0).astype(BF16).astype(F32)


def once(spec_of, shape):
    spec = spec_of(shape)
    return pl.BlockSpec(spec.block_shape, spec.index_map, pipeline_mode=pl.Buffered(1))


def pack_spec(shape):
    return pl.BlockSpec((1,) + shape, lambda i, sc: (sc[0],) + (0,) * len(shape))


def first_spec(shape):
    return pl.BlockSpec((1,) + shape, lambda i, sc: (0,) * (1 + len(shape)))


def whole_spec(shape):
    return pl.BlockSpec(shape, lambda i, sc: (0,) * len(shape))


def kind_spec(shape):
    return pl.BlockSpec((1,) + shape, lambda i, sc: (sc[1],) + (0,) * len(shape))


def attend(scalars, tok3, w_qkv, qv_bias, vec, bias):
    width = w_qkv.shape[1]
    heads = width // HD
    dim = tok3.shape[2]
    low = jax.ShapeDtypeStruct((1, LONG, width), BF16)
    return pl.pallas_call(
        forward_kernel,
        out_shape=[
            jax.ShapeDtypeStruct((1, width, LONG), F32),
            low,
            low,
            low,
            jax.ShapeDtypeStruct((1, heads, LONG), F32),
            jax.ShapeDtypeStruct((1, LONG, dim), BF16),
        ],
        grid_spec=pltpu.PrefetchScalarGridSpec(
            num_scalar_prefetch=1,
            grid=(1,),
            in_specs=[
                pack_spec((LONG, dim)),
                whole_spec((3, width, dim)),
                whole_spec((2, width)),
                whole_spec((8, dim)),
                kind_spec((heads, LONG, LONG)),
            ],
            out_specs=[first_spec((width, LONG))]
            + [first_spec((LONG, width))] * 3
            + [first_spec((heads, LONG)), first_spec((LONG, dim))],
        ),
        compiler_params=params(),
        cost_estimate=spent(7.4),
        name="attend",
    )(scalars, tok3, w_qkv, qv_bias, vec, bias)


def fold_large(ds, h, dl_ref, dt_ref):
    last = GRID * GRID
    full = ds[:, 0:LONG]
    lane = lax.broadcasted_iota(jnp.int32, full.shape, 1)
    row = lax.broadcasted_iota(jnp.int32, full.shape, 0)
    pad = jnp.sum(jnp.where(lane > last, full, 0.0), axis=1, keepdims=True)
    body = row > 0
    t0 = jnp.sum(jnp.where((lane == 0) & body, full, 0.0))
    t1 = jnp.sum(jnp.where((lane > 0) & (row == 0), full, 0.0))
    t2 = jnp.sum(jnp.where((lane == 0) & (row == 0), full, 0.0))
    full = jnp.where((lane == 0) | (lane > last), 0.0, full)
    full = jnp.where(lane == 1, full + pad, full)
    ds[:, 0:LONG] = jnp.where(body, full, 0.0)
    for r in range(GRID + 1):
        size = GRID if r < GRID else LONG - GRID * GRID
        off = (GRID - r) * GRID
        dl_ref[h, 0:size, off : off + LONG] += ds[r * GRID : r * GRID + size, 0:LONG]
    tail_add(dt_ref, h, t0, t1, t2)


def tail_add(dt_ref, h, t0, t1, t2):
    lane = lax.broadcasted_iota(jnp.int32, (8, 128), 1)
    row = lax.broadcasted_iota(jnp.int32, (8, 128), 0)
    add = jnp.where(lane == 0, t0, jnp.where(lane == 1, t1, jnp.where(lane == 2, t2, 0.0)))
    dt_ref[h] += jnp.where(row == 0, add, 0.0)


def fold_small(ds, h, ds_ref, dt_ref):
    last = SMALL * SMALL
    for base, wide in ((0, SHORT), (SHORT, LONG - SHORT)):
        full = ds[base : base + SHORT, 0:LONG]
        if base:
            full = full[:, base : base + wide]
        else:
            full = full[:, 0:wide]
        lane = lax.broadcasted_iota(jnp.int32, full.shape, 1)
        row = lax.broadcasted_iota(jnp.int32, full.shape, 0)
        pad = jnp.sum(jnp.where(lane > last, full, 0.0), axis=1, keepdims=True)
        body = row > 0
        t0 = jnp.sum(jnp.where((lane == 0) & body, full, 0.0))
        t1 = jnp.sum(jnp.where((lane > 0) & (row == 0), full, 0.0))
        t2 = jnp.sum(jnp.where((lane == 0) & (row == 0), full, 0.0))
        full = jnp.where((lane == 0) | (lane > last), 0.0, full)
        full = jnp.where(lane == 1, full + pad, full)
        ds[base : base + SHORT, 0:wide] = full
        for r in range(SMALL):
            off = (SMALL - 1 - r) * SMALL
            lo = base + 1 + r * SMALL
            ds_ref[h, 0:SMALL, off : off + wide] += ds[lo : lo + SMALL, 0:wide]
        tail_add(dt_ref, h, t0, t1, t2)


def backward_kernel(first, *refs):
    sc_ref, w_ref, bias_ref, q_ref, k_ref, v_ref, do_ref, lse_ref = refs[:8]
    refs = refs[8:]
    if not first:
        al_ref, as_ref, at_ref = refs[:3]
        refs = refs[3:]
    kept_ref, sent_ref, dq_ref, dk_ref, dv_ref, dl_ref, ds_ref, dt_ref, scr = refs
    if first:
        dl_ref[...] = jnp.zeros_like(dl_ref)
        ds_ref[...] = jnp.zeros_like(ds_ref)
        dt_ref[...] = jnp.zeros_like(dt_ref)
    else:
        dl_ref[...] = al_ref[...]
        ds_ref[...] = as_ref[...]
        dt_ref[...] = at_ref[...]
    q, k, v = q_ref[0], k_ref[0], v_ref[0]
    do_t = do_ref[0].astype(BF16)
    do = do_ref[0].T.astype(BF16)
    k_t = turned(k)
    d_qt = []
    d_k = jnp.zeros(k.shape, F32)
    d_v = jnp.zeros(k.shape, F32)
    for h in range(k.shape[1] // HD):
        own = head_lanes(k.shape, h)
        s = dot_nt(jnp.where(own, k, jnp.zeros_like(k)), q) + bias_ref[0, h].astype(F32)
        p = jnp.exp(s - lse_ref[0, h : h + 1, :])
        dp = dot(jnp.where(own, v, jnp.zeros_like(v)), do_t)
        inner = jnp.sum(p * dp, axis=0, keepdims=True)
        ds = (p * (dp - inner)).astype(BF16)
        d_v = jnp.where(own, dot(p.astype(BF16), do), d_v)
        d_k = jnp.where(own, dot(ds, q), d_k)
        d_qt.append(dot(k_t[h * HD : (h + 1) * HD], ds))
        scr[:, 0:LONG] = ds.astype(F32)

        @pl.when(sc_ref[1] == 0)
        def _():
            fold_large(scr, h, dl_ref, dt_ref)

        @pl.when(sc_ref[1] == 1)
        def _():
            fold_small(scr, h, ds_ref, dt_ref)

    d_qt = jnp.concatenate(d_qt, axis=0).astype(BF16) * jnp.asarray(HD**-0.5, BF16)
    d_q = d_qt.astype(F32).T.astype(BF16)
    d_k = d_k.astype(BF16)
    d_v = d_v.astype(BF16)
    dn = dot(d_q, w_ref[0]) + dot(d_k, w_ref[1]) + dot(d_v, w_ref[2])
    part_halves(sc_ref[2], dn, kept_ref, sent_ref)
    dq_ref[...] = d_qt
    dk_ref[...] = turned(d_k)
    dv_ref[...] = turned(d_v)


def attend_back(scalars, w_qkv, bias, saved, do, sums):
    width, dim = w_qkv.shape[1:]
    heads = width // HD
    q, k, v, lse = saved
    first = sums is None
    pair = (LONG, dim // 2)
    sum_shapes = [(heads, GRID, WIDE_L), (heads, 16, WIDE_S), (heads, 8, 128)]
    specs = [
        once(whole_spec, (3, width, dim)),
        once(kind_spec, (heads, LONG, LONG)),
        once(first_spec, (LONG, width)),
        once(first_spec, (LONG, width)),
        once(first_spec, (LONG, width)),
        once(first_spec, (width, LONG)),
        once(first_spec, (heads, LONG)),
    ]
    if not first:
        specs += [once(whole_spec, s) for s in sum_shapes]
    return pl.pallas_call(
        partial(backward_kernel, first),
        out_shape=[jax.ShapeDtypeStruct(pair, F32)] * 2
        + [jax.ShapeDtypeStruct((width, LONG), BF16)] * 3
        + [jax.ShapeDtypeStruct(s, F32) for s in sum_shapes],
        grid_spec=pltpu.PrefetchScalarGridSpec(
            num_scalar_prefetch=1,
            grid=(1,),
            in_specs=specs,
            out_specs=[once(whole_spec, pair)] * 2
            + [once(whole_spec, (width, LONG))] * 3
            + [once(whole_spec, s) for s in sum_shapes],
            scratch_shapes=[pltpu.VMEM((LONG, 640), F32)],
        ),
        compiler_params=params(),
        cost_estimate=spent(12.4),
        name="attend_back",
    )(scalars, w_qkv, bias, q, k, v, do, lse, *(sums or ()))


def qkv_kernel(sc_ref, nf, no, qf, kf, vf, qo, ko, vo, pa, pb, *refs):
    db_ref = refs[2]
    blocks = [
        dot(far[...], nf[0]) + dot(own[...], no[0]) for far, own in ((qf, qo), (kf, ko), (vf, vo))
    ]
    blocks.append(pa[...] + pb[...])
    rows = blocks[0].shape[0]
    for i in range(2):
        at = pl.ds(i * rows, rows)
        refs[0][at] = jnp.where(sc_ref[4] == 0, blocks[i], blocks[2 + i])
        refs[1][at] = jnp.where(sc_ref[4] == 0, blocks[2 + i], blocks[i])
    for i, (far, own) in enumerate(((qf, qo), (vf, vo))):
        db_ref[:, i : i + 1] = jnp.sum(far[...].astype(F32), axis=1, keepdims=True) + jnp.sum(
            own[...].astype(F32), axis=1, keepdims=True
        )


def qkv_grad(scalars, n_far, n_own, far, own, proj_a, proj_b):
    dim = n_far.shape[2]
    width = far[0].shape[0]
    return pl.pallas_call(
        qkv_kernel,
        in_specs=[SCALARS] + [PLAIN] * 10,
        out_shape=[jax.ShapeDtypeStruct((2 * width, dim), F32)] * 2
        + [jax.ShapeDtypeStruct((width, 128), F32)],
        compiler_params=params(),
        cost_estimate=spent(4.5),
        name="qkv_grad",
    )(scalars, n_far, n_own, *far, *own, proj_a, proj_b)


def wide_rows(lo_ref, hi_ref):
    return jnp.concatenate([lo_ref[0], hi_ref[0]], axis=1)


def column_sum(x):
    return jnp.sum(x, axis=0, keepdims=True)


def feed_kernel(first, *refs):
    if not first:
        refs = refs[:14] + refs[15:]
    (sc_ref, tok_ref, out_ref, o0, oc, ox, od, wp0, wpc, wpx, wpd) = refs[:11]
    vec, w1, w2 = refs[11:14]
    mid_ref, a_ref, kept_ref, sent_ref, g_ref, n_ref, du_ref, dm_ref, o_scr, w_scr = refs[14:]
    low = lambda r: r.astype(BF16)
    place = sc_ref[3]
    for hop, (part, weight) in enumerate(((o0, wp0), (oc, wpc), (ox, wpx), (od, wpd))):
        at = place ^ hop
        o_scr[at] = low(part[0])
        w_scr[at] = low(weight[...])
    size = o_scr.shape[0] * o_scr.shape[1]
    o_all = o_scr[...].reshape(size, o_scr.shape[2])
    a = dot_tn(o_all, w_scr[...].reshape(size, w_scr.shape[2])) + vec[6:7]
    a_ref[0] = a
    mid = tok_ref[0].astype(F32) + vec[4:5] * a
    mid_ref[0] = mid
    n2 = layer_norm(mid, vec[2:3], vec[3:4])[0].astype(BF16)
    n_ref[0] = n2
    u = dot(n2, w1[...]) + vec[7:8]
    cdf = 0.5 * (1.0 + lax.erf(u * np.float32(np.sqrt(0.5))))
    slope = cdf + u * (jnp.exp(-0.5 * u * u) * np.float32(1 / np.sqrt(2 * np.pi)))
    g_ref[0] = (u * cdf).astype(BF16)
    dm = (vec[5:6] * out_ref[0].astype(F32)).astype(BF16)
    dm_ref[0] = dm
    du = (slope * dot_nt(dm, w2[...])).astype(BF16)
    du_ref[0] = du
    dn = dot_nt(du, w1[...])
    part_halves(sc_ref[2], dn, kept_ref, sent_ref)


def feed(scalars, tok3, out3, o_parts, w_parts, vec, w1, w2, mid=None):
    dim = tok3.shape[2]
    hid = w1.shape[1]
    width = w_parts[0].shape[0]
    pair = jax.ShapeDtypeStruct((LONG, dim // 2), F32)
    row = jax.ShapeDtypeStruct((1, LONG, dim), F32)
    both = jax.ShapeDtypeStruct((2, LONG, dim), F32)
    held = () if mid is None else (mid,)
    low = lambda n: jax.ShapeDtypeStruct((1, LONG, n), BF16)
    specs = (
        [once(pack_spec, (LONG, dim))] * 2
        + [once(first_spec, (width, LONG))] * 4
        + [once(whole_spec, (width, dim))] * 4
        + [
            once(whole_spec, (8, dim)),
            once(whole_spec, (dim, hid)),
            once(whole_spec, (hid, dim)),
        ]
    )
    specs += [pl.BlockSpec(memory_space=pl.ANY)] * len(held)
    return pl.pallas_call(
        partial(feed_kernel, mid is None),
        out_shape=[both, row, pair, pair, low(hid), low(dim), low(hid), low(dim)],
        grid_spec=pltpu.PrefetchScalarGridSpec(
            num_scalar_prefetch=1,
            grid=(1,),
            in_specs=specs,
            out_specs=[once(pack_spec, (LONG, dim)), once(first_spec, (LONG, dim))]
            + [once(whole_spec, pair.shape)] * 2
            + [once(first_spec, (LONG, n)) for n in (hid, dim, hid, dim)],
            scratch_shapes=[
                pltpu.VMEM((4, width, LONG), BF16),
                pltpu.VMEM((4, width, dim), BF16),
            ],
        ),
        compiler_params=params(),
        input_output_aliases={14: 0} if held else {},
        cost_estimate=spent(10),
        name="feed",
    )(scalars, tok3, out3, *o_parts, *w_parts, vec, w1, w2, *held)


SCALARS = pl.BlockSpec(memory_space=pltpu.SMEM)
PLAIN = pl.BlockSpec(memory_space=pltpu.VMEM)


def out_kernel(sc_ref, up, g, w2, kept_ref, sent_ref, sum_ref):
    m = dot(g[0], w2[...])
    part_halves(sc_ref[2], m, kept_ref, sent_ref)
    e = up[0].astype(F32)
    sum_ref[0:1] = column_sum(e * m)
    sum_ref[1:2] = column_sum(e)


def feed_out(scalars, up3, g, w2):
    hid, dim = w2.shape
    return pl.pallas_call(
        out_kernel,
        out_shape=[jax.ShapeDtypeStruct(n, F32) for n in [(LONG, dim // 2)] * 2 + [(2, dim)]],
        grid_spec=pltpu.PrefetchScalarGridSpec(
            num_scalar_prefetch=1,
            grid=(1,),
            in_specs=[
                once(pack_spec, (LONG, dim)),
                once(first_spec, (LONG, hid)),
                once(whole_spec, (hid, dim)),
            ],
            out_specs=[once(whole_spec, (LONG, dim // 2))] * 2 + [once(whole_spec, (2, dim))],
        ),
        compiler_params=params(),
        cost_estimate=spent(3.5),
        name="feed_out",
    )(scalars, up3, g, w2)


def part_blocks(bit, blocks, refs):
    for i in range(len(blocks) // 2):
        refs[2 * i][...] = jnp.where(bit == 0, blocks[2 * i], blocks[2 * i + 1])
        refs[2 * i + 1][...] = jnp.where(bit == 0, blocks[2 * i + 1], blocks[2 * i])


def feed_grad_kernel(sc_ref, up, gf, nf, uf, mf, go, no, uo, mo, w2, *refs):
    db1_ref, db2_ref = refs[4:6]
    d1 = dot_tn(nf[0], uf[0]) + dot_tn(no[0], uo[0])
    rows = d1.shape[0] // 2
    part_blocks(sc_ref[4], (d1[:rows], d1[rows:]), refs[:2])
    d2 = dot_tn(gf[0], mf[0]) + dot_tn(go[0], mo[0])
    part_blocks(sc_ref[5], (d2[:rows], d2[rows:]), refs[2:4])
    db1_ref[...] = column_sum(uf[0].astype(F32)) + column_sum(uo[0].astype(F32))
    db2_ref[...] = column_sum(mf[0].astype(F32)) + column_sum(mo[0].astype(F32))
    out_kernel(sc_ref, up, go, w2, *refs[6:])


def feed_grad(scalars, up3, far, own, w2):
    hid, dim = w2.shape
    shapes = [(dim // 2, hid)] * 2 + [(hid // 2, dim)] * 2 + [(1, hid), (1, dim)]
    shapes += [(LONG, dim // 2)] * 2 + [(2, dim)]
    kept = [once(first_spec, (LONG, n)) for n in (hid, dim, hid, dim)]
    return pl.pallas_call(
        feed_grad_kernel,
        out_shape=[jax.ShapeDtypeStruct(n, F32) for n in shapes],
        grid_spec=pltpu.PrefetchScalarGridSpec(
            num_scalar_prefetch=1,
            grid=(1,),
            in_specs=[once(pack_spec, (LONG, dim))]
            + kept * 2
            + [once(whole_spec, (hid, dim))],
            out_specs=[once(whole_spec, n) for n in shapes],
        ),
        compiler_params=params(),
        cost_estimate=spent(9.5),
        name="feed_grad",
    )(scalars, up3, *far, *own, w2)


def norm_back(upstream, unit_rows, inverse, gain_row):
    scaled = upstream * gain_row
    centred = scaled - jnp.mean(scaled, axis=-1, keepdims=True)
    centred = centred - unit_rows * jnp.mean(scaled * unit_rows, axis=-1, keepdims=True)
    return inverse * centred, column_sum(upstream * unit_rows), column_sum(upstream)


def joined(sc_ref, mine, peer):
    core = sc_ref[2]
    lo = jnp.where(core == 0, mine[...], peer[...])
    hi = jnp.where(core == 0, peer[...], mine[...])
    return jnp.concatenate([lo, hi], axis=1)


def middle_kernel(
    sc_ref, out_ref, mid_ref, a_ref, mine, peer, vec, wp0, wpx, o0, ox,
    dmid_ref, do0_ref, dox_ref, dp0_ref, dpx_ref, sum_ref
):
    dn2 = joined(sc_ref, mine, peer)
    _, unit, inverse = layer_norm(mid_ref[0], vec[2:3], vec[3:4])
    back, d_gain, d_shift = norm_back(dn2, unit, inverse, vec[2:3])
    dmid = out_ref[0].astype(F32) + back
    dmid_ref[0] = dmid
    da = (vec[4:5] * dmid).astype(BF16)
    do0_ref[0] = dot_nt(wp0[...], da).astype(BF16).astype(F32)
    dox_ref[0] = dot_nt(wpx[...].astype(BF16), da).astype(BF16).astype(F32)
    dp0_ref[...] = dot(o0[0].astype(BF16), da)
    dpx_ref[...] = dot(ox[0].astype(BF16), da)
    sum_ref[0:1] = d_gain
    sum_ref[1:2] = d_shift
    sum_ref[2:3] = column_sum(dmid * a_ref[0])
    sum_ref[3:4] = column_sum(da.astype(F32))


def middle_back(scalars, out3, mid, a, mine, peer, vec, w_parts, o_parts):
    dim = mid.shape[2]
    width = w_parts[0].shape[0]
    row = jax.ShapeDtypeStruct((1, LONG, dim), F32)
    low = jax.ShapeDtypeStruct((1, width, LONG), F32)
    mat = jax.ShapeDtypeStruct((width, dim), F32)
    return pl.pallas_call(
        middle_kernel,
        out_shape=[row, low, low, mat, mat, jax.ShapeDtypeStruct((4, dim), F32)],
        grid_spec=pltpu.PrefetchScalarGridSpec(
            num_scalar_prefetch=1,
            grid=(1,),
            in_specs=[
                once(pack_spec, (LONG, dim)),
                once(pack_spec, (LONG, dim)),
                once(first_spec, (LONG, dim)),
                once(whole_spec, (LONG, dim // 2)),
                once(whole_spec, (LONG, dim // 2)),
                once(whole_spec, (8, dim)),
                once(whole_spec, (width, dim)),
                once(whole_spec, (width, dim)),
                once(first_spec, (width, LONG)),
                once(first_spec, (width, LONG)),
            ],
            out_specs=[
                once(first_spec, (LONG, dim)),
                once(first_spec, (width, LONG)),
                once(first_spec, (width, LONG)),
                once(whole_spec, (width, dim)),
                once(whole_spec, (width, dim)),
                once(whole_spec, (4, dim)),
            ],
        ),
        compiler_params=params(),
        cost_estimate=spent(7.7),
        name="middle_back",
    )(scalars, out3, mid, a, mine, peer, vec, *w_parts[::2], *o_parts[::2])


def final_kernel(sc_ref, tok_ref, dmid_ref, mine, peer, vec, two, scale, out_ref, sent_ref, sum_ref):
    dn1 = joined(sc_ref, mine, peer)
    _, unit, inverse = layer_norm(tok_ref[0].astype(F32), vec[0:1], vec[1:2])
    back, d_gain, d_shift = norm_back(dn1, unit, inverse, vec[0:1])
    result = dmid_ref[0] + back
    out_ref[0] = result
    half = result.shape[1] // 2
    rows = jnp.concatenate([two[...], d_gain, d_shift, scale[...]], axis=0)
    sum_ref[...] = rows
    sent_ref[0:LONG] = jnp.where(sc_ref[2] == 0, result[:, :half], result[:, half:])
    sent_ref[LONG : LONG + 8] = rows[:, :half]
    sent_ref[LONG + 8 : LONG + 16] = rows[:, half:]


def final_back(scalars, tok3, dmid, mine, peer, vec, two, scale):
    dim = tok3.shape[2]
    return pl.pallas_call(
        final_kernel,
        out_shape=[
            jax.ShapeDtypeStruct((1, LONG, dim), F32),
            jax.ShapeDtypeStruct((LONG + 16, dim // 2), F32),
            jax.ShapeDtypeStruct((8, dim), F32),
        ],
        grid_spec=pltpu.PrefetchScalarGridSpec(
            num_scalar_prefetch=1,
            grid=(1,),
            in_specs=[
                once(pack_spec, (LONG, dim)),
                once(first_spec, (LONG, dim)),
                once(whole_spec, (LONG, dim // 2)),
                once(whole_spec, (LONG, dim // 2)),
                once(whole_spec, (8, dim)),
                once(whole_spec, (4, dim)),
                once(whole_spec, (2, dim)),
            ],
            out_specs=[
                once(first_spec, (LONG, dim)),
                once(whole_spec, (LONG + 16, dim // 2)),
                once(whole_spec, (8, dim)),
            ],
        ),
        compiler_params=params(),
        cost_estimate=spent(5.6),
        name="final_back",
    )(scalars, tok3, dmid, mine, peer, vec, two, scale)


def last_kernel(sc_ref, kept, got, flat_ref, b2, _, qkv_ref, proj_ref, *refs):
    gains, shifts, scales, singles, bias, table = refs
    rows = kept.shape[0]
    width = rows // 2
    swap = sc_ref[4] == 0
    for i, lo in enumerate((0, width)):
        a = kept[lo : lo + width]
        b = got[lo : lo + width]
        qkv_ref[i] = jnp.where(swap, a, b)
        other = jnp.where(swap, b, a)
        if i == 0:
            qkv_ref[2] = other
        else:
            proj_ref[...] = other
    flat = flat_ref[...]
    gains[0:1] = flat[4:5]
    gains[1:2] = flat[0:1]
    shifts[0:1] = flat[5:6]
    shifts[1:2] = flat[1:2]
    scales[0:1] = flat[2:3]
    scales[1:2] = flat[6:7] + b2[...].astype(F32) * flat[10:11]
    singles[0:1] = flat[3:4]
    singles[1:3] = flat[8:10]
    count = table.shape[1]
    for h in range(table.shape[0]):
        for i in range(3):
            row = flat[11 + 3 * h + i : 12 + 3 * h + i]
            lo = i * flat.shape[1]
            hi = min(lo + flat.shape[1], count)
            table[h : h + 1, lo:hi] = row[:, : hi - lo]
    row = flat[11 + 3 * table.shape[0] : 12 + 3 * table.shape[0]]
    bias[0:1] = row[:, :width]
    bias[1:2] = row[:, width : 2 * width]


def last_parts(scalars, kept, got, flat, b2, after, heads, count):
    rows, dim = kept.shape
    width = rows // 2
    shapes = [(3, width, dim), (width, dim)] + [(2, dim)] * 3 + [(3, dim), (2, width), (heads, count)]
    return pl.pallas_call(
        last_kernel,
        in_specs=[SCALARS] + [PLAIN] * 4 + [pl.BlockSpec(memory_space=pl.ANY)],
        out_shape=[jax.ShapeDtypeStruct(n, F32) for n in shapes],
        compiler_params=params(),
        cost_estimate=spent(3),
        name="last_parts",
    )(scalars, kept, got, flat, b2, after)


CORE = [(i, i ^ 1) for i in range(4)]
ACROSS = [(i, i ^ 2) for i in range(4)]


def to_core(x):
    return lax.ppermute(x, "narrow", CORE)


def to_chip(x):
    return lax.ppermute(x, "narrow", ACROSS)


def pick(pair, index):
    return lax.dynamic_index_in_dim(pair, index, 0, keepdims=False)


def small_sum(x, size):
    step = 1
    while step < size:
        x = x + lax.ppermute(x, "wide", [(i, i ^ step) for i in range(size)])
        step *= 2
    return x


def tie(*values):
    return lax.optimization_barrier(values)


def in_order(bit, first, second):
    return jnp.where(bit == 0, first, second), jnp.where(bit == 0, second, first)


WIDE_PLACES = 8
DUE = {
    "one": (1, 2, 3, 5, 8),
    "two": (1, 3, 5, 9, 13),
    "last": (4, 6, 9, 11, 14),
    "flat": (9, 11, 14),
}


class Wave:
    def __init__(self, place):
        self.place = place
        self.live = {}
        self.done = {}

    def bit(self, step):
        return (self.place >> (step.bit_length() - 1)) & 1

    def send(self, value, step):
        return lax.ppermute(value, "wide", [(i, i ^ step) for i in range(WIDE_PLACES)])

    def add(self, name, kept, sent, steps, due, whole=False):
        got = self.send(sent, steps[0])
        self.live[name] = dict(steps=steps, stage=0, kept=kept, got=got, due=list(due), whole=whole)

    def advance(self, c, got):
        stage, kept, (first, second, third) = c["stage"], c["kept"], c["steps"]
        if c["whole"]:
            total = kept + got
            return (total, total, (first, second, third)[stage + 1]) if stage < 2 else (total, None, None)
        if stage == 0:
            rows = kept.shape[0] // 2
            split = lambda v: v.reshape((2, rows) + v.shape[1:])
            side = self.bit(second)
            kept, got = split(kept), split(got)
            send = pick(kept, 1 - side) + pick(got, 1 - side)
            return pick(kept, side) + pick(got, side), send, second
        if stage < 3:
            total = kept + got
        elif stage == 3:
            total = jnp.concatenate(in_order(self.bit(second), kept, got))
        else:
            return (kept, got), None, None
        return total, total, (third, second, first)[stage - 1]

    def event(self, now, then):
        ripe = [n for n, c in self.live.items() if c["due"][0] <= now]
        if not ripe:
            return then
        then, *values = tie(then, *[self.live[n]["got"] for n in ripe])
        moves = {n: self.advance(self.live[n], got) for n, got in zip(ripe, values)}
        for n in ripe:
            if moves[n][1] is None:
                self.done[n] = moves[n][0]
                del self.live[n], moves[n]
        if not moves:
            return then
        held = tie(then, *[m[1] for m in moves.values()])
        for (n, (kept, _, step)), value in zip(moves.items(), held[1:]):
            c = self.live[n]
            c["kept"] = kept
            c["got"] = self.send(value, step)
            c["stage"] += 1
            c["due"].pop(0)
        return held[0]


def on_device(
    tokens, w_qkv, qv_bias, w_proj, proj_bias, w_fc1, fc1_bias, w_fc2, fc2_bias, norm_gains,
    norm_shifts, layer_scales, rel_table, image_ids, pad_mask, grid_rows, grid_cols, d_out, wide
):
    rows, dim = tokens.shape
    width = w_qkv.shape[2]
    place = lax.axis_index("narrow")
    chip, core = place >> 1, place & 1
    spot = lax.axis_index("wide")
    tok3 = tokens.reshape(2, LONG, dim)
    out3 = d_out.reshape(2, LONG, dim)
    w_turned = w_qkv.transpose(0, 2, 1)
    kind_a = image_ids[LONG - 1] & 1
    kind_b = image_ids[2 * LONG - 1] & 1
    common = (core, place, spot & 1, (spot >> 1) & 1)
    sc_far = jnp.stack([1 - chip, jnp.where(chip == 0, kind_b, kind_a), *common])
    sc_own = jnp.stack([chip, jnp.where(chip == 0, kind_a, kind_b), *common])
    pairs = zip(norm_gains.astype(F32), norm_shifts.astype(F32))
    vec = jnp.stack(
        [v for pair in pairs for v in pair]
        + list(layer_scales.astype(F32))
        + [proj_bias.astype(F32), fc1_bias.astype(F32)]
    )

    wp_near = w_proj.astype(F32)
    wp_far = to_chip(wp_near)
    bias = make_bias(rel_table)
    first = lambda sc: attend(sc, tok3, w_turned, qv_bias, vec, bias)
    o_far, *saved_far, n_far = first(sc_far)
    wp_far, o_sent = tie(wp_far, o_far)
    x_own = to_chip(o_sent)
    w_parts = (w_proj, to_core(wp_near), wp_far, to_core(wp_far))
    o_own, *saved_own, n_own = first(sc_own)
    x_own, o_sent = tie(x_own, o_own)
    x_far = to_chip(o_sent)
    far_parts = (o_far, to_core(o_far), x_far, to_core(x_far))
    own_parts = (o_own, to_core(o_own), x_own, to_core(x_own))

    shared = (w_parts, vec, w_fc1, w_fc2)
    mid, _, dn_kept, dn_send, *kept_far = feed(sc_far, tok3, out3, far_parts, *shared)
    peer = to_core(dn_send)
    sc, _ = tie(sc_far, dn_send)
    m_far_kept, m_far_send, scale_far = feed_out(sc, out3, kept_far[0], w_fc2)
    peer, scale_far = tie(peer, scale_far)
    half, sc = tie(dn_kept + peer, sc_own)
    dn_got = to_chip(half)
    mid, a_own, dn_kept, dn_send, *kept_own = feed(sc, tok3, out3, own_parts, *shared, mid)
    peer = to_core(dn_send)
    *blocks, d_fc1_bias, d_fc2_bias, m_own_kept, m_own_send, scale_own = feed_grad(
        sc_own, out3, kept_far, kept_own, w_fc2
    )

    wave = Wave(spot)
    custom = wide == WIDE_PLACES
    if custom:
        wave.add("one", blocks[0], blocks[1], (1, 2, 4), DUE["one"])
        wave.add("two", blocks[2], blocks[3], (2, 1, 4), DUE["two"])
    dn_got, scale_own = tie(dn_got, scale_own)
    part, peer = tie(dn_kept + dn_got, peer)
    mine = part + peer
    theirs = to_core(mine)
    dmid, do_own, do_send, dp_own, dp_send, sums_two = middle_back(
        sc_own, out3, mid, a_own, mine, theirs, vec, w_parts, own_parts
    )
    do_far = to_chip(do_send)
    m_far_peer, m_own_peer, _ = tie(to_core(m_far_send), to_core(m_own_send), dmid)
    m_half_far = m_far_kept + m_far_peer
    m_half_own = m_own_kept + m_own_peer
    scale = scale_far + scale_own
    up_sum = scale[1:2]
    scale, _ = tie(scale, dmid)
    scale = scale + to_core(scale)
    do_far, m_half_far, m_half_own, scale = tie(do_far, m_half_far, m_half_own, scale)
    do_far, sc = tie(do_far, sc_far)
    sc = wave.event(1, sc)
    dp_send, sc = tie(dp_send, sc)
    dp_got = to_chip(dp_send)

    dn_kept, dn_send, *far, dl, ds, dt = attend_back(sc, w_turned, bias, saved_far, do_far, None)
    dn_send, dp_got = tie(dn_send, dp_got)
    dn_send = wave.event(2, dn_send)
    peer = to_core(dn_send)
    half, sc, dp_got = tie(dn_kept + peer, sc_own, dp_got)
    dn_got = to_chip(half)
    dn_kept, dn_send, *own, dl, ds, dt = attend_back(
        sc, w_turned, bias, saved_own, do_own, (dl, ds, dt)
    )
    *pieces, d_qv_bias = qkv_grad(sc_own, n_far, n_own, far, own, dp_own, dp_got)
    dn_got, d_qv_bias, dn_send = tie(dn_got, d_qv_bias, dn_send)
    dn_send = wave.event(3, dn_send)
    peer = to_core(dn_send)
    if custom:
        wave.add("last", pieces[0], pieces[1], (1, 2, 4), DUE["last"])
    part, peer = tie(dn_kept + dn_got, peer)
    mine = part + peer
    theirs = to_core(mine)
    tok_own, tok_send, own_rows = final_back(
        sc_own, tok3, dmid, mine, theirs, vec, sums_two, scale
    )
    tok_got = to_chip(tok_send)
    dl, ds, dt, own_rows = tie(dl, ds, dt, own_rows)
    table_back = strips_back(dl, ds, dt)
    heads, count = table_back.shape
    row_bias = jnp.pad(d_qv_bias[:, :2].T.reshape(1, -1), ((0, 0), (0, dim - 2 * width)))
    rest = jnp.pad(table_back, ((0, 0), (0, 3 * dim - count))).reshape(3 * heads, dim)
    rest = [d_fc2_bias, d_fc1_bias, up_sum, rest, row_bias, jnp.zeros((12 - 3 * heads, dim), F32)]
    rest = jnp.concatenate(rest)
    rest, own_rows = tie(rest, own_rows)
    mark = wave.event(4, own_rows)
    mark = wave.event(5, mark)
    tok_got, mark = tie(tok_got, mark)
    tok_peer = to_core(tok_got)
    m_send, mark = tie(m_half_far, mark)
    m_all_own = to_chip(m_send)
    mark = wave.event(6, mark)
    own_rows = mark + jnp.concatenate([tok_got[LONG : LONG + 8], tok_got[LONG + 8 :]], axis=1)
    flat = jnp.concatenate([own_rows, rest])
    mark = flat
    if custom:
        wave.add("flat", mark, mark, (4, 2, 1), DUE["flat"], True)
    tok_peer, mark = tie(tok_peer, mark)
    tok_far = jnp.concatenate(in_order(core, tok_got[:LONG], tok_peer[:LONG]), axis=1)[None]
    d_tokens = jnp.concatenate(in_order(chip, tok_own, tok_far)).reshape(rows, dim)
    d_tokens, mark = tie(d_tokens, mark)
    m_all_own, mark = tie(m_all_own, mark)
    m_all_own = m_half_own + m_all_own
    m_own_peer = to_core(m_all_own)
    m_send, m_all_own = tie(m_half_own, m_all_own)
    m_all_far = to_chip(m_send)
    mark = wave.event(8, mark)
    if custom:
        d_fc1 = jnp.concatenate(in_order(spot & 1, *wave.done["one"]))
        d_fc1, mark = tie(d_fc1, mark)
    mark = wave.event(9, mark)
    m_all_far, mark = tie(m_all_far, mark)
    m_all_far = m_half_far + m_all_far
    m_far_peer = to_core(m_all_far)
    mark = wave.event(11, mark)
    m_own_peer, m_far_peer, mark = tie(m_own_peer, m_far_peer, mark)
    m_own = jnp.concatenate(in_order(core, m_all_own, m_own_peer), axis=1)[None]
    m_far = jnp.concatenate(in_order(core, m_all_far, m_far_peer), axis=1)[None]
    m_full = jnp.concatenate(in_order(chip, m_own, m_far)) + fc2_bias.astype(F32)
    block_out = (mid + layer_scales[1].astype(F32) * m_full).astype(BF16).reshape(rows, dim)
    block_out, mark = tie(block_out, mark)
    mark = wave.event(13, mark)
    if custom:
        d_fc2 = jnp.concatenate(in_order((spot >> 1) & 1, *wave.done["two"]))
        d_fc2, mark = tie(d_fc2, mark)
    mark = wave.event(14, mark)
    if custom:
        got = wave.done
        kept, last = got["last"]
        flat = got["flat"]
    else:
        low, high = spot & 1, (spot >> 1) & 1
        d_fc1 = jnp.concatenate(in_order(low, blocks[0], blocks[1]))
        d_fc2 = jnp.concatenate(in_order(high, blocks[2], blocks[3]))
        pieces = in_order(low, *pieces)
        pieces, d_fc1, d_fc2 = lax.psum((pieces, d_fc1, d_fc2), "wide")
        kept, last = in_order(low, *pieces)
        flat = small_sum(flat, wide)
    d_qkv, d_proj, d_norm_gains, d_norm_shifts, d_layer_scales, singles, d_qv_bias, d_table = last_parts(
        sc_own, kept, last, flat, fc2_bias[None], mark, heads, count
    )
    d_proj_bias, d_fc2_bias, d_fc1_bias = singles
    d_qkv = d_qkv.transpose(0, 2, 1)
    return (
        block_out,
        d_tokens,
        d_qkv,
        d_qv_bias,
        d_proj,
        d_proj_bias,
        d_fc1,
        d_fc1_bias,
        d_fc2,
        d_fc2_bias,
        d_norm_gains,
        d_norm_shifts,
        d_layer_scales,
        d_table,
    )


def solution(mesh):
    in_specs = (
        P("wide", None),
        P(None, None, "narrow"),
        P(None, "narrow"),
        P("narrow", None),
        P(),
        P(None, "narrow"),
        P("narrow"),
        P("narrow", None),
        P(),
        P(),
        P(),
        P(),
        P("narrow", None),
        P("wide"),
        P("wide"),
        P("wide"),
        P("wide"),
        P("wide", None),
    )
    out_specs = (
        P("wide", None),
        P("wide", None),
        P(None, None, "narrow"),
        P(None, "narrow"),
        P("narrow", None),
        P(),
        P(None, "narrow"),
        P("narrow"),
        P("narrow", None),
        P(),
        P(),
        P(),
        P(),
        P("narrow", None),
    )
    return jax.shard_map(
        partial(on_device, wide=mesh.shape["wide"]),
        mesh=mesh,
        in_specs=in_specs,
        out_specs=out_specs,
        check_vma=False,
    )
```

```python
from functools import partial

import jax
import jax.numpy as jnp
import numpy as np
from jax import lax
from jax.experimental import pallas as pl
from jax.experimental.pallas import tpu as pltpu
from jax.sharding import PartitionSpec as P

HD = 64
GRID = 24
SMALL = 14
SHORT = 208
LONG = 584
EPSILON = 1e-06
SIDE = 2 * GRID - 1
WIDE_L = 1280
WIDE_S = 640
NEG = -1e30
F32 = jnp.float32
BF16 = jnp.bfloat16
VMEM_LIMIT = 56 << 20
COST_SCALE = 1.2e8


def params(**kw):
    return pltpu.CompilerParams(vmem_limit_bytes=VMEM_LIMIT, **kw)


def spent(microseconds):
    work = int(microseconds * COST_SCALE)
    return pl.CostEstimate(flops=work, transcendentals=0, bytes_accessed=1024)


def dot(a, b):
    return jnp.dot(a, b, preferred_element_type=F32)


def dot_nt(a, b):
    return lax.dot_general(a, b, (((1,), (1,)), ((), ())), preferred_element_type=F32)


def dot_tn(a, b):
    return lax.dot_general(a, b, (((0,), (0,)), ((), ())), preferred_element_type=F32)


def large_pick():
    pick = np.zeros((2, SIDE, GRID, GRID), np.float32)
    for s in range(GRID):
        for c in range(GRID):
            if s == 0:
                pick[1, c, s, c] = 1
            else:
                pick[0, c + GRID - s, s, c] = 1
    return pick.reshape(2 * SIDE, GRID * GRID)


def small_pick():
    pick = np.zeros((SIDE, 16, SMALL), np.float32)
    for s in range(SMALL):
        for c in range(SMALL):
            pick[c - s + GRID - 1, s, c] = 1
    return pick.reshape(SIDE, 16 * SMALL)


def strips_back(d_large, d_small, d_tails):
    heads = d_large.shape[0]
    rows = 2 * SMALL - 1
    hi = lax.Precision.HIGHEST
    large = d_large[:, :, 1 : 1 + (SIDE + 1) * GRID].reshape(heads, GRID, SIDE + 1, GRID)
    both = jnp.einsum(
        "hsuc,ksc->huk",
        large,
        jnp.asarray(large_pick().reshape(2 * SIDE, GRID, GRID)),
        precision=hi,
    )
    grid_grad = both[:, 1:, :SIDE] + both[:, :SIDE, SIDE:]
    small = d_small[:, :, 1 : 1 + rows * SMALL].reshape(heads, 16, rows, SMALL)
    part = jnp.einsum(
        "hsuc,ksc->huk", small, jnp.asarray(small_pick().reshape(SIDE, 16, SMALL)), precision=hi
    )
    low = GRID - SMALL
    grid_grad = grid_grad + jnp.pad(part, ((0, 0), (low, SIDE - low - rows), (0, 0)))
    return jnp.concatenate(
        [grid_grad.reshape(heads, SIDE * SIDE), d_tails[:, 0, :3]], axis=1
    )


def tail_fix(block, t0, t1, t2, last, real):
    shape = block.shape
    row = lax.broadcasted_iota(jnp.int32, shape, 0)
    lane = lax.broadcasted_iota(jnp.int32, shape, 1)
    block = jnp.where(lane > last, block[:, 1:2], block)
    block = jnp.where(lane == 0, t0, block)
    block = jnp.where(row == 0, jnp.where(lane == 0, t2, t1), block)
    return jnp.where(row >= real, NEG, block)


def windows(table, grid, first, width):
    shape = (table.shape[0], width)
    row = lax.broadcasted_iota(jnp.int32, shape, 0) - first
    lane = lax.broadcasted_iota(jnp.int32, shape, 1)
    inside = (lane >= grid * row) & (lane < grid * row + grid)
    spread = dot_tn(table, inside.astype(F32).astype(BF16))
    start = jnp.sum(jnp.where(inside, grid * row, 0), axis=0, keepdims=True)
    return spread, lane[0:1] - start


def bias_kernel(tail_ref, table_ref, out_ref, scr, large_ref, small_ref, rows):
    large_ref[...] = jnp.zeros_like(large_ref)
    small_ref[...] = jnp.zeros_like(small_ref)
    rows[...] = jnp.zeros_like(rows)
    for h in range(table_ref.shape[0]):
        table = table_ref[h].astype(BF16)
        spread, within = windows(table, GRID, 0, (SIDE + 1) * GRID)
        rows[8:56, :] = spread
        strip = jnp.zeros((GRID, (SIDE + 1) * GRID), F32)
        top = jnp.zeros((1, (SIDE + 1) * GRID), F32)
        for c in range(GRID):
            here = within == c
            strip = jnp.where(here, rows[30 - c : 54 - c, :], strip)
            top = jnp.where(here, rows[54 - c : 55 - c, :], top)
        large_ref[h, :, 1 + GRID : 1 + GRID + SIDE * GRID] = strip[:, : SIDE * GRID]
        large_ref[h, 0:1, :] = jnp.zeros((1, WIDE_L), F32)
        large_ref[h, 0:1, 1 : 1 + SIDE * GRID] = top[:, : SIDE * GRID]
        spread, within = windows(table, SMALL, GRID - SMALL, 384)
        rows[8:56, 0:384] = spread
        strip = jnp.zeros((16, 384), F32)
        for c in range(SMALL):
            strip = jnp.where(within == c, rows[31 - c : 47 - c, 0:384], strip)
        count = (2 * SMALL - 1) * SMALL
        small_ref[h, :, 1 : 1 + count] = strip[:, :count]
        t0, t1, t2 = tail_ref[h, 0], tail_ref[h, 1], tail_ref[h, 2]
        for r in range(GRID + 1):
            size = GRID if r < GRID else LONG - GRID * GRID
            off = (GRID - r) * GRID
            scr[r * GRID : r * GRID + size, 0:LONG] = large_ref[h, 0:size, off : off + LONG]
        last = GRID * GRID
        out_ref[0, h] = tail_fix(scr[:, 0:LONG], t0, t1, t2, last, last + 1).astype(BF16)
        last = SMALL * SMALL
        for r in range(SMALL):
            off = (SMALL - 1 - r) * SMALL
            wide = LONG - SHORT
            scr[1 + r * SMALL : 1 + (r + 1) * SMALL, 0:wide] = small_ref[
                h, 0:SMALL, off : off + wide
            ]
        block = tail_fix(scr[0:SHORT, 0 : LONG - SHORT], t0, t1, t2, last, last + 1)
        scr[...] = jnp.full(scr.shape, NEG, F32)
        scr[0:SHORT, 0:SHORT] = block[:, 0:SHORT]
        scr[SHORT : 2 * SHORT, SHORT:LONG] = block
        out_ref[1, h] = scr[:, 0:LONG].astype(BF16)


def make_bias(rel_table):
    heads = rel_table.shape[0]
    tails = rel_table[:, SIDE * SIDE :].astype(F32)
    table = rel_table[:, : SIDE * SIDE].reshape(heads, SIDE, SIDE)[:, :, ::-1]
    table = jnp.pad(table.astype(F32), ((0, 0), (0, 1), (0, 1)))
    return pl.pallas_call(
        bias_kernel,
        out_shape=jax.ShapeDtypeStruct((2, heads, LONG, LONG), BF16),
        in_specs=[
            pl.BlockSpec(memory_space=pltpu.SMEM),
            pl.BlockSpec(memory_space=pltpu.VMEM),
        ],
        out_specs=pl.BlockSpec(memory_space=pltpu.VMEM),
        scratch_shapes=[
            pltpu.VMEM((LONG, 640), F32),
            pltpu.VMEM((heads, GRID, WIDE_L), F32),
            pltpu.VMEM((heads, 16, WIDE_S), F32),
            pltpu.VMEM((64, (SIDE + 1) * GRID), F32),
        ],
        compiler_params=params(),
        cost_estimate=spent(6),
        name="bias",
    )(tails, table)


def layer_norm(values, gain_row, shift_row):
    row_mean = jnp.mean(values, axis=-1, keepdims=True)
    centred = values - row_mean
    inverse = lax.rsqrt(jnp.mean(centred * centred, axis=-1, keepdims=True) + EPSILON)
    unit_rows = centred * inverse
    return unit_rows * gain_row + shift_row, unit_rows, inverse


def part_halves(core, value, kept_ref, sent_ref):
    half = value.shape[1] // 2
    lo, hi = value[:, :half], value[:, half:]
    kept_ref[...] = jnp.where(core == 0, lo, hi)
    sent_ref[...] = jnp.where(core == 0, hi, lo)


def head_lanes(shape, h):
    lane = lax.broadcasted_iota(jnp.int32, shape, 1)
    return (lane >= h * HD) & (lane < (h + 1) * HD)


def turned(block):
    return block.astype(F32).T.astype(BF16)


def forward_kernel(
    sc_ref, tok_ref, w_ref, qv_ref, vec, bias_ref, o_ref, q_ref, k_ref, v_ref, lse_ref, n_ref
):
    x = tok_ref[0].astype(F32)
    n1 = layer_norm(x, vec[0:1], vec[1:2])[0].astype(BF16)
    qv = qv_ref[...].astype(F32)
    q = ((dot_nt(n1, w_ref[0]) + qv[0:1]) * HD**-0.5).astype(BF16)
    k = dot_nt(n1, w_ref[1]).astype(BF16)
    v = (dot_nt(n1, w_ref[2]) + qv[1:2]).astype(BF16)
    q_ref[0] = q
    k_ref[0] = k
    v_ref[0] = v
    n_ref[0] = n1
    v_t = turned(v)
    outs = []
    for h in range(k.shape[1] // HD):
        k_h = jnp.where(head_lanes(k.shape, h), k, jnp.zeros_like(k))
        s = dot_nt(k_h, q) + bias_ref[0, h].astype(F32)
        top = jnp.max(s, axis=0, keepdims=True)
        e = jnp.exp(s - top)
        total = jnp.sum(e, axis=0, keepdims=True)
        p = (e * (1.0 / total)).astype(BF16)
        outs.append(dot(v_t[h * HD : (h + 1) * HD], p))
        lse_ref[0, h : h + 1, :] = top + jnp.log(total)
    o_ref[0] = jnp.concatenate(outs, axis=0).astype(BF16).astype(F32)


def once(spec_of, shape):
    spec = spec_of(shape)
    return pl.BlockSpec(spec.block_shape, spec.index_map, pipeline_mode=pl.Buffered(1))


def pack_spec(shape):
    return pl.BlockSpec((1,) + shape, lambda i, sc: (sc[0],) + (0,) * len(shape))


def first_spec(shape):
    return pl.BlockSpec((1,) + shape, lambda i, sc: (0,) * (1 + len(shape)))


def whole_spec(shape):
    return pl.BlockSpec(shape, lambda i, sc: (0,) * len(shape))


def kind_spec(shape):
    return pl.BlockSpec((1,) + shape, lambda i, sc: (sc[1],) + (0,) * len(shape))


def attend(scalars, tok3, w_qkv, qv_bias, vec, bias):
    width = w_qkv.shape[1]
    heads = width // HD
    dim = tok3.shape[2]
    low = jax.ShapeDtypeStruct((1, LONG, width), BF16)
    return pl.pallas_call(
        forward_kernel,
        out_shape=[
            jax.ShapeDtypeStruct((1, width, LONG), F32),
            low,
            low,
            low,
            jax.ShapeDtypeStruct((1, heads, LONG), F32),
            jax.ShapeDtypeStruct((1, LONG, dim), BF16),
        ],
        grid_spec=pltpu.PrefetchScalarGridSpec(
            num_scalar_prefetch=1,
            grid=(1,),
            in_specs=[
                pack_spec((LONG, dim)),
                whole_spec((3, width, dim)),
                whole_spec((2, width)),
                whole_spec((8, dim)),
                kind_spec((heads, LONG, LONG)),
            ],
            out_specs=[first_spec((width, LONG))]
            + [first_spec((LONG, width))] * 3
            + [first_spec((heads, LONG)), first_spec((LONG, dim))],
        ),
        compiler_params=params(),
        cost_estimate=spent(7.4),
        name="attend",
    )(scalars, tok3, w_qkv, qv_bias, vec, bias)


def fold_large(ds, h, dl_ref, dt_ref):
    last = GRID * GRID
    full = ds[:, 0:LONG]
    lane = lax.broadcasted_iota(jnp.int32, full.shape, 1)
    row = lax.broadcasted_iota(jnp.int32, full.shape, 0)
    pad = jnp.sum(jnp.where(lane > last, full, 0.0), axis=1, keepdims=True)
    body = row > 0
    t0 = jnp.sum(jnp.where((lane == 0) & body, full, 0.0))
    t1 = jnp.sum(jnp.where((lane > 0) & (row == 0), full, 0.0))
    t2 = jnp.sum(jnp.where((lane == 0) & (row == 0), full, 0.0))
    full = jnp.where((lane == 0) | (lane > last), 0.0, full)
    full = jnp.where(lane == 1, full + pad, full)
    ds[:, 0:LONG] = jnp.where(body, full, 0.0)
    for r in range(GRID + 1):
        size = GRID if r < GRID else LONG - GRID * GRID
        off = (GRID - r) * GRID
        dl_ref[h, 0:size, off : off + LONG] += ds[r * GRID : r * GRID + size, 0:LONG]
    tail_add(dt_ref, h, t0, t1, t2)


def tail_add(dt_ref, h, t0, t1, t2):
    lane = lax.broadcasted_iota(jnp.int32, (8, 128), 1)
    row = lax.broadcasted_iota(jnp.int32, (8, 128), 0)
    add = jnp.where(lane == 0, t0, jnp.where(lane == 1, t1, jnp.where(lane == 2, t2, 0.0)))
    dt_ref[h] += jnp.where(row == 0, add, 0.0)


def fold_small(ds, h, ds_ref, dt_ref):
    last = SMALL * SMALL
    for base, wide in ((0, SHORT), (SHORT, LONG - SHORT)):
        full = ds[base : base + SHORT, 0:LONG]
        if base:
            full = full[:, base : base + wide]
        else:
            full = full[:, 0:wide]
        lane = lax.broadcasted_iota(jnp.int32, full.shape, 1)
        row = lax.broadcasted_iota(jnp.int32, full.shape, 0)
        pad = jnp.sum(jnp.where(lane > last, full, 0.0), axis=1, keepdims=True)
        body = row > 0
        t0 = jnp.sum(jnp.where((lane == 0) & body, full, 0.0))
        t1 = jnp.sum(jnp.where((lane > 0) & (row == 0), full, 0.0))
        t2 = jnp.sum(jnp.where((lane == 0) & (row == 0), full, 0.0))
        full = jnp.where((lane == 0) | (lane > last), 0.0, full)
        full = jnp.where(lane == 1, full + pad, full)
        ds[base : base + SHORT, 0:wide] = full
        for r in range(SMALL):
            off = (SMALL - 1 - r) * SMALL
            lo = base + 1 + r * SMALL
            ds_ref[h, 0:SMALL, off : off + wide] += ds[lo : lo + SMALL, 0:wide]
        tail_add(dt_ref, h, t0, t1, t2)


def backward_kernel(first, *refs):
    sc_ref, w_ref, bias_ref, q_ref, k_ref, v_ref, do_ref, lse_ref = refs[:8]
    refs = refs[8:]
    if not first:
        al_ref, as_ref, at_ref = refs[:3]
        refs = refs[3:]
    kept_ref, sent_ref, dq_ref, dk_ref, dv_ref, dl_ref, ds_ref, dt_ref, scr = refs
    if first:
        dl_ref[...] = jnp.zeros_like(dl_ref)
        ds_ref[...] = jnp.zeros_like(ds_ref)
        dt_ref[...] = jnp.zeros_like(dt_ref)
    else:
        dl_ref[...] = al_ref[...]
        ds_ref[...] = as_ref[...]
        dt_ref[...] = at_ref[...]
    q, k, v = q_ref[0], k_ref[0], v_ref[0]
    do_t = do_ref[0].astype(BF16)
    do = do_ref[0].T.astype(BF16)
    k_t = turned(k)
    d_qt = []
    d_k = jnp.zeros(k.shape, F32)
    d_v = jnp.zeros(k.shape, F32)
    for h in range(k.shape[1] // HD):
        own = head_lanes(k.shape, h)
        s = dot_nt(jnp.where(own, k, jnp.zeros_like(k)), q) + bias_ref[0, h].astype(F32)
        p = jnp.exp(s - lse_ref[0, h : h + 1, :])
        dp = dot(jnp.where(own, v, jnp.zeros_like(v)), do_t)
        inner = jnp.sum(p * dp, axis=0, keepdims=True)
        ds = (p * (dp - inner)).astype(BF16)
        d_v = jnp.where(own, dot(p.astype(BF16), do), d_v)
        d_k = jnp.where(own, dot(ds, q), d_k)
        d_qt.append(dot(k_t[h * HD : (h + 1) * HD], ds))
        scr[:, 0:LONG] = ds.astype(F32)

        @pl.when(sc_ref[1] == 0)
        def _():
            fold_large(scr, h, dl_ref, dt_ref)

        @pl.when(sc_ref[1] == 1)
        def _():
            fold_small(scr, h, ds_ref, dt_ref)

    d_qt = jnp.concatenate(d_qt, axis=0).astype(BF16) * jnp.asarray(HD**-0.5, BF16)
    d_q = d_qt.astype(F32).T.astype(BF16)
    d_k = d_k.astype(BF16)
    d_v = d_v.astype(BF16)
    dn = dot(d_q, w_ref[0]) + dot(d_k, w_ref[1]) + dot(d_v, w_ref[2])
    part_halves(sc_ref[2], dn, kept_ref, sent_ref)
    dq_ref[...] = d_qt
    dk_ref[...] = turned(d_k)
    dv_ref[...] = turned(d_v)


def attend_back(scalars, w_qkv, bias, saved, do, sums):
    width, dim = w_qkv.shape[1:]
    heads = width // HD
    q, k, v, lse = saved
    first = sums is None
    pair = (LONG, dim // 2)
    sum_shapes = [(heads, GRID, WIDE_L), (heads, 16, WIDE_S), (heads, 8, 128)]
    specs = [
        once(whole_spec, (3, width, dim)),
        once(kind_spec, (heads, LONG, LONG)),
        once(first_spec, (LONG, width)),
        once(first_spec, (LONG, width)),
        once(first_spec, (LONG, width)),
        once(first_spec, (width, LONG)),
        once(first_spec, (heads, LONG)),
    ]
    if not first:
        specs += [once(whole_spec, s) for s in sum_shapes]
    return pl.pallas_call(
        partial(backward_kernel, first),
        out_shape=[jax.ShapeDtypeStruct(pair, F32)] * 2
        + [jax.ShapeDtypeStruct((width, LONG), BF16)] * 3
        + [jax.ShapeDtypeStruct(s, F32) for s in sum_shapes],
        grid_spec=pltpu.PrefetchScalarGridSpec(
            num_scalar_prefetch=1,
            grid=(1,),
            in_specs=specs,
            out_specs=[once(whole_spec, pair)] * 2
            + [once(whole_spec, (width, LONG))] * 3
            + [once(whole_spec, s) for s in sum_shapes],
            scratch_shapes=[pltpu.VMEM((LONG, 640), F32)],
        ),
        compiler_params=params(),
        cost_estimate=spent(12.4),
        name="attend_back",
    )(scalars, w_qkv, bias, q, k, v, do, lse, *(sums or ()))


def qkv_kernel(sc_ref, nf, no, qf, kf, vf, qo, ko, vo, pa, pb, *refs):
    db_ref = refs[2]
    blocks = [
        dot(far[...], nf[0]) + dot(own[...], no[0]) for far, own in ((qf, qo), (kf, ko), (vf, vo))
    ]
    blocks.append(pa[...] + pb[...])
    rows = blocks[0].shape[0]
    for i in range(2):
        at = pl.ds(i * rows, rows)
        refs[0][at] = jnp.where(sc_ref[4] == 0, blocks[i], blocks[2 + i])
        refs[1][at] = jnp.where(sc_ref[4] == 0, blocks[2 + i], blocks[i])
    for i, (far, own) in enumerate(((qf, qo), (vf, vo))):
        db_ref[:, i : i + 1] = jnp.sum(far[...].astype(F32), axis=1, keepdims=True) + jnp.sum(
            own[...].astype(F32), axis=1, keepdims=True
        )


def qkv_grad(scalars, n_far, n_own, far, own, proj_a, proj_b):
    dim = n_far.shape[2]
    width = far[0].shape[0]
    return pl.pallas_call(
        qkv_kernel,
        in_specs=[SCALARS] + [PLAIN] * 10,
        out_shape=[jax.ShapeDtypeStruct((2 * width, dim), F32)] * 2
        + [jax.ShapeDtypeStruct((width, 128), F32)],
        compiler_params=params(),
        cost_estimate=spent(4.5),
        name="qkv_grad",
    )(scalars, n_far, n_own, *far, *own, proj_a, proj_b)


def wide_rows(lo_ref, hi_ref):
    return jnp.concatenate([lo_ref[0], hi_ref[0]], axis=1)


def column_sum(x):
    return jnp.sum(x, axis=0, keepdims=True)


def feed_kernel(first, *refs):
    if not first:
        refs = refs[:14] + refs[15:]
    (sc_ref, tok_ref, out_ref, o0, oc, ox, od, wp0, wpc, wpx, wpd) = refs[:11]
    vec, w1, w2 = refs[11:14]
    mid_ref, a_ref, kept_ref, sent_ref, g_ref, n_ref, du_ref, dm_ref, o_scr, w_scr = refs[14:]
    low = lambda r: r.astype(BF16)
    place = sc_ref[3]
    for hop, (part, weight) in enumerate(((o0, wp0), (oc, wpc), (ox, wpx), (od, wpd))):
        at = place ^ hop
        o_scr[at] = low(part[0])
        w_scr[at] = low(weight[...])
    size = o_scr.shape[0] * o_scr.shape[1]
    o_all = o_scr[...].reshape(size, o_scr.shape[2])
    a = dot_tn(o_all, w_scr[...].reshape(size, w_scr.shape[2])) + vec[6:7]
    a_ref[0] = a
    mid = tok_ref[0].astype(F32) + vec[4:5] * a
    mid_ref[0] = mid
    n2 = layer_norm(mid, vec[2:3], vec[3:4])[0].astype(BF16)
    n_ref[0] = n2
    u = dot(n2, w1[...]) + vec[7:8]
    cdf = 0.5 * (1.0 + lax.erf(u * np.float32(np.sqrt(0.5))))
    slope = cdf + u * (jnp.exp(-0.5 * u * u) * np.float32(1 / np.sqrt(2 * np.pi)))
    g_ref[0] = (u * cdf).astype(BF16)
    dm = (vec[5:6] * out_ref[0].astype(F32)).astype(BF16)
    dm_ref[0] = dm
    du = (slope * dot_nt(dm, w2[...])).astype(BF16)
    du_ref[0] = du
    dn = dot_nt(du, w1[...])
    part_halves(sc_ref[2], dn, kept_ref, sent_ref)


def feed(scalars, tok3, out3, o_parts, w_parts, vec, w1, w2, mid=None):
    dim = tok3.shape[2]
    hid = w1.shape[1]
    width = w_parts[0].shape[0]
    pair = jax.ShapeDtypeStruct((LONG, dim // 2), F32)
    row = jax.ShapeDtypeStruct((1, LONG, dim), F32)
    both = jax.ShapeDtypeStruct((2, LONG, dim), F32)
    held = () if mid is None else (mid,)
    low = lambda n: jax.ShapeDtypeStruct((1, LONG, n), BF16)
    specs = (
        [once(pack_spec, (LONG, dim))] * 2
        + [once(first_spec, (width, LONG))] * 4
        + [once(whole_spec, (width, dim))] * 4
        + [
            once(whole_spec, (8, dim)),
            once(whole_spec, (dim, hid)),
            once(whole_spec, (hid, dim)),
        ]
    )
    specs += [pl.BlockSpec(memory_space=pl.ANY)] * len(held)
    return pl.pallas_call(
        partial(feed_kernel, mid is None),
        out_shape=[both, row, pair, pair, low(hid), low(dim), low(hid), low(dim)],
        grid_spec=pltpu.PrefetchScalarGridSpec(
            num_scalar_prefetch=1,
            grid=(1,),
            in_specs=specs,
            out_specs=[once(pack_spec, (LONG, dim)), once(first_spec, (LONG, dim))]
            + [once(whole_spec, pair.shape)] * 2
            + [once(first_spec, (LONG, n)) for n in (hid, dim, hid, dim)],
            scratch_shapes=[
                pltpu.VMEM((4, width, LONG), BF16),
                pltpu.VMEM((4, width, dim), BF16),
            ],
        ),
        compiler_params=params(),
        input_output_aliases={14: 0} if held else {},
        cost_estimate=spent(10),
        name="feed",
    )(scalars, tok3, out3, *o_parts, *w_parts, vec, w1, w2, *held)


SCALARS = pl.BlockSpec(memory_space=pltpu.SMEM)
PLAIN = pl.BlockSpec(memory_space=pltpu.VMEM)


def out_kernel(sc_ref, up, g, w2, kept_ref, sent_ref, sum_ref):
    m = dot(g[0], w2[...])
    part_halves(sc_ref[2], m, kept_ref, sent_ref)
    e = up[0].astype(F32)
    sum_ref[0:1] = column_sum(e * m)
    sum_ref[1:2] = column_sum(e)


def feed_out(scalars, up3, g, w2):
    hid, dim = w2.shape
    return pl.pallas_call(
        out_kernel,
        out_shape=[jax.ShapeDtypeStruct(n, F32) for n in [(LONG, dim // 2)] * 2 + [(2, dim)]],
        grid_spec=pltpu.PrefetchScalarGridSpec(
            num_scalar_prefetch=1,
            grid=(1,),
            in_specs=[
                once(pack_spec, (LONG, dim)),
                once(first_spec, (LONG, hid)),
                once(whole_spec, (hid, dim)),
            ],
            out_specs=[once(whole_spec, (LONG, dim // 2))] * 2 + [once(whole_spec, (2, dim))],
        ),
        compiler_params=params(),
        cost_estimate=spent(3.5),
        name="feed_out",
    )(scalars, up3, g, w2)


def part_blocks(bit, blocks, refs):
    for i in range(len(blocks) // 2):
        refs[2 * i][...] = jnp.where(bit == 0, blocks[2 * i], blocks[2 * i + 1])
        refs[2 * i + 1][...] = jnp.where(bit == 0, blocks[2 * i + 1], blocks[2 * i])


def feed_grad_kernel(sc_ref, up, gf, nf, uf, mf, go, no, uo, mo, w2, *refs):
    db1_ref, db2_ref = refs[4:6]
    d1 = dot_tn(nf[0], uf[0]) + dot_tn(no[0], uo[0])
    rows = d1.shape[0] // 2
    part_blocks(sc_ref[4], (d1[:rows], d1[rows:]), refs[:2])
    d2 = dot_tn(gf[0], mf[0]) + dot_tn(go[0], mo[0])
    part_blocks(sc_ref[5], (d2[:rows], d2[rows:]), refs[2:4])
    db1_ref[...] = column_sum(uf[0].astype(F32)) + column_sum(uo[0].astype(F32))
    db2_ref[...] = column_sum(mf[0].astype(F32)) + column_sum(mo[0].astype(F32))
    out_kernel(sc_ref, up, go, w2, *refs[6:])


def feed_grad(scalars, up3, far, own, w2):
    hid, dim = w2.shape
    shapes = [(dim // 2, hid)] * 2 + [(hid // 2, dim)] * 2 + [(1, hid), (1, dim)]
    shapes += [(LONG, dim // 2)] * 2 + [(2, dim)]
    kept = [once(first_spec, (LONG, n)) for n in (hid, dim, hid, dim)]
    return pl.pallas_call(
        feed_grad_kernel,
        out_shape=[jax.ShapeDtypeStruct(n, F32) for n in shapes],
        grid_spec=pltpu.PrefetchScalarGridSpec(
            num_scalar_prefetch=1,
            grid=(1,),
            in_specs=[once(pack_spec, (LONG, dim))]
            + kept * 2
            + [once(whole_spec, (hid, dim))],
            out_specs=[once(whole_spec, n) for n in shapes],
        ),
        compiler_params=params(),
        cost_estimate=spent(9.5),
        name="feed_grad",
    )(scalars, up3, *far, *own, w2)


def norm_back(upstream, unit_rows, inverse, gain_row):
    scaled = upstream * gain_row
    centred = scaled - jnp.mean(scaled, axis=-1, keepdims=True)
    centred = centred - unit_rows * jnp.mean(scaled * unit_rows, axis=-1, keepdims=True)
    return inverse * centred, column_sum(upstream * unit_rows), column_sum(upstream)


def joined(sc_ref, mine, peer):
    core = sc_ref[2]
    lo = jnp.where(core == 0, mine[...], peer[...])
    hi = jnp.where(core == 0, peer[...], mine[...])
    return jnp.concatenate([lo, hi], axis=1)


def middle_kernel(
    sc_ref, out_ref, mid_ref, a_ref, mine, peer, vec, wp0, wpx, o0, ox,
    dmid_ref, do0_ref, dox_ref, dp0_ref, dpx_ref, sum_ref
):
    dn2 = joined(sc_ref, mine, peer)
    _, unit, inverse = layer_norm(mid_ref[0], vec[2:3], vec[3:4])
    back, d_gain, d_shift = norm_back(dn2, unit, inverse, vec[2:3])
    dmid = out_ref[0].astype(F32) + back
    dmid_ref[0] = dmid
    da = (vec[4:5] * dmid).astype(BF16)
    do0_ref[0] = dot_nt(wp0[...], da).astype(BF16).astype(F32)
    dox_ref[0] = dot_nt(wpx[...].astype(BF16), da).astype(BF16).astype(F32)
    dp0_ref[...] = dot(o0[0].astype(BF16), da)
    dpx_ref[...] = dot(ox[0].astype(BF16), da)
    sum_ref[0:1] = d_gain
    sum_ref[1:2] = d_shift
    sum_ref[2:3] = column_sum(dmid * a_ref[0])
    sum_ref[3:4] = column_sum(da.astype(F32))


def middle_back(scalars, out3, mid, a, mine, peer, vec, w_parts, o_parts):
    dim = mid.shape[2]
    width = w_parts[0].shape[0]
    row = jax.ShapeDtypeStruct((1, LONG, dim), F32)
    low = jax.ShapeDtypeStruct((1, width, LONG), F32)
    mat = jax.ShapeDtypeStruct((width, dim), F32)
    return pl.pallas_call(
        middle_kernel,
        out_shape=[row, low, low, mat, mat, jax.ShapeDtypeStruct((4, dim), F32)],
        grid_spec=pltpu.PrefetchScalarGridSpec(
            num_scalar_prefetch=1,
            grid=(1,),
            in_specs=[
                once(pack_spec, (LONG, dim)),
                once(pack_spec, (LONG, dim)),
                once(first_spec, (LONG, dim)),
                once(whole_spec, (LONG, dim // 2)),
                once(whole_spec, (LONG, dim // 2)),
                once(whole_spec, (8, dim)),
                once(whole_spec, (width, dim)),
                once(whole_spec, (width, dim)),
                once(first_spec, (width, LONG)),
                once(first_spec, (width, LONG)),
            ],
            out_specs=[
                once(first_spec, (LONG, dim)),
                once(first_spec, (width, LONG)),
                once(first_spec, (width, LONG)),
                once(whole_spec, (width, dim)),
                once(whole_spec, (width, dim)),
                once(whole_spec, (4, dim)),
            ],
        ),
        compiler_params=params(),
        cost_estimate=spent(7.7),
        name="middle_back",
    )(scalars, out3, mid, a, mine, peer, vec, *w_parts[::2], *o_parts[::2])


def final_kernel(sc_ref, tok_ref, dmid_ref, mine, peer, vec, two, scale, out_ref, sent_ref, sum_ref):
    dn1 = joined(sc_ref, mine, peer)
    _, unit, inverse = layer_norm(tok_ref[0].astype(F32), vec[0:1], vec[1:2])
    back, d_gain, d_shift = norm_back(dn1, unit, inverse, vec[0:1])
    result = dmid_ref[0] + back
    out_ref[0] = result
    half = result.shape[1] // 2
    rows = jnp.concatenate([two[...], d_gain, d_shift, scale[...]], axis=0)
    sum_ref[...] = rows
    sent_ref[0:LONG] = jnp.where(sc_ref[2] == 0, result[:, :half], result[:, half:])
    sent_ref[LONG : LONG + 8] = rows[:, :half]
    sent_ref[LONG + 8 : LONG + 16] = rows[:, half:]


def final_back(scalars, tok3, dmid, mine, peer, vec, two, scale):
    dim = tok3.shape[2]
    return pl.pallas_call(
        final_kernel,
        out_shape=[
            jax.ShapeDtypeStruct((1, LONG, dim), F32),
            jax.ShapeDtypeStruct((LONG + 16, dim // 2), F32),
            jax.ShapeDtypeStruct((8, dim), F32),
        ],
        grid_spec=pltpu.PrefetchScalarGridSpec(
            num_scalar_prefetch=1,
            grid=(1,),
            in_specs=[
                once(pack_spec, (LONG, dim)),
                once(first_spec, (LONG, dim)),
                once(whole_spec, (LONG, dim // 2)),
                once(whole_spec, (LONG, dim // 2)),
                once(whole_spec, (8, dim)),
                once(whole_spec, (4, dim)),
                once(whole_spec, (2, dim)),
            ],
            out_specs=[
                once(first_spec, (LONG, dim)),
                once(whole_spec, (LONG + 16, dim // 2)),
                once(whole_spec, (8, dim)),
            ],
        ),
        compiler_params=params(),
        cost_estimate=spent(5.6),
        name="final_back",
    )(scalars, tok3, dmid, mine, peer, vec, two, scale)


def last_kernel(sc_ref, kept, got, flat_ref, b2, _, qkv_ref, proj_ref, *refs):
    gains, shifts, scales, singles, bias, table = refs
    rows = kept.shape[0]
    width = rows // 2
    swap = sc_ref[4] == 0
    for i, lo in enumerate((0, width)):
        a = kept[lo : lo + width]
        b = got[lo : lo + width]
        qkv_ref[i] = jnp.where(swap, a, b)
        other = jnp.where(swap, b, a)
        if i == 0:
            qkv_ref[2] = other
        else:
            proj_ref[...] = other
    flat = flat_ref[...]
    gains[0:1] = flat[4:5]
    gains[1:2] = flat[0:1]
    shifts[0:1] = flat[5:6]
    shifts[1:2] = flat[1:2]
    scales[0:1] = flat[2:3]
    scales[1:2] = flat[6:7] + b2[...].astype(F32) * flat[10:11]
    singles[0:1] = flat[3:4]
    singles[1:3] = flat[8:10]
    count = table.shape[1]
    for h in range(table.shape[0]):
        for i in range(3):
            row = flat[11 + 3 * h + i : 12 + 3 * h + i]
            lo = i * flat.shape[1]
            hi = min(lo + flat.shape[1], count)
            table[h : h + 1, lo:hi] = row[:, : hi - lo]
    row = flat[11 + 3 * table.shape[0] : 12 + 3 * table.shape[0]]
    bias[0:1] = row[:, :width]
    bias[1:2] = row[:, width : 2 * width]


def last_parts(scalars, kept, got, flat, b2, after, heads, count):
    rows, dim = kept.shape
    width = rows // 2
    shapes = [(3, width, dim), (width, dim)] + [(2, dim)] * 3 + [(3, dim), (2, width), (heads, count)]
    return pl.pallas_call(
        last_kernel,
        in_specs=[SCALARS] + [PLAIN] * 4 + [pl.BlockSpec(memory_space=pl.ANY)],
        out_shape=[jax.ShapeDtypeStruct(n, F32) for n in shapes],
        compiler_params=params(),
        cost_estimate=spent(3),
        name="last_parts",
    )(scalars, kept, got, flat, b2, after)


CORE = [(i, i ^ 1) for i in range(4)]
ACROSS = [(i, i ^ 2) for i in range(4)]


def to_core(x):
    return lax.ppermute(x, "narrow", CORE)


def to_chip(x):
    return lax.ppermute(x, "narrow", ACROSS)


def pick(pair, index):
    return lax.dynamic_index_in_dim(pair, index, 0, keepdims=False)


def small_sum(x, size):
    step = 1
    while step < size:
        x = x + lax.ppermute(x, "wide", [(i, i ^ step) for i in range(size)])
        step *= 2
    return x


def tie(*values):
    return lax.optimization_barrier(values)


def in_order(bit, first, second):
    return jnp.where(bit == 0, first, second), jnp.where(bit == 0, second, first)


WIDE_PLACES = 8
DUE = {
    "one": (1, 2, 3, 5, 8),
    "two": (1, 3, 5, 9, 13),
    "last": (4, 6, 9, 11, 14),
    "flat": (9, 11, 14),
}


class Wave:
    def __init__(self, place):
        self.place = place
        self.live = {}
        self.done = {}

    def bit(self, step):
        return (self.place >> (step.bit_length() - 1)) & 1

    def send(self, value, step):
        return lax.ppermute(value, "wide", [(i, i ^ step) for i in range(WIDE_PLACES)])

    def add(self, name, kept, sent, steps, due, whole=False):
        got = self.send(sent, steps[0])
        self.live[name] = dict(steps=steps, stage=0, kept=kept, got=got, due=list(due), whole=whole)

    def advance(self, c, got):
        stage, kept, (first, second, third) = c["stage"], c["kept"], c["steps"]
        if c["whole"]:
            total = kept + got
            return (total, total, (first, second, third)[stage + 1]) if stage < 2 else (total, None, None)
        if stage == 0:
            rows = kept.shape[0] // 2
            split = lambda v: v.reshape((2, rows) + v.shape[1:])
            side = self.bit(second)
            kept, got = split(kept), split(got)
            send = pick(kept, 1 - side) + pick(got, 1 - side)
            return pick(kept, side) + pick(got, side), send, second
        if stage < 3:
            total = kept + got
        elif stage == 3:
            total = jnp.concatenate(in_order(self.bit(second), kept, got))
        else:
            return (kept, got), None, None
        return total, total, (third, second, first)[stage - 1]

    def event(self, now, then):
        ripe = [n for n, c in self.live.items() if c["due"][0] <= now]
        if not ripe:
            return then
        then, *values = tie(then, *[self.live[n]["got"] for n in ripe])
        moves = {n: self.advance(self.live[n], got) for n, got in zip(ripe, values)}
        for n in ripe:
            if moves[n][1] is None:
                self.done[n] = moves[n][0]
                del self.live[n], moves[n]
        if not moves:
            return then
        held = tie(then, *[m[1] for m in moves.values()])
        for (n, (kept, _, step)), value in zip(moves.items(), held[1:]):
            c = self.live[n]
            c["kept"] = kept
            c["got"] = self.send(value, step)
            c["stage"] += 1
            c["due"].pop(0)
        return held[0]


def on_device(
    tokens, w_qkv, qv_bias, w_proj, proj_bias, w_fc1, fc1_bias, w_fc2, fc2_bias, norm_gains,
    norm_shifts, layer_scales, rel_table, image_ids, pad_mask, grid_rows, grid_cols, d_out, wide
):
    rows, dim = tokens.shape
    width = w_qkv.shape[2]
    place = lax.axis_index("narrow")
    chip, core = place >> 1, place & 1
    spot = lax.axis_index("wide")
    tok3 = tokens.reshape(2, LONG, dim)
    out3 = d_out.reshape(2, LONG, dim)
    w_turned = w_qkv.transpose(0, 2, 1)
    kind_a = image_ids[LONG - 1] & 1
    kind_b = image_ids[2 * LONG - 1] & 1
    common = (core, place, spot & 1, (spot >> 1) & 1)
    sc_far = jnp.stack([1 - chip, jnp.where(chip == 0, kind_b, kind_a), *common])
    sc_own = jnp.stack([chip, jnp.where(chip == 0, kind_a, kind_b), *common])
    pairs = zip(norm_gains.astype(F32), norm_shifts.astype(F32))
    vec = jnp.stack(
        [v for pair in pairs for v in pair]
        + list(layer_scales.astype(F32))
        + [proj_bias.astype(F32), fc1_bias.astype(F32)]
    )

    wp_near = w_proj.astype(F32)
    wp_far = to_chip(wp_near)
    bias = make_bias(rel_table)
    first = lambda sc: attend(sc, tok3, w_turned, qv_bias, vec, bias)
    o_own, *saved_own, n_own = first(sc_own)
    wp_far, o_sent = tie(wp_far, o_own)
    x_far = to_chip(o_sent)
    w_parts = (w_proj, to_core(wp_near), wp_far, to_core(wp_far))
    o_own, sc = tie(o_own, sc_far)
    o_far, *saved_far, n_far = first(sc)
    x_far, o_sent = tie(x_far, o_far)
    x_own = to_chip(o_sent)
    far_parts = (o_far, to_core(o_far), x_far, to_core(x_far))

    shared = (w_parts, vec, w_fc1, w_fc2)
    mid, _, dn_kept, dn_send, *kept_far = feed(sc_far, tok3, out3, far_parts, *shared)
    dn_send, x_own = tie(dn_send, x_own)
    own_parts = (o_own, to_core(o_own), x_own, to_core(x_own))
    peer = to_core(dn_send)
    sc, _ = tie(sc_far, dn_send)
    m_far_kept, m_far_send, scale_far = feed_out(sc, out3, kept_far[0], w_fc2)
    peer, scale_far = tie(peer, scale_far)
    half, sc = tie(dn_kept + peer, sc_own)
    dn_got = to_chip(half)
    mid, a_own, dn_kept, dn_send, *kept_own = feed(sc, tok3, out3, own_parts, *shared, mid)
    peer = to_core(dn_send)
    *blocks, d_fc1_bias, d_fc2_bias, m_own_kept, m_own_send, scale_own = feed_grad(
        sc_own, out3, kept_far, kept_own, w_fc2
    )

    wave = Wave(spot)
    custom = wide == WIDE_PLACES
    if custom:
        wave.add("one", blocks[0], blocks[1], (1, 2, 4), DUE["one"])
        wave.add("two", blocks[2], blocks[3], (2, 1, 4), DUE["two"])
    dn_got, scale_own = tie(dn_got, scale_own)
    part, peer = tie(dn_kept + dn_got, peer)
    mine = part + peer
    theirs = to_core(mine)
    dmid, do_own, do_send, dp_own, dp_send, sums_two = middle_back(
        sc_own, out3, mid, a_own, mine, theirs, vec, w_parts, own_parts
    )
    do_far = to_chip(do_send)
    m_far_peer, m_own_peer, _ = tie(to_core(m_far_send), to_core(m_own_send), dmid)
    m_half_far = m_far_kept + m_far_peer
    m_half_own = m_own_kept + m_own_peer
    scale = scale_far + scale_own
    up_sum = scale[1:2]
    scale, _ = tie(scale, dmid)
    scale = scale + to_core(scale)
    do_far, m_half_far, m_half_own, scale = tie(do_far, m_half_far, m_half_own, scale)
    do_far, sc = tie(do_far, sc_far)
    sc = wave.event(1, sc)
    dp_send, sc = tie(dp_send, sc)
    dp_got = to_chip(dp_send)

    dn_kept, dn_send, *far, dl, ds, dt = attend_back(sc, w_turned, bias, saved_far, do_far, None)
    dn_send, dp_got = tie(dn_send, dp_got)
    dn_send = wave.event(2, dn_send)
    peer = to_core(dn_send)
    half, sc, dp_got = tie(dn_kept + peer, sc_own, dp_got)
    dn_got = to_chip(half)
    dn_kept, dn_send, *own, dl, ds, dt = attend_back(
        sc, w_turned, bias, saved_own, do_own, (dl, ds, dt)
    )
    *pieces, d_qv_bias = qkv_grad(sc_own, n_far, n_own, far, own, dp_own, dp_got)
    dn_got, d_qv_bias, dn_send = tie(dn_got, d_qv_bias, dn_send)
    dn_send = wave.event(3, dn_send)
    peer = to_core(dn_send)
    if custom:
        wave.add("last", pieces[0], pieces[1], (1, 2, 4), DUE["last"])
    part, peer = tie(dn_kept + dn_got, peer)
    mine = part + peer
    theirs = to_core(mine)
    tok_own, tok_send, own_rows = final_back(
        sc_own, tok3, dmid, mine, theirs, vec, sums_two, scale
    )
    tok_got = to_chip(tok_send)
    dl, ds, dt, own_rows = tie(dl, ds, dt, own_rows)
    table_back = strips_back(dl, ds, dt)
    heads, count = table_back.shape
    row_bias = jnp.pad(d_qv_bias[:, :2].T.reshape(1, -1), ((0, 0), (0, dim - 2 * width)))
    rest = jnp.pad(table_back, ((0, 0), (0, 3 * dim - count))).reshape(3 * heads, dim)
    rest = [d_fc2_bias, d_fc1_bias, up_sum, rest, row_bias, jnp.zeros((12 - 3 * heads, dim), F32)]
    rest = jnp.concatenate(rest)
    rest, own_rows = tie(rest, own_rows)
    mark = wave.event(4, own_rows)
    mark = wave.event(5, mark)
    tok_got, mark = tie(tok_got, mark)
    tok_peer = to_core(tok_got)
    m_send, mark = tie(m_half_far, mark)
    m_all_own = to_chip(m_send)
    mark = wave.event(6, mark)
    own_rows = mark + jnp.concatenate([tok_got[LONG : LONG + 8], tok_got[LONG + 8 :]], axis=1)
    flat = jnp.concatenate([own_rows, rest])
    mark = flat
    if custom:
        wave.add("flat", mark, mark, (4, 2, 1), DUE["flat"], True)
    tok_peer, mark = tie(tok_peer, mark)
    tok_far = jnp.concatenate(in_order(core, tok_got[:LONG], tok_peer[:LONG]), axis=1)[None]
    d_tokens = jnp.concatenate(in_order(chip, tok_own, tok_far)).reshape(rows, dim)
    d_tokens, mark = tie(d_tokens, mark)
    m_all_own, mark = tie(m_all_own, mark)
    m_all_own = m_half_own + m_all_own
    m_own_peer = to_core(m_all_own)
    m_send, m_all_own = tie(m_half_own, m_all_own)
    m_all_far = to_chip(m_send)
    mark = wave.event(8, mark)
    if custom:
        d_fc1 = jnp.concatenate(in_order(spot & 1, *wave.done["one"]))
        d_fc1, mark = tie(d_fc1, mark)
    mark = wave.event(9, mark)
    m_all_far, mark = tie(m_all_far, mark)
    m_all_far = m_half_far + m_all_far
    m_far_peer = to_core(m_all_far)
    mark = wave.event(11, mark)
    m_own_peer, m_far_peer, mark = tie(m_own_peer, m_far_peer, mark)
    m_own = jnp.concatenate(in_order(core, m_all_own, m_own_peer), axis=1)[None]
    m_far = jnp.concatenate(in_order(core, m_all_far, m_far_peer), axis=1)[None]
    m_full = jnp.concatenate(in_order(chip, m_own, m_far)) + fc2_bias.astype(F32)
    block_out = (mid + layer_scales[1].astype(F32) * m_full).astype(BF16).reshape(rows, dim)
    block_out, mark = tie(block_out, mark)
    mark = wave.event(13, mark)
    if custom:
        d_fc2 = jnp.concatenate(in_order((spot >> 1) & 1, *wave.done["two"]))
        d_fc2, mark = tie(d_fc2, mark)
    mark = wave.event(14, mark)
    if custom:
        got = wave.done
        kept, last = got["last"]
        flat = got["flat"]
    else:
        low, high = spot & 1, (spot >> 1) & 1
        d_fc1 = jnp.concatenate(in_order(low, blocks[0], blocks[1]))
        d_fc2 = jnp.concatenate(in_order(high, blocks[2], blocks[3]))
        pieces = in_order(low, *pieces)
        pieces, d_fc1, d_fc2 = lax.psum((pieces, d_fc1, d_fc2), "wide")
        kept, last = in_order(low, *pieces)
        flat = small_sum(flat, wide)
    d_qkv, d_proj, d_norm_gains, d_norm_shifts, d_layer_scales, singles, d_qv_bias, d_table = last_parts(
        sc_own, kept, last, flat, fc2_bias[None], mark, heads, count
    )
    d_proj_bias, d_fc2_bias, d_fc1_bias = singles
    d_qkv = d_qkv.transpose(0, 2, 1)
    return (
        block_out,
        d_tokens,
        d_qkv,
        d_qv_bias,
        d_proj,
        d_proj_bias,
        d_fc1,
        d_fc1_bias,
        d_fc2,
        d_fc2_bias,
        d_norm_gains,
        d_norm_shifts,
        d_layer_scales,
        d_table,
    )


def solution(mesh):
    in_specs = (
        P("wide", None),
        P(None, None, "narrow"),
        P(None, "narrow"),
        P("narrow", None),
        P(),
        P(None, "narrow"),
        P("narrow"),
        P("narrow", None),
        P(),
        P(),
        P(),
        P(),
        P("narrow", None),
        P("wide"),
        P("wide"),
        P("wide"),
        P("wide"),
        P("wide", None),
    )
    out_specs = (
        P("wide", None),
        P("wide", None),
        P(None, None, "narrow"),
        P(None, "narrow"),
        P("narrow", None),
        P(),
        P(None, "narrow"),
        P("narrow"),
        P("narrow", None),
        P(),
        P(),
        P(),
        P(),
        P("narrow", None),
    )
    return jax.shard_map(
        partial(on_device, wide=mesh.shape["wide"]),
        mesh=mesh,
        in_specs=in_specs,
        out_specs=out_specs,
        check_vma=False,
    )
```
